256 devices in a mesh: gx: 8 (over y, core), gy: 4 (over x), gz: 8 (over z).
Axes of the slice: x: 4, y: 4, z: 8, core: 2. Of those that a mesh axis runs over, the one named last changes fastest.
Arguments:
- block_state: bfloat16 [8, 128, 10, 32, 1024], P('gx', ('gy', 'gz')), may hold values from -6 to 6
- block_level: int32 [8, 128], P('gx'), may hold values from 0 to 2, as said below
- block_velocity: bfloat16 [8, 128, 3], P('gx', ('gy', 'gz')), may hold values from -1 to 1
- diffusivity: float32 [10], replicated, may hold values from 0.05 to 0.6
- reaction_matrix: float32 [10, 10], replicated, may hold values from -3 to 3
- ghost_source: int32 [8, 128, 6], P('gx'), may hold values from 0 to 127, as said below
- swap_bit: int32 [8, 4, 8], P('gx', 'gy', 'gz'), may hold values from -1 to 2, as said below
- swap_slot: int32 [8, 4, 8], P('gx', 'gy', 'gz'), may hold values from 0 to 3, as said below
Outputs:
- new_state: bfloat16 [8, 128, 10, 32, 1024], P('gx', ('gy', 'gz'))
The draws below stay inside these ranges and needn't reach their ends.
Inputs may be any that keep to these rules, and one draw needn't show every extreme that they name: `block_level`: levels are 0, 1 or 2; all blocks of some devices have level 2. `ghost_source`: ghost sources lie in the same gx slab; blocks of a slab are numbered device by device in gy+gz order, 4 a device. Among the 24 ghost faces of the blocks of one device, at most 2 come from the blocks of any one device, and exactly 2 from some device. `swap_bit`: all devices of one (gy, gz) column share the value, so trade partners are paired; -1 means that the column trades no block. `swap_slot`: of two partners, the one whose sum of 2 ** level over its blocks is larger (ties: the lower gx index) names its first block of highest level, the other its first block of lowest level.
All inputs are finite; a program needn't handle non-finite values.
Results may differ from the reference program's by a relative error of at most 0.001.
Values may be sent and summed in bfloat16 or wider, within the bound.
No kernel may reach another device: no remote copies, remote signals or barrier semaphores. Data moves between devices by JAX's collectives and lax.ppermute only.
A program may use at most 128 MiB of HBM per device.

```python
import math
import jax
import jax.numpy as jnp
from jax import lax

F = 10
B = 32
NB = 4
SLAB_BLOCKS = 128
CAP = 2
N_GX = 8
N_GY = 4
N_GZ = 8


def level_table(key):
    slab = N_GY * N_GZ
    bit_total = N_GX.bit_length() - 1
    top = 1 << bit_total - 1
    heated = jax.random.randint(jax.random.fold_in(key, 101), (N_GX, slab, 1), 0, 4) == 0
    lower = jax.random.randint(jax.random.fold_in(key, 102), (N_GX, slab, NB), 0, 2)
    table = jnp.where(heated, 2, lower).astype(jnp.int32)
    slab_ids = jnp.arange(N_GX, dtype=jnp.int32)[:, None, None]
    column = jnp.arange(slab, dtype=jnp.int32)[None, :, None]
    within = jnp.arange(NB, dtype=jnp.int32)[None, None, :]
    low_group = jnp.bitwise_and(slab_ids, top) == 0
    pattern = jnp.where(low_group & (within == NB - 1), 2, 0).astype(jnp.int32)
    table = jnp.where(column == 0, pattern, table)
    table = jnp.where(column == 1, jnp.int32(2), table)
    return table.astype(jnp.int32)


def bit_table(key):
    bit_total = N_GX.bit_length() - 1
    slab = N_GY * N_GZ
    column = jax.random.randint(jax.random.fold_in(key, 103), (slab,), -1, bit_total)
    column = column.at[0].set(bit_total - 1).at[1].set(-1)
    column = column.reshape(1, N_GY, N_GZ)
    return jnp.broadcast_to(column, (N_GX, N_GY, N_GZ)).astype(jnp.int32)


def draw_block_level(key, part):
    return level_table(key).reshape(N_GX, N_GY * N_GZ * NB)


def draw_swap_bit(key, part):
    return bit_table(key)


def draw_swap_slot(key, part):
    slab = N_GY * N_GZ
    levels = level_table(key)
    bits = bit_table(key).reshape(N_GX, slab)
    loads = jnp.sum(jnp.left_shift(jnp.int32(1), levels), axis=2)
    slab_ids = jnp.arange(N_GX, dtype=jnp.int32)[:, None]
    flips = jnp.where(bits < 0, jnp.int32(0), jnp.left_shift(jnp.int32(1), jnp.maximum(bits, 0)))
    partner = jnp.bitwise_xor(slab_ids, flips)
    other = jnp.take_along_axis(loads, partner, axis=0)
    heavier = (loads > other) | (loads == other) & (slab_ids < partner)
    chosen = jnp.where(heavier, jnp.argmax(levels, axis=2), jnp.argmin(levels, axis=2))
    return chosen.astype(jnp.int32).reshape(N_GX, N_GY, N_GZ)


def draw_ghost_source(key, part):
    slab = N_GY * N_GZ
    requests = 6 * NB
    limit = CAP
    keys = jax.random.split(jax.random.fold_in(key, 104), N_GX * slab)

    def one_device(subkey):
        first_key, order_key, shuffle_key, slot_key = jax.random.split(subkey, 4)
        first = jax.random.randint(first_key, (), 0, slab)
        owners = jnp.arange(slab * limit, dtype=jnp.int32) // limit
        scores = jax.random.permutation(order_key, slab * limit).astype(jnp.int32)
        scores = scores + jnp.where(owners == first, slab * limit, 0)
        ordering = jnp.argsort(scores, stable=True)
        others = owners[ordering][:requests - limit]
        devices = jnp.concatenate([jnp.full((limit,), first, jnp.int32), others])
        devices = devices[jax.random.permutation(shuffle_key, requests)]
        slots = jax.random.randint(slot_key, (requests,), 0, NB)
        return devices * NB + slots
    table = jax.vmap(one_device)(keys)
    return table.reshape(N_GX, slab * NB, 6).astype(jnp.int32)


def steps_of(rng, shape, pieces, smallest, top_value):
    def one(axis_at, shards_of):
        steps = jax.random.uniform(jax.random.fold_in(jax.random.fold_in(rng, 6), axis_at), (shards_of,), jnp.float32, smallest / len(pieces), top_value / len(pieces))
        return jnp.repeat(jnp.exp(steps), shape[axis_at] // shards_of).reshape((-1,) + (1,) * (len(shape) - axis_at - 1))

    level = one(*pieces[0])
    for cut in pieces[1:]:
        level = level * one(*cut)
    return level


def normal_values(stream_key, shape, scale, most, shards=(), kind=jnp.bfloat16):
    level = steps_of(stream_key, shape, shards, -0.22, 0.18) if shards else 1.0
    entries = jax.random.normal(stream_key, shape, jnp.float32) * scale * level
    return jnp.minimum(jnp.maximum(entries, -most), most).astype(kind)


def setup_inputs(seed: int = 0) -> dict:
    arg_keys = jax.random.split(jax.random.key(seed), 9)
    block_state = normal_values(arg_keys[0], (N_GX, SLAB_BLOCKS, F, B, B * B), 1.0, 6.0, ((0, 8), (1, 32)))
    block_level = draw_block_level(jax.random.fold_in(arg_keys[8], 71), 0)
    block_velocity = jnp.clip(jax.random.uniform(arg_keys[2], (N_GX, SLAB_BLOCKS, 3), jnp.float32, -1.0, 1.0) * steps_of(arg_keys[2], (N_GX, SLAB_BLOCKS, 3), ((0, 8), (1, 32)), -0.4, 0.0), -1.0, 1.0).astype(jnp.bfloat16)
    diffusivity = jnp.clip(jnp.exp(jax.random.uniform(arg_keys[3], (F,), jnp.float32, math.log(0.05), math.log(0.6))), 0.05, 0.6)
    reaction_matrix = normal_values(arg_keys[4], (F, F), 0.5, 3.0, (), jnp.float32)
    ghost_source = draw_ghost_source(jax.random.fold_in(arg_keys[8], 71), 0)
    swap_bit = draw_swap_bit(jax.random.fold_in(arg_keys[8], 71), 0)
    swap_slot = draw_swap_slot(jax.random.fold_in(arg_keys[8], 71), 0)
    return dict(block_state=block_state, block_level=block_level, block_velocity=block_velocity, diffusivity=diffusivity, reaction_matrix=reaction_matrix, ghost_source=ghost_source, swap_bit=swap_bit, swap_slot=swap_slot)


dt_base = 0.05


def face_layer(donor, face_no):
    layers = [donor[:, 0], donor[:, -1], donor[:, :, 0], donor[:, :, -1], donor[:, :, :, 0], donor[:, :, :, -1]]
    return layers[face_no]


def coarsen_face(layer):
    fields, rows, cols = layer.shape
    means = jnp.mean(layer.reshape(fields, rows // 2, 2, cols // 2, 2), axis=(2, 4))
    return jnp.repeat(jnp.repeat(means, 2, axis=1), 2, axis=2)


def upwind_term(values, minus, plus, speed):
    return jnp.maximum(speed, 0.0) * (values - minus) + jnp.minimum(speed, 0.0) * (plus - values)


def advance(species_field, layers, own_level, velocity, diffusivity, reaction_matrix):
    substeps = jnp.left_shift(jnp.int32(1), own_level)
    scale = substeps.astype(jnp.float32)
    step_size = dt_base / scale
    rates = diffusivity[:, None, None, None]

    def substep(index, values):
        minus_x = jnp.concatenate([layers[0][:, None], values[:, :-1]], axis=1)
        plus_x = jnp.concatenate([values[:, 1:], layers[1][:, None]], axis=1)
        minus_y = jnp.concatenate([layers[2][:, :, None], values[:, :, :-1]], axis=2)
        plus_y = jnp.concatenate([values[:, :, 1:], layers[3][:, :, None]], axis=2)
        negative_depth_face = jnp.concatenate([layers[4][..., None], values[..., :-1]], axis=3)
        plus_z = jnp.concatenate([values[..., 1:], layers[5][..., None]], axis=3)
        diffused_field = (minus_x + plus_x) + (minus_y + plus_y) + (negative_depth_face + plus_z) - 6.0 * values
        upwind = (upwind_term(values, minus_x, plus_x, velocity[0])
                  + upwind_term(values, minus_y, plus_y, velocity[1])
                  + upwind_term(values, negative_depth_face, plus_z, velocity[2]))
        sender_rank = jnp.einsum("fg,gxyz->fxyz", reaction_matrix, values, precision=lax.Precision.HIGHEST)
        change = rates * diffused_field * (scale * scale) - upwind * scale + sender_rank
        return values + step_size * change

    return lax.fori_loop(jnp.int32(0), substeps, substep, species_field)


def reference(block_state, block_level, block_velocity, diffusivity, reaction_matrix, ghost_source, swap_bit, swap_slot):
    slab = N_GY * N_GZ
    total = N_GX * SLAB_BLOCKS

    def per_block(index):
        slab_no = index // SLAB_BLOCKS
        row_no = index % SLAB_BLOCKS
        species_field = block_state[slab_no, row_no].astype(jnp.float32).reshape(F, B, B, B)
        own_level = block_level[slab_no, row_no]
        layers = []
        for face_no in range(6):
            sender_rank = ghost_source[slab_no, row_no, face_no]
            donor = block_state[slab_no, sender_rank].astype(jnp.float32).reshape(F, B, B, B)
            layer = face_layer(donor, face_no ^ 1)
            layers.append(jnp.where(block_level[slab_no, sender_rank] != own_level, coarsen_face(layer), layer))
        velocity = block_velocity[slab_no, row_no].astype(jnp.float32)
        result = advance(species_field, layers, own_level, velocity, diffusivity, reaction_matrix)
        return result.astype(jnp.bfloat16).reshape(F, B, B * B)

    fresh = lax.map(per_block, jnp.arange(total, dtype=jnp.int32)).reshape(N_GX, SLAB_BLOCKS, F, B, B * B)
    bits = swap_bit.reshape(N_GX, slab).astype(jnp.int32)
    slots = swap_slot.reshape(N_GX, slab).astype(jnp.int32)
    slab_ids = jnp.arange(N_GX, dtype=jnp.int32)[:, None]
    column = jnp.arange(slab, dtype=jnp.int32)[None, :]
    flips = jnp.where(bits < 0, jnp.int32(0), jnp.left_shift(jnp.int32(1), jnp.maximum(bits, 0)))
    partner = jnp.bitwise_xor(slab_ids, flips)
    partner_slot = slots[partner, column]
    within = jnp.arange(NB, dtype=jnp.int32)[None, None, :]
    traded = within == slots[:, :, None]
    from_slab = jnp.where(traded, partner[:, :, None], slab_ids[:, :, None])
    from_row = column[:, :, None] * NB + jnp.where(traded, partner_slot[:, :, None], within)
    return fresh[from_slab.reshape(N_GX, SLAB_BLOCKS), from_row.reshape(N_GX, SLAB_BLOCKS)]
```

```python
import functools

import jax
import jax.numpy as jnp
from jax import lax
from jax.experimental import pallas as pl
from jax.experimental.pallas import tpu as pltpu
from jax.sharding import PartitionSpec as P

f32 = jnp.float32
bf16 = jnp.bfloat16
dt_base = 0.05
LANES = 128
ROWS = 8
PAD = 8


def swapped(x, axis, bit):
    return lax.ppermute(x, axis, [(i, i ^ 1 << bit) for i in range(lax.axis_size(axis))])


def lane_roll(x, shift):
    shift = shift % LANES
    return x if shift == 0 else pltpu.roll(x, shift, x.ndim - 1)


def pack_kernel(send_ref, u_ref, o_ref, sel_ref, face_ref):
    blk = pl.program_id(0)
    _, fields, cells, plane = u_ref.shape
    groups = LANES // cells
    tiles = plane // LANES

    @pl.when(blk == 0)
    def _():
        row = lax.broadcasted_iota(jnp.int32, sel_ref.shape, 0)
        col = lax.broadcasted_iota(jnp.int32, sel_ref.shape, 1)
        high = col // LANES
        within = col % LANES
        t = within % cells
        jj = within // cells
        source = (groups * t + jj) * cells + high * (cells - 1)
        sel_ref[...] = jnp.where((t < tiles) & (row == source), 1.0, 0.0).astype(bf16)

    lane = lax.broadcasted_iota(jnp.int32, (1, ROWS, LANES), 2)

    def put(face_no, value):
        face_ref[blk * 6 + face_no] = value.reshape(fields * ROWS, LANES).astype(bf16)

    for face_no, edge in ((0, 0), (1, cells - 1)):
        pieces = [
            u_ref[0, :, edge : edge + 1, pl.ds(LANES * t, LANES)].astype(f32)
            for t in range(tiles)
        ]
        put(face_no, jnp.concatenate(pieces, axis=1))
    for face_no, tile, group in ((2, 0, 0), (3, tiles - 1, groups - 1)):
        strip = u_ref[0, :, :, pl.ds(LANES * tile, LANES)].astype(f32)
        total = jnp.zeros((fields, ROWS, LANES), f32)
        for b in range(groups):
            moved = lane_roll(strip[:, ROWS * b : ROWS * b + ROWS], cells * (b - group))
            total = jnp.where(lane // cells == b, moved, total)
        put(face_no, total)
    picked = jnp.dot(
        u_ref[0].reshape(fields * cells, plane), sel_ref[...], preferred_element_type=f32
    ).reshape(fields, cells, 2 * LANES)
    for face_no, high in ((4, 0), (5, 1)):
        total = jnp.zeros((fields, ROWS, LANES), f32)
        for b in range(groups):
            part = picked[:, ROWS * b : ROWS * b + ROWS, LANES * high : LANES * high + LANES]
            total = total + lane_roll(part, tiles * b)
        put(face_no, total)

    @pl.when(blk == pl.num_programs(0) - 1)
    def _():
        def copy(slot, carry):
            o_ref[slot] = face_ref[send_ref[slot]]
            return carry

        lax.fori_loop(0, o_ref.shape[0], copy, 0)


def pack_faces(blocks, send, slots):
    per_dev, fields, cells, plane = blocks.shape
    return pl.pallas_call(
        pack_kernel,
        grid_spec=pltpu.PrefetchScalarGridSpec(
            num_scalar_prefetch=1,
            grid=(per_dev,),
            in_specs=[pl.BlockSpec((1, fields, cells, plane), lambda b, s: (b, 0, 0, 0))],
            out_specs=pl.BlockSpec((slots, fields * ROWS, LANES), lambda b, s: (0, 0, 0)),
            scratch_shapes=[
                pltpu.VMEM((plane, 2 * LANES), bf16),
                pltpu.VMEM((per_dev * 6, fields * ROWS, LANES), bf16),
            ],
        ),
        out_shape=jax.ShapeDtypeStruct((slots, fields * ROWS, LANES), bf16),
        compiler_params=pltpu.CompilerParams(vmem_limit_bytes=32 << 20),
        name="pack_faces",
    )(send, blocks)


def advance_kernel(first, per_dev, ints_ref, vals_ref, u_ref, arr_ref, o_ref, sa_ref, sb_ref, e_ref, rk_ref):
    _, fields, cells, plane = u_ref.shape
    groups = LANES // cells
    tiles = plane // LANES
    blk = ints_ref[pl.program_id(0) + first]
    level = ints_ref[per_dev + blk]
    lookup = lambda q: ints_ref[2 * per_dev + q]
    coarse = lambda q: ints_ref[2 * per_dev + 6 * per_dev + q]
    velocity = [vals_ref[blk * 3 + d] for d in range(3)]
    diffusivity = lambda f: vals_ref[3 * per_dev + f]
    reaction = lambda f, e: vals_ref[3 * per_dev + fields + f * fields + e]

    n = jnp.left_shift(jnp.int32(1), level)
    scale = n.astype(f32)
    dt = dt_base / scale
    lane = lax.broadcasted_iota(jnp.int32, (ROWS, LANES), 1)
    sub = lax.broadcasted_iota(jnp.int32, (ROWS, LANES), 0)
    k_first = lane % cells == 0
    k_last = lane % cells == cells - 1

    for t in range(tiles):
        for half in range(cells // 16):
            sa_ref[:, t + 1, pl.ds(PAD + 16 * half, 16), :] = u_ref[
                0, :, pl.ds(16 * half, 16), pl.ds(LANES * t, LANES)
            ].astype(f32)

    def pair_lanes(x, step):
        even = ((lane // step) % 2 == 0)[None]
        return x + jnp.where(even, lane_roll(x, -step), lane_roll(x, step))

    def pair_rows(x):
        even = (sub % 2 == 0)[None]
        return x + jnp.where(even, pltpu.roll(x, ROWS - 1, 1), pltpu.roll(x, 1, 1))

    def face(face_no, pair_a, pair_b):
        q = blk * 6 + face_no
        layer = arr_ref[lookup(q)].astype(f32).reshape(fields, ROWS, LANES)
        return jnp.where(coarse(q) > 0, pair_b(pair_a(layer)) * 0.25, layer)

    by_cells = lambda x: pair_lanes(x, cells)
    by_one = lambda x: pair_lanes(x, 1)
    states = (sa_ref, sb_ref)
    low, high = face(0, by_cells, by_one), face(1, by_cells, by_one)
    for state in states:
        for t in range(tiles):
            state[:, t + 1, PAD - 1 : PAD, :] = low[:, t : t + 1, :]
            state[:, t + 1, PAD + cells : PAD + cells + 1, :] = high[:, t : t + 1, :]
    low, high = face(2, by_one, pair_rows), face(3, by_one, pair_rows)
    for b in range(groups):
        low_b = lane_roll(low, cells * (groups - 1 - b))
        high_b = lane_roll(high, -cells * b)
        for state in states:
            state[:, 0, pl.ds(PAD + ROWS * b, ROWS), :] = low_b
            state[:, tiles + 1, pl.ds(PAD + ROWS * b, ROWS), :] = high_b
    low, high = face(4, by_cells, pair_rows), face(5, by_cells, pair_rows)
    for b in range(groups):
        for t in range(tiles):
            at = tiles * b + t
            e_ref[:, t, pl.ds(ROWS * b, ROWS), :] = jnp.where(
                k_first[None], lane_roll(low, -at), lane_roll(high, cells - 1 - at)
            )

    adv = dt * scale
    dif = dt * scale * scale
    minus = [adv * jnp.maximum(v, 0.0) for v in velocity]
    plus = [-(adv * jnp.minimum(v, 0.0)) for v in velocity]
    outflow = sum(minus) + sum(plus)
    rates = [dif * diffusivity(f) for f in range(fields)]

    size = fields * ROWS
    ri = lax.broadcasted_iota(jnp.int32, (size, size), 0)
    ci = lax.broadcasted_iota(jnp.int32, (size, size), 1)
    matrix = jnp.zeros((size, size), f32)
    for f in range(fields):
        line = jnp.zeros((size, size), f32)
        for e in range(fields):
            term = dt * reaction(f, e)
            if e == f:
                term = term - (6.0 * rates[f] + outflow)
            line = jnp.where(ci // ROWS == e, term, line)
        matrix = jnp.where(ri // ROWS == f, line, matrix)
    matrix = jnp.where(ri % ROWS == ci % ROWS, matrix, 0.0)
    matrix_high = matrix.astype(bf16)
    rk_ref[:, 0:size] = matrix_high
    rk_ref[:, size : 2 * size] = (matrix - matrix_high.astype(f32)).astype(bf16)
    rk_ref[:, 2 * size : 3 * size] = matrix_high

    def substep(src, dst):
        own = rk_ref[...]

        def two_tiles(pair, carry):
            for it in range(cells // ROWS):
                row = PAD + ROWS * it
                centre = [
                    [src[f, 2 * pair + 1 + q, pl.ds(row, ROWS), :] for f in range(fields)]
                    for q in range(2)
                ]
                both = jnp.concatenate([jnp.concatenate(c, axis=0) for c in centre], axis=1)
                both_high = both.astype(bf16)
                both_low = (both - both_high.astype(f32)).astype(bf16)
                stacked = jnp.concatenate([both_high, both_high, both_low], axis=0)
                mixed = jnp.dot(own, stacked, preferred_element_type=f32)
                for q in range(2):
                    t = 2 * pair + q
                    for f in range(fields):
                        c = centre[q][f]
                        minus_x = src[f, t + 1, pl.ds(row - 1, ROWS), :]
                        plus_x = src[f, t + 1, pl.ds(row + 1, ROWS), :]
                        left = src[f, t, pl.ds(row, ROWS), :]
                        right = src[f, t + 2, pl.ds(row, ROWS), :]
                        edge = e_ref[f, t, pl.ds(ROWS * it, ROWS), :]
                        minus_y = lane_roll(jnp.where(lane >= LANES - cells, left, c), cells)
                        plus_y = lane_roll(jnp.where(lane < cells, right, c), -cells)
                        minus_z = jnp.where(k_first, edge, lane_roll(c, 1))
                        plus_z = jnp.where(k_last, edge, lane_roll(c, -1))
                        near = (rates[f] + minus[0]) * minus_x + (rates[f] + plus[0]) * plus_x
                        near += (rates[f] + minus[1]) * minus_y + (rates[f] + plus[1]) * plus_y
                        near += (rates[f] + minus[2]) * minus_z + (rates[f] + plus[2]) * plus_z
                        own_terms = mixed[ROWS * f : ROWS * f + ROWS, LANES * q : LANES * q + LANES]
                        dst[f, t + 1, pl.ds(row, ROWS), :] = near + (c + own_terms)
            return carry

        lax.fori_loop(0, tiles // 2, two_tiles, 0)

    def finish(src):
        for t in range(tiles):
            for half in range(cells // 16):
                o_ref[0, :, pl.ds(16 * half, 16), pl.ds(LANES * t, LANES)] = src[
                    :, t + 1, pl.ds(PAD + 16 * half, 16), :
                ].astype(bf16)

    @pl.when(n == 1)
    def _():
        substep(sa_ref, sb_ref)
        finish(sb_ref)

    @pl.when(n > 1)
    def _():
        def two(i, carry):
            substep(sa_ref, sb_ref)
            substep(sb_ref, sa_ref)
            return carry

        lax.fori_loop(0, n // 2, two, 0)
        finish(sa_ref)


def advance(ints, vals, blocks, arrived, first, count, slots_out):
    per_dev, fields, cells, plane = blocks.shape
    tiles = plane // LANES
    shape = (1, fields, cells, plane)
    if slots_out == 1:
        out_map = lambda b, i, v: (0, 0, 0, 0)
    else:
        out_map = lambda b, i, v: (i[b + first], 0, 0, 0)
    return pl.pallas_call(
        functools.partial(advance_kernel, first, per_dev),
        grid_spec=pltpu.PrefetchScalarGridSpec(
            num_scalar_prefetch=2,
            grid=(count,),
            in_specs=[
                pl.BlockSpec(shape, lambda b, i, v: (i[b + first], 0, 0, 0)),
                pl.BlockSpec(arrived.shape, lambda b, i, v: (0, 0, 0)),
            ],
            out_specs=pl.BlockSpec(shape, out_map),
            scratch_shapes=[
                pltpu.VMEM((fields, tiles + 2, cells + 2 * PAD, LANES), f32),
                pltpu.VMEM((fields, tiles + 2, cells + 2 * PAD, LANES), f32),
                pltpu.VMEM((fields, tiles, cells, LANES), f32),
                pltpu.VMEM((fields * ROWS, 3 * fields * ROWS), bf16),
            ],
        ),
        out_shape=jax.ShapeDtypeStruct((slots_out, fields, cells, plane), bf16),
        compiler_params=pltpu.CompilerParams(vmem_limit_bytes=40 << 20),
        name="advance",
    )(ints, vals, blocks, arrived)


def plan(wanted, my_index, per_dev):
    peers, requests = wanted.shape
    at = lax.broadcasted_iota(jnp.int32, wanted.shape, 1)
    source_dev = wanted // per_dev
    code = wanted % per_dev * 6 + jnp.bitwise_xor(at % 6, 1)
    key = at * 64 + code
    match = source_dev == my_index
    first = jnp.min(jnp.where(match, key, 64 * requests), axis=1) % 64
    second = jnp.maximum(jnp.max(jnp.where(match, key, 0), axis=1), 0) % 64
    send = jnp.stack([first, second], axis=1).reshape(2 * peers)
    mine = lax.dynamic_slice_in_dim(wanted, my_index, 1, 0)[0]
    my_source = mine // per_dev
    order = jnp.arange(requests, dtype=jnp.int32)
    repeated = (my_source[:, None] == my_source[None, :]) & (order[None, :] < order[:, None])
    lookup = my_source * 2 + jnp.any(repeated, axis=1).astype(jnp.int32)
    return send, mine, lookup


def local(
    block_state,
    block_level,
    block_velocity,
    diffusivity,
    reaction_matrix,
    ghost_source,
    swap_bit,
    swap_slot,
):
    blocks = block_state[0]
    per_dev, fields, cells, plane = blocks.shape
    peers = lax.axis_size(("gy", "gz"))
    my_index = lax.axis_index(("gy", "gz"))
    levels = block_level[0]
    wanted = ghost_source[0].reshape(peers, per_dev * 6)
    send, mine, lookup = plan(wanted, my_index, per_dev)
    outgoing = pack_faces(blocks, send, 2 * peers)
    arrived = lax.all_to_all(outgoing, ("gy", "gz"), split_axis=0, concat_axis=0, tiled=True)

    own_levels = lax.dynamic_slice_in_dim(levels, my_index * per_dev, per_dev, 0)
    known = mine[:, None] == jnp.arange(levels.shape[0], dtype=jnp.int32)[None, :]
    source_levels = jnp.sum(jnp.where(known, levels[None, :], 0), axis=1)
    coarse = (source_levels.reshape(per_dev, 6) != own_levels[:, None]).astype(jnp.int32)
    bit_here = swap_bit[0, 0, 0]
    slot_here = swap_slot[0, 0, 0]
    rest = jnp.arange(per_dev, dtype=jnp.int32)
    rest = jnp.where(rest == 0, slot_here, rest - (rest <= slot_here))
    ints = jnp.concatenate([rest, own_levels, lookup, coarse.reshape(-1)])
    vals = jnp.concatenate(
        [block_velocity[0].astype(f32).reshape(-1), diffusivity, reaction_matrix.reshape(-1)]
    )
    departing = advance(ints, vals, blocks, arrived, 0, 1, 1)
    coming = departing
    for bit_no in range(lax.axis_size("gx").bit_length() - 1):
        coming = jnp.where(bit_here == bit_no, swapped(departing, "gx", bit_no), coming)
    stay = advance(ints, vals, blocks, arrived, 1, per_dev - 1, per_dev)
    result = lax.dynamic_update_slice_in_dim(stay, coming, slot_here, 0)
    return result[None]


def solution(mesh):
    in_specs = (
        P("gx", ("gy", "gz"), None, None, None),
        P("gx", None),
        P("gx", ("gy", "gz"), None),
        P(),
        P(),
        P("gx", None, None),
        P("gx", "gy", "gz"),
        P("gx", "gy", "gz"),
    )
    out_specs = P("gx", ("gy", "gz"), None, None, None)
    return jax.shard_map(local, mesh=mesh, in_specs=in_specs, out_specs=out_specs, check_vma=False)
```

```python
import functools

import jax
import jax.numpy as jnp
from jax import lax
from jax.experimental import pallas as pl
from jax.experimental.pallas import tpu as pltpu
from jax.sharding import PartitionSpec as P

f32 = jnp.float32
bf16 = jnp.bfloat16
dt_base = 0.05
LANES = 128
ROWS = 8
PAD = 8


def swapped(x, axis, bit):
    return lax.ppermute(x, axis, [(i, i ^ 1 << bit) for i in range(lax.axis_size(axis))])


def lane_roll(x, shift):
    shift = shift % LANES
    return x if shift == 0 else pltpu.roll(x, shift, x.ndim - 1)


def pack_kernel(send_ref, u_ref, o_ref, sel_ref, face_ref):
    blk = pl.program_id(0)
    _, fields, cells, plane = u_ref.shape
    groups = LANES // cells
    tiles = plane // LANES

    @pl.when(blk == 0)
    def _():
        row = lax.broadcasted_iota(jnp.int32, sel_ref.shape, 0)
        col = lax.broadcasted_iota(jnp.int32, sel_ref.shape, 1)
        high = col // LANES
        within = col % LANES
        t = within % cells
        jj = within // cells
        source = (groups * t + jj) * cells + high * (cells - 1)
        sel_ref[...] = jnp.where((t < tiles) & (row == source), 1.0, 0.0).astype(bf16)

    lane = lax.broadcasted_iota(jnp.int32, (1, ROWS, LANES), 2)

    def put(face_no, value):
        face_ref[blk * 6 + face_no] = value.reshape(fields * ROWS, LANES).astype(bf16)

    for face_no, edge in ((0, 0), (1, cells - 1)):
        pieces = [
            u_ref[0, :, edge : edge + 1, pl.ds(LANES * t, LANES)].astype(f32)
            for t in range(tiles)
        ]
        put(face_no, jnp.concatenate(pieces, axis=1))
    for face_no, tile, group in ((2, 0, 0), (3, tiles - 1, groups - 1)):
        strip = u_ref[0, :, :, pl.ds(LANES * tile, LANES)].astype(f32)
        total = jnp.zeros((fields, ROWS, LANES), f32)
        for b in range(groups):
            moved = lane_roll(strip[:, ROWS * b : ROWS * b + ROWS], cells * (b - group))
            total = jnp.where(lane // cells == b, moved, total)
        put(face_no, total)
    picked = jnp.dot(
        u_ref[0].reshape(fields * cells, plane), sel_ref[...], preferred_element_type=f32
    ).reshape(fields, cells, 2 * LANES)
    for face_no, high in ((4, 0), (5, 1)):
        total = jnp.zeros((fields, ROWS, LANES), f32)
        for b in range(groups):
            part = picked[:, ROWS * b : ROWS * b + ROWS, LANES * high : LANES * high + LANES]
            total = total + lane_roll(part, tiles * b)
        put(face_no, total)

    @pl.when(blk == pl.num_programs(0) - 1)
    def _():
        def copy(slot, carry):
            o_ref[slot] = face_ref[send_ref[slot]]
            return carry

        lax.fori_loop(0, o_ref.shape[0], copy, 0)


def pack_faces(blocks, send, slots):
    per_dev, fields, cells, plane = blocks.shape
    return pl.pallas_call(
        pack_kernel,
        grid_spec=pltpu.PrefetchScalarGridSpec(
            num_scalar_prefetch=1,
            grid=(per_dev,),
            in_specs=[pl.BlockSpec((1, fields, cells, plane), lambda b, s: (b, 0, 0, 0))],
            out_specs=pl.BlockSpec((slots, fields * ROWS, LANES), lambda b, s: (0, 0, 0)),
            scratch_shapes=[
                pltpu.VMEM((plane, 2 * LANES), bf16),
                pltpu.VMEM((per_dev * 6, fields * ROWS, LANES), bf16),
            ],
        ),
        out_shape=jax.ShapeDtypeStruct((slots, fields * ROWS, LANES), bf16),
        compiler_params=pltpu.CompilerParams(vmem_limit_bytes=32 << 20),
        name="pack_faces",
    )(send, blocks)


def coefficients(ints_ref, vals_ref, blk, per_dev, fields):
    n = jnp.left_shift(jnp.int32(1), ints_ref[per_dev + blk])
    scale = n.astype(f32)
    dt = dt_base / scale
    adv = dt * scale
    dif = dt * scale * scale
    velocity = [vals_ref[blk * 3 + d] for d in range(3)]
    minus = [adv * jnp.maximum(v, 0.0) for v in velocity]
    plus = [-(adv * jnp.minimum(v, 0.0)) for v in velocity]
    rates = [dif * vals_ref[3 * per_dev + f] for f in range(fields)]
    return n, dt, minus, plus, rates


def substep(src, put, edge_ref, own, minus, plus, rates, fields, cells, tiles):
    lane = lax.broadcasted_iota(jnp.int32, (ROWS, LANES), 1)
    k_first = lane % cells == 0
    k_last = lane % cells == cells - 1

    def two_tiles(pair, carry):
        for it in range(cells // ROWS):
            row = PAD + ROWS * it
            centre = [
                [src[f, 2 * pair + 1 + q, pl.ds(row, ROWS), :] for f in range(fields)]
                for q in range(2)
            ]
            both = jnp.concatenate([jnp.concatenate(c, axis=0) for c in centre], axis=1)
            both_high = both.astype(bf16)
            both_low = (both - both_high.astype(f32)).astype(bf16)
            stacked = jnp.concatenate([both_high, both_high, both_low], axis=0)
            mixed = jnp.dot(own, stacked, preferred_element_type=f32)
            for q in range(2):
                t = 2 * pair + q
                for f in range(fields):
                    c = centre[q][f]
                    minus_x = src[f, t + 1, pl.ds(row - 1, ROWS), :]
                    plus_x = src[f, t + 1, pl.ds(row + 1, ROWS), :]
                    left = src[f, t, pl.ds(row, ROWS), :]
                    right = src[f, t + 2, pl.ds(row, ROWS), :]
                    edge = 0.0 if edge_ref is None else edge_ref[f, t, pl.ds(ROWS * it, ROWS), :]
                    minus_y = lane_roll(jnp.where(lane >= LANES - cells, left, c), cells)
                    plus_y = lane_roll(jnp.where(lane < cells, right, c), -cells)
                    minus_z = jnp.where(k_first, edge, lane_roll(c, 1))
                    plus_z = jnp.where(k_last, edge, lane_roll(c, -1))
                    near = (rates[f] + minus[0]) * minus_x + (rates[f] + plus[0]) * plus_x
                    near += (rates[f] + minus[1]) * minus_y + (rates[f] + plus[1]) * plus_y
                    near += (rates[f] + minus[2]) * minus_z + (rates[f] + plus[2]) * plus_z
                    own_terms = mixed[ROWS * f : ROWS * f + ROWS, LANES * q : LANES * q + LANES]
                    put(f, t, it, near + (c + own_terms))
        return carry

    lax.fori_loop(0, tiles // 2, two_tiles, 0)


def first_kernel(per_dev, ints_ref, vals_ref, u_ref, o_ref, rk_out_ref, sa_ref):
    _, fields, cells, plane = u_ref.shape
    tiles = plane // LANES
    blk = pl.program_id(0)
    n, dt, minus, plus, rates = coefficients(ints_ref, vals_ref, blk, per_dev, fields)
    reaction = lambda f, e: vals_ref[3 * per_dev + fields + f * fields + e]

    @pl.when(blk == 0)
    def _():
        zeros = jnp.zeros((fields, cells + 2 * PAD, LANES), f32)
        sa_ref[:, 0] = zeros
        sa_ref[:, tiles + 1] = zeros
        sa_ref[:, :, 0:PAD] = jnp.zeros((fields, tiles + 2, PAD, LANES), f32)
        sa_ref[:, :, PAD + cells :] = jnp.zeros((fields, tiles + 2, PAD, LANES), f32)

    for t in range(tiles):
        for half in range(cells // 16):
            sa_ref[:, t + 1, pl.ds(PAD + 16 * half, 16), :] = u_ref[
                0, :, pl.ds(16 * half, 16), pl.ds(LANES * t, LANES)
            ].astype(f32)

    outflow = sum(minus) + sum(plus)
    size = fields * ROWS
    ri = lax.broadcasted_iota(jnp.int32, (size, size), 0)
    ci = lax.broadcasted_iota(jnp.int32, (size, size), 1)
    matrix = jnp.zeros((size, size), f32)
    for f in range(fields):
        line = jnp.zeros((size, size), f32)
        for e in range(fields):
            term = dt * reaction(f, e)
            if e == f:
                term = term - (6.0 * rates[f] + outflow)
            line = jnp.where(ci // ROWS == e, term, line)
        matrix = jnp.where(ri // ROWS == f, line, matrix)
    matrix = jnp.where(ri % ROWS == ci % ROWS, matrix, 0.0)
    high = matrix.astype(bf16)
    rk_out_ref[0, :, 0:size] = high
    rk_out_ref[0, :, size : 2 * size] = (matrix - high.astype(f32)).astype(bf16)
    rk_out_ref[0, :, 2 * size : 3 * size] = high

    def put(f, t, it, value):
        o_ref[0, f, t, pl.ds(ROWS * it, ROWS), :] = value

    substep(sa_ref, put, None, rk_out_ref[0], minus, plus, rates, fields, cells, tiles)


def first_substep(ints, vals, blocks):
    per_dev, fields, cells, plane = blocks.shape
    tiles = plane // LANES
    size = fields * ROWS
    return pl.pallas_call(
        functools.partial(first_kernel, per_dev),
        grid_spec=pltpu.PrefetchScalarGridSpec(
            num_scalar_prefetch=2,
            grid=(per_dev,),
            in_specs=[pl.BlockSpec((1, fields, cells, plane), lambda b, i, v: (b, 0, 0, 0))],
            out_specs=[
                pl.BlockSpec((1, fields, tiles, cells, LANES), lambda b, i, v: (b, 0, 0, 0, 0)),
                pl.BlockSpec((1, size, 3 * size), lambda b, i, v: (b, 0, 0)),
            ],
            scratch_shapes=[pltpu.VMEM((fields, tiles + 2, cells + 2 * PAD, LANES), f32)],
        ),
        out_shape=[
            jax.ShapeDtypeStruct((per_dev, fields, tiles, cells, LANES), f32),
            jax.ShapeDtypeStruct((per_dev, size, 3 * size), bf16),
        ],
        compiler_params=pltpu.CompilerParams(vmem_limit_bytes=32 << 20),
        name="first_substep",
    )(ints, vals, blocks)


def advance_kernel(first, per_dev, ints_ref, vals_ref, s_ref, rk_ref, arr_ref, o_ref, sa_ref, sb_ref, e_ref):
    _, fields, tiles, cells, _ = s_ref.shape
    groups = LANES // cells
    blk = ints_ref[pl.program_id(0) + first]
    lookup = lambda q: ints_ref[2 * per_dev + q]
    coarse = lambda q: ints_ref[2 * per_dev + 6 * per_dev + q]
    n, dt, minus, plus, rates = coefficients(ints_ref, vals_ref, blk, per_dev, fields)
    lane = lax.broadcasted_iota(jnp.int32, (ROWS, LANES), 1)
    sub = lax.broadcasted_iota(jnp.int32, (ROWS, LANES), 0)
    k_first = lane % cells == 0
    k_last = lane % cells == cells - 1

    def pair_lanes(x, step):
        even = ((lane // step) % 2 == 0)[None]
        return x + jnp.where(even, lane_roll(x, -step), lane_roll(x, step))

    def pair_rows(x):
        even = (sub % 2 == 0)[None]
        return x + jnp.where(even, pltpu.roll(x, ROWS - 1, 1), pltpu.roll(x, 1, 1))

    def face(face_no, pair_a, pair_b):
        q = blk * 6 + face_no
        layer = arr_ref[lookup(q)].astype(f32).reshape(fields, ROWS, LANES)
        return jnp.where(coarse(q) > 0, pair_b(pair_a(layer)) * 0.25, layer)

    def per_field(terms):
        return jnp.concatenate([jnp.full((1, ROWS, LANES), x, f32) for x in terms], axis=0)

    by_cells = lambda x: pair_lanes(x, cells)
    by_one = lambda x: pair_lanes(x, 1)
    states = (sa_ref, sb_ref)
    rate = per_field(rates)

    low, high = face(4, by_cells, pair_rows), face(5, by_cells, pair_rows)
    weight = jnp.where(
        k_first[None], rate + minus[2], jnp.where(k_last[None], rate + plus[2], 0.0)
    )
    for b in range(groups):
        rows = pl.ds(ROWS * b, ROWS)
        for t in range(tiles):
            at = tiles * b + t
            edge = jnp.where(k_first[None], lane_roll(low, -at), lane_roll(high, cells - 1 - at))
            e_ref[:, t, rows, :] = edge
            sa_ref[:, t + 1, pl.ds(PAD + ROWS * b, ROWS), :] = s_ref[0, :, t, rows, :] + weight * edge

    low, high = face(2, by_one, pair_rows), face(3, by_one, pair_rows)
    for b in range(groups):
        rows = pl.ds(PAD + ROWS * b, ROWS)
        low_b = lane_roll(low, -cells * b)
        high_b = lane_roll(high, cells * (groups - 1 - b))
        sa_ref[:, 1, rows, :] += jnp.where(lane < cells, (rate + minus[1]) * low_b, 0.0)
        sa_ref[:, tiles, rows, :] += jnp.where(lane >= LANES - cells, (rate + plus[1]) * high_b, 0.0)
        low_b = lane_roll(low, cells * (groups - 1 - b))
        high_b = lane_roll(high, -cells * b)
        for state in states:
            state[:, 0, rows, :] = low_b
            state[:, tiles + 1, rows, :] = high_b

    low, high = face(0, by_cells, by_one), face(1, by_cells, by_one)
    low_part = (rate + minus[0]) * low
    high_part = (rate + plus[0]) * high
    for t in range(tiles):
        sa_ref[:, t + 1, PAD : PAD + 1, :] += low_part[:, t : t + 1, :]
        sa_ref[:, t + 1, PAD + cells - 1 : PAD + cells, :] += high_part[:, t : t + 1, :]
        for state in states:
            state[:, t + 1, PAD - 1 : PAD, :] = low[:, t : t + 1, :]
            state[:, t + 1, PAD + cells : PAD + cells + 1, :] = high[:, t : t + 1, :]

    own = rk_ref[0]

    def step(src, dst):
        def put(f, t, it, value):
            dst[f, t + 1, pl.ds(PAD + ROWS * it, ROWS), :] = value

        substep(src, put, e_ref, own, minus, plus, rates, fields, cells, tiles)

    def finish(src):
        for t in range(tiles):
            for half in range(cells // 16):
                o_ref[0, :, pl.ds(16 * half, 16), pl.ds(LANES * t, LANES)] = src[
                    :, t + 1, pl.ds(PAD + 16 * half, 16), :
                ].astype(bf16)

    @pl.when(n == 1)
    def _():
        finish(sa_ref)

    @pl.when(n > 1)
    def _():
        def two(i, carry):
            step(sa_ref, sb_ref)
            step(sb_ref, sa_ref)
            return carry

        lax.fori_loop(0, (n - 2) // 2, two, 0)
        step(sa_ref, sb_ref)
        finish(sb_ref)


def advance(ints, vals, started, own, arrived, plane, first, count, slots_out):
    per_dev, fields, tiles, cells, _ = started.shape
    padded = (fields, tiles + 2, cells + 2 * PAD, LANES)
    shape = (1, fields, cells, plane)
    if slots_out == 1:
        out_map = lambda b, i, v: (0, 0, 0, 0)
    else:
        out_map = lambda b, i, v: (i[b + first], 0, 0, 0)
    return pl.pallas_call(
        functools.partial(advance_kernel, first, per_dev),
        grid_spec=pltpu.PrefetchScalarGridSpec(
            num_scalar_prefetch=2,
            grid=(count,),
            in_specs=[
                pl.BlockSpec((1,) + started.shape[1:], lambda b, i, v: (i[b + first], 0, 0, 0, 0)),
                pl.BlockSpec((1,) + own.shape[1:], lambda b, i, v: (i[b + first], 0, 0)),
                pl.BlockSpec(arrived.shape, lambda b, i, v: (0, 0, 0)),
            ],
            out_specs=pl.BlockSpec(shape, out_map),
            scratch_shapes=[
                pltpu.VMEM(padded, f32),
                pltpu.VMEM(padded, f32),
                pltpu.VMEM((fields, tiles, cells, LANES), f32),
            ],
        ),
        out_shape=jax.ShapeDtypeStruct((slots_out, fields, cells, plane), bf16),
        compiler_params=pltpu.CompilerParams(vmem_limit_bytes=40 << 20),
        name="advance",
    )(ints, vals, started, own, arrived)


def plan(wanted, my_index, per_dev):
    peers, requests = wanted.shape
    at = lax.broadcasted_iota(jnp.int32, wanted.shape, 1)
    source_dev = wanted // per_dev
    code = wanted % per_dev * 6 + jnp.bitwise_xor(at % 6, 1)
    key = at * 64 + code
    match = source_dev == my_index
    first = jnp.min(jnp.where(match, key, 64 * requests), axis=1) % 64
    second = jnp.maximum(jnp.max(jnp.where(match, key, 0), axis=1), 0) % 64
    send = jnp.stack([first, second], axis=1).reshape(2 * peers)
    mine = lax.dynamic_slice_in_dim(wanted, my_index, 1, 0)[0]
    my_source = mine // per_dev
    order = jnp.arange(requests, dtype=jnp.int32)
    repeated = (my_source[:, None] == my_source[None, :]) & (order[None, :] < order[:, None])
    lookup = my_source * 2 + jnp.any(repeated, axis=1).astype(jnp.int32)
    return send, mine, lookup


def local(
    block_state,
    block_level,
    block_velocity,
    diffusivity,
    reaction_matrix,
    ghost_source,
    swap_bit,
    swap_slot,
):
    blocks = block_state[0]
    per_dev, fields, cells, plane = blocks.shape
    peers = lax.axis_size(("gy", "gz"))
    my_index = lax.axis_index(("gy", "gz"))
    levels = block_level[0]
    wanted = ghost_source[0].reshape(peers, per_dev * 6)
    send, mine, lookup = plan(wanted, my_index, per_dev)
    outgoing = pack_faces(blocks, send, 2 * peers)
    arrived = lax.all_to_all(outgoing, ("gy", "gz"), split_axis=0, concat_axis=0, tiled=True)

    own_levels = lax.dynamic_slice_in_dim(levels, my_index * per_dev, per_dev, 0)
    known = mine[:, None] == jnp.arange(levels.shape[0], dtype=jnp.int32)[None, :]
    source_levels = jnp.sum(jnp.where(known, levels[None, :], 0), axis=1)
    coarse = (source_levels.reshape(per_dev, 6) != own_levels[:, None]).astype(jnp.int32)
    bit_here = swap_bit[0, 0, 0]
    slot_here = swap_slot[0, 0, 0]
    rest = jnp.arange(per_dev, dtype=jnp.int32)
    rest = jnp.where(rest == 0, slot_here, rest - (rest <= slot_here))
    ints = jnp.concatenate([rest, own_levels, lookup, coarse.reshape(-1)])
    vals = jnp.concatenate(
        [block_velocity[0].astype(f32).reshape(-1), diffusivity, reaction_matrix.reshape(-1)]
    )
    started, own = first_substep(ints, vals, blocks)
    departing = advance(ints, vals, started, own, arrived, plane, 0, 1, 1)
    coming = departing
    for bit_no in range(lax.axis_size("gx").bit_length() - 1):
        coming = jnp.where(bit_here == bit_no, swapped(departing, "gx", bit_no), coming)
    stay = advance(ints, vals, started, own, arrived, plane, 1, per_dev - 1, per_dev)
    result = lax.dynamic_update_slice_in_dim(stay, coming, slot_here, 0)
    return result[None]


def solution(mesh):
    in_specs = (
        P("gx", ("gy", "gz"), None, None, None),
        P("gx", None),
        P("gx", ("gy", "gz"), None),
        P(),
        P(),
        P("gx", None, None),
        P("gx", "gy", "gz"),
        P("gx", "gy", "gz"),
    )
    out_specs = P("gx", ("gy", "gz"), None, None, None)
    return jax.shard_map(local, mesh=mesh, in_specs=in_specs, out_specs=out_specs, check_vma=False)
```

```python
import functools

import jax
import jax.numpy as jnp
from jax import lax
from jax.experimental import pallas as pl
from jax.experimental.pallas import tpu as pltpu
from jax.sharding import PartitionSpec as P

f32 = jnp.float32
bf16 = jnp.bfloat16
dt_base = 0.05
LANES = 128
ROWS = 8
PAD = 8


def swapped(x, axis, bit):
    return lax.ppermute(x, axis, [(i, i ^ 1 << bit) for i in range(lax.axis_size(axis))])


def lane_roll(x, shift):
    shift = shift % LANES
    return x if shift == 0 else pltpu.roll(x, shift, x.ndim - 1)


def in_hbm(x):
    return pltpu.with_memory_space_constraint(x, pltpu.HBM)


def pack_kernel(send_ref, u_ref, o_ref, sel_ref, face_ref):
    blk = pl.program_id(0)
    _, fields, cells, plane = u_ref.shape
    groups = LANES // cells
    tiles = plane // LANES

    @pl.when(blk == 0)
    def _():
        row = lax.broadcasted_iota(jnp.int32, sel_ref.shape, 0)
        col = lax.broadcasted_iota(jnp.int32, sel_ref.shape, 1)
        high = col // LANES
        within = col % LANES
        t = within % cells
        jj = within // cells
        source = (groups * t + jj) * cells + high * (cells - 1)
        sel_ref[...] = jnp.where((t < tiles) & (row == source), 1.0, 0.0).astype(bf16)

    lane = lax.broadcasted_iota(jnp.int32, (1, ROWS, LANES), 2)

    def put(face_no, value):
        face_ref[blk * 6 + face_no] = value.reshape(fields * ROWS, LANES).astype(bf16)

    for face_no, edge in ((0, 0), (1, cells - 1)):
        pieces = [
            u_ref[0, :, edge : edge + 1, pl.ds(LANES * t, LANES)].astype(f32)
            for t in range(tiles)
        ]
        put(face_no, jnp.concatenate(pieces, axis=1))
    for face_no, tile, group in ((2, 0, 0), (3, tiles - 1, groups - 1)):
        strip = u_ref[0, :, :, pl.ds(LANES * tile, LANES)].astype(f32)
        total = jnp.zeros((fields, ROWS, LANES), f32)
        for b in range(groups):
            moved = lane_roll(strip[:, ROWS * b : ROWS * b + ROWS], cells * (b - group))
            total = jnp.where(lane // cells == b, moved, total)
        put(face_no, total)
    picked = jnp.dot(
        u_ref[0].reshape(fields * cells, plane), sel_ref[...], preferred_element_type=f32
    ).reshape(fields, cells, 2 * LANES)
    for face_no, high in ((4, 0), (5, 1)):
        total = jnp.zeros((fields, ROWS, LANES), f32)
        for b in range(groups):
            part = picked[:, ROWS * b : ROWS * b + ROWS, LANES * high : LANES * high + LANES]
            total = total + lane_roll(part, tiles * b)
        put(face_no, total)

    @pl.when(blk == pl.num_programs(0) - 1)
    def _():
        def copy(slot, carry):
            o_ref[slot] = face_ref[send_ref[slot]]
            return carry

        lax.fori_loop(0, o_ref.shape[0], copy, 0)


def pack_faces(blocks, send, slots):
    per_dev, fields, cells, plane = blocks.shape
    return pl.pallas_call(
        pack_kernel,
        grid_spec=pltpu.PrefetchScalarGridSpec(
            num_scalar_prefetch=1,
            grid=(per_dev,),
            in_specs=[pl.BlockSpec((1, fields, cells, plane), lambda b, s: (b, 0, 0, 0))],
            out_specs=pl.BlockSpec((slots, fields * ROWS, LANES), lambda b, s: (0, 0, 0)),
            scratch_shapes=[
                pltpu.VMEM((plane, 2 * LANES), bf16),
                pltpu.VMEM((per_dev * 6, fields * ROWS, LANES), bf16),
            ],
        ),
        out_shape=jax.ShapeDtypeStruct((slots, fields * ROWS, LANES), bf16),
        compiler_params=pltpu.CompilerParams(vmem_limit_bytes=16 << 20),
        name="pack_faces",
    )(send, in_hbm(blocks))


def coefficients(ints_ref, vals_ref, blk, per_dev, fields):
    n = jnp.left_shift(jnp.int32(1), ints_ref[per_dev + blk])
    scale = n.astype(f32)
    dt = dt_base / scale
    adv = dt * scale
    dif = dt * scale * scale
    velocity = [vals_ref[blk * 3 + d] for d in range(3)]
    minus = [adv * jnp.maximum(v, 0.0) for v in velocity]
    plus = [-(adv * jnp.minimum(v, 0.0)) for v in velocity]
    rates = [dif * vals_ref[3 * per_dev + f] for f in range(fields)]
    return n, dt, minus, plus, rates


def substep(src, put, edge_ref, own, minus, plus, rates, fields, cells, tiles):
    lane = lax.broadcasted_iota(jnp.int32, (ROWS, LANES), 1)
    k_first = lane % cells == 0
    k_last = lane % cells == cells - 1

    def two_tiles(pair, carry):
        for it in range(cells // ROWS):
            row = PAD + ROWS * it
            centre = [
                [src[f, 2 * pair + 1 + q, pl.ds(row, ROWS), :] for f in range(fields)]
                for q in range(2)
            ]
            both = jnp.concatenate([jnp.concatenate(c, axis=0) for c in centre], axis=1)
            both_high = both.astype(bf16)
            both_low = (both - both_high.astype(f32)).astype(bf16)
            stacked = jnp.concatenate([both_high, both_high, both_low], axis=0)
            mixed = jnp.dot(own, stacked, preferred_element_type=f32)
            for q in range(2):
                t = 2 * pair + q
                for f in range(fields):
                    c = centre[q][f]
                    minus_x = src[f, t + 1, pl.ds(row - 1, ROWS), :]
                    plus_x = src[f, t + 1, pl.ds(row + 1, ROWS), :]
                    left = src[f, t, pl.ds(row, ROWS), :]
                    right = src[f, t + 2, pl.ds(row, ROWS), :]
                    edge = 0.0 if edge_ref is None else edge_ref[f, t, pl.ds(ROWS * it, ROWS), :]
                    minus_y = lane_roll(jnp.where(lane >= LANES - cells, left, c), cells)
                    plus_y = lane_roll(jnp.where(lane < cells, right, c), -cells)
                    minus_z = jnp.where(k_first, edge, lane_roll(c, 1))
                    plus_z = jnp.where(k_last, edge, lane_roll(c, -1))
                    near = (rates[f] + minus[0]) * minus_x + (rates[f] + plus[0]) * plus_x
                    near += (rates[f] + minus[1]) * minus_y + (rates[f] + plus[1]) * plus_y
                    near += (rates[f] + minus[2]) * minus_z + (rates[f] + plus[2]) * plus_z
                    own_terms = mixed[ROWS * f : ROWS * f + ROWS, LANES * q : LANES * q + LANES]
                    put(f, t, it, near + (c + own_terms))
        return carry

    lax.fori_loop(0, tiles // 2, two_tiles, 0)


def first_kernel(first, per_dev, ints_ref, vals_ref, u_ref, o_ref, rk_out_ref, sa_ref):
    _, fields, cells, plane = u_ref.shape
    tiles = plane // LANES
    blk = ints_ref[pl.program_id(0) + first]
    n, dt, minus, plus, rates = coefficients(ints_ref, vals_ref, blk, per_dev, fields)
    reaction = lambda f, e: vals_ref[3 * per_dev + fields + f * fields + e]

    @pl.when(pl.program_id(0) == 0)
    def _():
        zeros = jnp.zeros((fields, cells + 2 * PAD, LANES), f32)
        sa_ref[:, 0] = zeros
        sa_ref[:, tiles + 1] = zeros
        sa_ref[:, :, 0:PAD] = jnp.zeros((fields, tiles + 2, PAD, LANES), f32)
        sa_ref[:, :, PAD + cells :] = jnp.zeros((fields, tiles + 2, PAD, LANES), f32)

    for t in range(tiles):
        for half in range(cells // 16):
            sa_ref[:, t + 1, pl.ds(PAD + 16 * half, 16), :] = u_ref[
                0, :, pl.ds(16 * half, 16), pl.ds(LANES * t, LANES)
            ].astype(f32)

    outflow = sum(minus) + sum(plus)
    size = fields * ROWS
    ri = lax.broadcasted_iota(jnp.int32, (size, size), 0)
    ci = lax.broadcasted_iota(jnp.int32, (size, size), 1)
    matrix = jnp.zeros((size, size), f32)
    for f in range(fields):
        line = jnp.zeros((size, size), f32)
        for e in range(fields):
            term = dt * reaction(f, e)
            if e == f:
                term = term - (6.0 * rates[f] + outflow)
            line = jnp.where(ci // ROWS == e, term, line)
        matrix = jnp.where(ri // ROWS == f, line, matrix)
    matrix = jnp.where(ri % ROWS == ci % ROWS, matrix, 0.0)
    high = matrix.astype(bf16)
    rk_out_ref[0, :, 0:size] = high
    rk_out_ref[0, :, size : 2 * size] = (matrix - high.astype(f32)).astype(bf16)
    rk_out_ref[0, :, 2 * size : 3 * size] = high

    def put(f, t, it, value):
        o_ref[0, f, t, pl.ds(ROWS * it, ROWS), :] = value

    substep(sa_ref, put, None, rk_out_ref[0], minus, plus, rates, fields, cells, tiles)


def first_substep(ints, vals, blocks, first, count):
    per_dev, fields, cells, plane = blocks.shape
    tiles = plane // LANES
    size = fields * ROWS
    return pl.pallas_call(
        functools.partial(first_kernel, first, per_dev),
        grid_spec=pltpu.PrefetchScalarGridSpec(
            num_scalar_prefetch=2,
            grid=(count,),
            in_specs=[
                pl.BlockSpec((1, fields, cells, plane), lambda b, i, v: (i[b + first], 0, 0, 0))
            ],
            out_specs=[
                pl.BlockSpec((1, fields, tiles, cells, LANES), lambda b, i, v: (b, 0, 0, 0, 0)),
                pl.BlockSpec((1, size, 3 * size), lambda b, i, v: (b, 0, 0)),
            ],
            scratch_shapes=[pltpu.VMEM((fields, tiles + 2, cells + 2 * PAD, LANES), f32)],
        ),
        out_shape=[
            jax.ShapeDtypeStruct((count, fields, tiles, cells, LANES), f32),
            jax.ShapeDtypeStruct((count, size, 3 * size), bf16),
        ],
        compiler_params=pltpu.CompilerParams(vmem_limit_bytes=16 << 20),
        name="first_substep",
    )(ints, vals, in_hbm(blocks))


def advance_kernel(first, per_dev, ints_ref, vals_ref, s_ref, rk_ref, arr_ref, *rest):
    o_ref, sa_ref, sb_ref, e_ref = rest[-4:]
    _, fields, tiles, cells, _ = s_ref.shape
    groups = LANES // cells
    blk = ints_ref[pl.program_id(0) + first]
    lookup = lambda q: ints_ref[2 * per_dev + q]
    coarse = lambda q: ints_ref[2 * per_dev + 6 * per_dev + q]
    n, dt, minus, plus, rates = coefficients(ints_ref, vals_ref, blk, per_dev, fields)
    lane = lax.broadcasted_iota(jnp.int32, (ROWS, LANES), 1)
    sub = lax.broadcasted_iota(jnp.int32, (ROWS, LANES), 0)
    k_first = lane % cells == 0
    k_last = lane % cells == cells - 1

    def pair_lanes(x, step):
        even = ((lane // step) % 2 == 0)[None]
        return x + jnp.where(even, lane_roll(x, -step), lane_roll(x, step))

    def pair_rows(x):
        even = (sub % 2 == 0)[None]
        return x + jnp.where(even, pltpu.roll(x, ROWS - 1, 1), pltpu.roll(x, 1, 1))

    def face(face_no, pair_a, pair_b):
        q = blk * 6 + face_no
        layer = arr_ref[lookup(q)].astype(f32).reshape(fields, ROWS, LANES)
        return jnp.where(coarse(q) > 0, pair_b(pair_a(layer)) * 0.25, layer)

    def per_field(terms):
        return jnp.concatenate([jnp.full((1, ROWS, LANES), x, f32) for x in terms], axis=0)

    by_cells = lambda x: pair_lanes(x, cells)
    by_one = lambda x: pair_lanes(x, 1)
    states = (sa_ref, sb_ref)
    rate = per_field(rates)

    low, high = face(4, by_cells, pair_rows), face(5, by_cells, pair_rows)
    weight = jnp.where(
        k_first[None], rate + minus[2], jnp.where(k_last[None], rate + plus[2], 0.0)
    )
    for b in range(groups):
        rows = pl.ds(ROWS * b, ROWS)
        for t in range(tiles):
            at = tiles * b + t
            edge = jnp.where(k_first[None], lane_roll(low, -at), lane_roll(high, cells - 1 - at))
            e_ref[:, t, rows, :] = edge
            sa_ref[:, t + 1, pl.ds(PAD + ROWS * b, ROWS), :] = s_ref[0, :, t, rows, :] + weight * edge

    low, high = face(2, by_one, pair_rows), face(3, by_one, pair_rows)
    for b in range(groups):
        rows = pl.ds(PAD + ROWS * b, ROWS)
        low_b = lane_roll(low, -cells * b)
        high_b = lane_roll(high, cells * (groups - 1 - b))
        sa_ref[:, 1, rows, :] += jnp.where(lane < cells, (rate + minus[1]) * low_b, 0.0)
        sa_ref[:, tiles, rows, :] += jnp.where(lane >= LANES - cells, (rate + plus[1]) * high_b, 0.0)
        low_b = lane_roll(low, cells * (groups - 1 - b))
        high_b = lane_roll(high, -cells * b)
        for state in states:
            state[:, 0, rows, :] = low_b
            state[:, tiles + 1, rows, :] = high_b

    low, high = face(0, by_cells, by_one), face(1, by_cells, by_one)
    low_part = (rate + minus[0]) * low
    high_part = (rate + plus[0]) * high
    for t in range(tiles):
        sa_ref[:, t + 1, PAD : PAD + 1, :] += low_part[:, t : t + 1, :]
        sa_ref[:, t + 1, PAD + cells - 1 : PAD + cells, :] += high_part[:, t : t + 1, :]
        for state in states:
            state[:, t + 1, PAD - 1 : PAD, :] = low[:, t : t + 1, :]
            state[:, t + 1, PAD + cells : PAD + cells + 1, :] = high[:, t : t + 1, :]

    own = rk_ref[0]

    def step(src, dst):
        def put(f, t, it, value):
            dst[f, t + 1, pl.ds(PAD + ROWS * it, ROWS), :] = value

        substep(src, put, e_ref, own, minus, plus, rates, fields, cells, tiles)

    def finish(src):
        for t in range(tiles):
            for half in range(cells // 16):
                o_ref[0, :, pl.ds(16 * half, 16), pl.ds(LANES * t, LANES)] = src[
                    :, t + 1, pl.ds(PAD + 16 * half, 16), :
                ].astype(bf16)

    @pl.when(n == 1)
    def _():
        finish(sa_ref)

    @pl.when(n > 1)
    def _():
        def two(i, carry):
            step(sa_ref, sb_ref)
            step(sb_ref, sa_ref)
            return carry

        lax.fori_loop(0, (n - 2) // 2, two, 0)
        step(sa_ref, sb_ref)
        finish(sb_ref)


def advance(ints, vals, started, own, arrived, plane, first, per_dev, slots, out_at, into=None):
    count, fields, tiles, cells, _ = started.shape
    padded = (fields, tiles + 2, cells + 2 * PAD, LANES)
    shape = (1, fields, cells, plane)
    whole = [] if into is None else [into]
    return pl.pallas_call(
        functools.partial(advance_kernel, first, per_dev),
        grid_spec=pltpu.PrefetchScalarGridSpec(
            num_scalar_prefetch=2,
            grid=(count,),
            in_specs=[
                pl.BlockSpec((1,) + started.shape[1:], lambda b, i, v: (b, 0, 0, 0, 0)),
                pl.BlockSpec((1,) + own.shape[1:], lambda b, i, v: (b, 0, 0)),
                pl.BlockSpec(arrived.shape, lambda b, i, v: (0, 0, 0)),
            ]
            + [pl.BlockSpec(memory_space=pl.ANY) for _ in whole],
            out_specs=pl.BlockSpec(shape, lambda b, i, v: (i[b + out_at], 0, 0, 0)),
            scratch_shapes=[
                pltpu.VMEM(padded, f32),
                pltpu.VMEM(padded, f32),
                pltpu.VMEM((fields, tiles, cells, LANES), f32),
            ],
        ),
        out_shape=jax.ShapeDtypeStruct((slots, fields, cells, plane), bf16),
        input_output_aliases={} if into is None else {5: 0},
        compiler_params=pltpu.CompilerParams(vmem_limit_bytes=16 << 20),
        name="advance",
    )(ints, vals, started, own, arrived, *whole)


def plan(wanted, my_index, per_dev):
    peers, requests = wanted.shape
    at = lax.broadcasted_iota(jnp.int32, wanted.shape, 1)
    source_dev = wanted // per_dev
    code = wanted % per_dev * 6 + jnp.bitwise_xor(at % 6, 1)
    key = at * 64 + code
    match = source_dev == my_index
    first = jnp.min(jnp.where(match, key, 64 * requests), axis=1) % 64
    second = jnp.maximum(jnp.max(jnp.where(match, key, 0), axis=1), 0) % 64
    send = jnp.stack([first, second], axis=1).reshape(2 * peers)
    mine = lax.dynamic_slice_in_dim(wanted, my_index, 1, 0)[0]
    my_source = mine // per_dev
    order = jnp.arange(requests, dtype=jnp.int32)
    repeated = (my_source[:, None] == my_source[None, :]) & (order[None, :] < order[:, None])
    lookup = my_source * 2 + jnp.any(repeated, axis=1).astype(jnp.int32)
    return send, mine, lookup


def local(
    block_state,
    block_level,
    block_velocity,
    diffusivity,
    reaction_matrix,
    ghost_source,
    swap_bit,
    swap_slot,
):
    blocks = block_state[0]
    per_dev, fields, cells, plane = blocks.shape
    peers = lax.axis_size(("gy", "gz"))
    my_index = lax.axis_index(("gy", "gz"))
    levels = block_level[0]
    wanted = ghost_source[0].reshape(peers, per_dev * 6)
    send, mine, lookup = plan(wanted, my_index, per_dev)
    outgoing = pack_faces(blocks, send, 2 * peers)
    arrived = lax.all_to_all(outgoing, ("gy", "gz"), split_axis=0, concat_axis=0, tiled=True)

    own_levels = lax.dynamic_slice_in_dim(levels, my_index * per_dev, per_dev, 0)
    known = mine[:, None] == jnp.arange(levels.shape[0], dtype=jnp.int32)[None, :]
    source_levels = jnp.sum(jnp.where(known, levels[None, :], 0), axis=1)
    coarse = (source_levels.reshape(per_dev, 6) != own_levels[:, None]).astype(jnp.int32)
    bit_here = swap_bit[0, 0, 0]
    slot_here = swap_slot[0, 0, 0]
    rest = jnp.arange(per_dev, dtype=jnp.int32)
    rest = jnp.where(rest == 0, slot_here, rest - (rest <= slot_here))
    ints = jnp.concatenate([rest, own_levels, lookup, coarse.reshape(-1)])
    speeds = block_velocity[0]
    vals = jnp.concatenate([speeds.astype(f32).reshape(-1), diffusivity, reaction_matrix.reshape(-1)])
    pick = lambda x, size: lax.dynamic_slice_in_dim(x.reshape(-1), slot_here * size, size, 0)

    facts = jnp.concatenate(
        [pick(own_levels, 1).astype(bf16), pick(coarse, 6).astype(bf16), pick(speeds, 3)]
    )
    bits = range(lax.axis_size("gx").bit_length() - 1)

    def trade(x):
        coming = x
        for bit_no in bits:
            coming = jnp.where(bit_here == bit_no, swapped(x, "gx", bit_no), coming)
        return coming

    departing = lax.dynamic_slice_in_dim(blocks, slot_here, 1, 0).reshape(fields * cells, plane)
    label = jnp.broadcast_to(jnp.pad(facts, (0, plane - facts.shape[0]))[None], (16, plane))
    coming = trade(jnp.concatenate([departing, label], axis=0))
    facts = coming[fields * cells]
    traded_ints = jnp.concatenate(
        [
            jnp.zeros((1,), jnp.int32),
            facts[0:1].astype(jnp.int32),
            jnp.arange(6, dtype=jnp.int32),
            facts[1:7].astype(jnp.int32),
            slot_here[None],
        ]
    )
    traded_vals = jnp.concatenate(
        [facts[7:10].astype(f32), diffusivity, reaction_matrix.reshape(-1)]
    )

    stay = first_substep(ints, vals, blocks, 1, per_dev - 1)
    coming, stay = lax.optimization_barrier((coming, stay))
    traded = first_substep(
        traded_ints, traded_vals, coming[: fields * cells].reshape(1, fields, cells, plane), 0, 1
    )
    arrived, traded, stay = lax.optimization_barrier((arrived, traded, stay))
    layers = trade(jnp.take(arrived, pick(lookup, 6), axis=0))
    result = advance(ints, vals, *stay, arrived, plane, 1, per_dev, per_dev, 1)
    result = advance(
        traded_ints, traded_vals, *traded, layers, plane, 0, 1, per_dev, 14, into=result
    )
    return result[None]


def solution(mesh):
    in_specs = (
        P("gx", ("gy", "gz"), None, None, None),
        P("gx", None),
        P("gx", ("gy", "gz"), None),
        P(),
        P(),
        P("gx", None, None),
        P("gx", "gy", "gz"),
        P("gx", "gy", "gz"),
    )
    out_specs = P("gx", ("gy", "gz"), None, None, None)
    return jax.shard_map(local, mesh=mesh, in_specs=in_specs, out_specs=out_specs, check_vma=False)
```

```python
import functools

import jax
import jax.numpy as jnp
from jax import lax
from jax.experimental import pallas as pl
from jax.experimental.pallas import tpu as pltpu
from jax.sharding import PartitionSpec as P

f32 = jnp.float32
bf16 = jnp.bfloat16
dt_base = 0.05
LANES = 128
ROWS = 8
PAD = 8
LABEL = (16, LANES)


def swapped(x, axis, bit):
    return lax.ppermute(x, axis, [(i, i ^ 1 << bit) for i in range(lax.axis_size(axis))])


def lane_roll(x, shift):
    shift = shift % LANES
    return x if shift == 0 else pltpu.roll(x, shift, x.ndim - 1)


def lane_ids():
    return lax.broadcasted_iota(jnp.int32, (1, ROWS, LANES), 2)


def row_ids():
    return lax.broadcasted_iota(jnp.int32, (1, ROWS, LANES), 1)


def pack_kernel(send_ref, u_ref, o_ref, sel_ref, face_ref):
    blk = pl.program_id(0)
    _, fields, cells, plane = u_ref.shape
    groups = LANES // cells
    tiles = plane // LANES

    @pl.when(blk == 0)
    def _():
        row = lax.broadcasted_iota(jnp.int32, sel_ref.shape, 0)
        col = lax.broadcasted_iota(jnp.int32, sel_ref.shape, 1)
        high = col // LANES
        within = col % LANES
        r = within % cells
        b = within // cells
        source = (tiles * b + r) * cells + high * (cells - 1)
        sel_ref[...] = jnp.where((r < tiles) & (row == source), 1.0, 0.0).astype(bf16)

    lane = lane_ids()
    group = lane // cells
    at_row = row_ids()

    def put(face_no, value):
        face_ref[blk * 6 + face_no] = value.reshape(fields * ROWS, LANES).astype(bf16)

    for face_no, edge in ((0, 0), (1, cells - 1)):
        pieces = [
            u_ref[0, :, edge : edge + 1, pl.ds(LANES * t, LANES)].astype(f32)
            for t in range(tiles)
        ]
        natural = jnp.concatenate(pieces, axis=1)
        total = jnp.zeros((fields, ROWS, LANES), f32)
        for d in range(groups):
            moved = lane_roll(natural, cells * d)
            for b in range(groups):
                for half in range(tiles // groups):
                    r = groups * half + (b - d) % groups
                    t = (tiles // groups) * b + half
                    shift = (r - t) % ROWS
                    here = pltpu.roll(moved, shift, 1) if shift else moved
                    total = jnp.where((group == b) & (at_row == r), here, total)
        put(face_no, total)
    for face_no, tile, source in ((2, 0, 0), (3, tiles - 1, groups - 1)):
        strip = u_ref[0, :, :, pl.ds(LANES * tile, LANES)].astype(f32)
        total = jnp.zeros((fields, ROWS, LANES), f32)
        for b in range(groups):
            moved = lane_roll(strip[:, ROWS * b : ROWS * b + ROWS], cells * (b - source))
            total = jnp.where(group == b, moved, total)
        put(face_no, total)
    picked = jnp.dot(
        u_ref[0].reshape(fields * cells, plane), sel_ref[...], preferred_element_type=f32
    ).reshape(fields, cells, 2 * LANES)
    for face_no, high in ((4, 0), (5, 1)):
        total = jnp.zeros((fields, ROWS, LANES), f32)
        for b in range(groups):
            part = picked[:, ROWS * b : ROWS * b + ROWS, LANES * high : LANES * high + LANES]
            total = total + lane_roll(part, tiles * b)
        put(face_no, total)

    @pl.when(blk == pl.num_programs(0) - 1)
    def _():
        def copy(slot, carry):
            o_ref[slot] = face_ref[send_ref[slot]]
            return carry

        lax.fori_loop(0, o_ref.shape[0], copy, 0)


def in_hbm(x):
    return pltpu.with_memory_space_constraint(x, pltpu.HBM)


def pack_faces(blocks, send, slots):
    per_dev, fields, cells, plane = blocks.shape
    return pl.pallas_call(
        pack_kernel,
        grid_spec=pltpu.PrefetchScalarGridSpec(
            num_scalar_prefetch=1,
            grid=(per_dev,),
            in_specs=[pl.BlockSpec((1, fields, cells, plane), lambda b, s: (b, 0, 0, 0))],
            out_specs=pl.BlockSpec((slots, fields * ROWS, LANES), lambda b, s: (0, 0, 0)),
            scratch_shapes=[
                pltpu.VMEM((plane, 2 * LANES), bf16),
                pltpu.VMEM((per_dev * 6, fields * ROWS, LANES), bf16),
            ],
        ),
        out_shape=jax.ShapeDtypeStruct((slots, fields * ROWS, LANES), bf16),
        compiler_params=pltpu.CompilerParams(vmem_limit_bytes=16 << 20),
        name="pack_faces",
    )(send, in_hbm(blocks))


class Facts:
    def __init__(self, ints_ref, vals_ref, blk, per_dev, fields):
        self.lookup = lambda face: ints_ref[2 * per_dev + blk * 6 + face]
        self.coarse = lambda face: ints_ref[8 * per_dev + blk * 6 + face]
        self.reaction = lambda f, e: vals_ref[3 * per_dev + fields + f * fields + e]
        self.n = jnp.left_shift(jnp.int32(1), ints_ref[per_dev + blk])
        scale = self.n.astype(f32)
        self.dt = dt_base / scale
        adv = self.dt * scale
        dif = self.dt * scale * scale
        velocity = [vals_ref[blk * 3 + d] for d in range(3)]
        self.minus = [adv * jnp.maximum(v, 0.0) for v in velocity]
        self.plus = [-(adv * jnp.minimum(v, 0.0)) for v in velocity]
        self.rates = [dif * vals_ref[3 * per_dev + f] for f in range(fields)]


def own_matrix(facts, fields, write):
    outflow = sum(facts.minus) + sum(facts.plus)
    size = fields * ROWS
    ri = lax.broadcasted_iota(jnp.int32, (size, size), 0)
    ci = lax.broadcasted_iota(jnp.int32, (size, size), 1)
    matrix = jnp.zeros((size, size), f32)
    for f in range(fields):
        line = jnp.zeros((size, size), f32)
        for e in range(fields):
            term = facts.dt * facts.reaction(f, e)
            if e == f:
                term = term - (6.0 * facts.rates[f] + outflow)
            line = jnp.where(ci // ROWS == e, term, line)
        matrix = jnp.where(ri // ROWS == f, line, matrix)
    matrix = jnp.where(ri % ROWS == ci % ROWS, matrix, 0.0)
    high = matrix.astype(bf16)
    write(0, high)
    write(size, (matrix - high.astype(f32)).astype(bf16))
    write(2 * size, high)


def to_planes(load, state, cells, tiles):
    groups = LANES // cells
    group = lane_ids() // cells
    for it in range(cells // ROWS):
        for half in range(tiles // groups):
            source = [load((tiles // groups) * b + half, it) for b in range(groups)]
            shifted = []
            for d in range(groups):
                x = source[d % groups]
                for g in range(1, groups):
                    x = jnp.where(group == g, source[(g + d) % groups], x)
                shifted.append(lane_roll(x, cells * d))
            for jj in range(groups):
                out = shifted[(0 - jj) % groups]
                for b in range(1, groups):
                    out = jnp.where(group == b, shifted[(b - jj) % groups], out)
                state[:, groups * half + jj + 1, pl.ds(PAD + ROWS * it, ROWS), :] = out


def from_planes(state, store, cells, tiles):
    groups = LANES // cells
    group = lane_ids() // cells
    for it in range(cells // 16):
        for half in range(tiles // groups):
            outs = [[] for _ in range(groups)]
            for sub in range(2):
                rows = pl.ds(PAD + 16 * it + ROWS * sub, ROWS)
                source = [state[:, groups * half + jj + 1, rows, :] for jj in range(groups)]
                shifted = []
                for d in range(groups):
                    x = source[(0 - d) % groups]
                    for g in range(1, groups):
                        x = jnp.where(group == g, source[(g - d) % groups], x)
                    shifted.append(lane_roll(x, -cells * d))
                for b in range(groups):
                    out = shifted[b % groups]
                    for jj in range(1, groups):
                        out = jnp.where(group == jj, shifted[(b - jj) % groups], out)
                    outs[b].append(out)
            for b in range(groups):
                both = jnp.concatenate(outs[b], axis=1).astype(bf16)
                store((tiles // groups) * b + half, it, both)


def wrap_planes(state, side_ref, cells, tiles):
    lane = lane_ids()
    for it in range(cells // ROWS):
        rows = pl.ds(PAD + ROWS * it, ROWS)
        side = 0.0 if side_ref is None else side_ref[:, pl.ds(ROWS * it, ROWS), :]
        state[:, 0, rows, :] = jnp.where(lane < cells, side, lane_roll(state[:, tiles, rows, :], cells))
        state[:, tiles + 1, rows, :] = jnp.where(
            lane >= LANES - cells, side, lane_roll(state[:, 1, rows, :], -cells)
        )


def substep(src, put, edge_ref, own, facts, fields, cells, tiles):
    lane = lax.broadcasted_iota(jnp.int32, (ROWS, LANES), 1)
    k_first = lane % cells == 0
    k_last = lane % cells == cells - 1
    minus, plus, rates = facts.minus, facts.plus, facts.rates

    def two_tiles(pair, carry):
        for it in range(cells // ROWS):
            row = PAD + ROWS * it
            centre = [
                [src[f, 2 * pair + 1 + q, pl.ds(row, ROWS), :] for f in range(fields)]
                for q in range(2)
            ]
            both = jnp.concatenate([jnp.concatenate(c, axis=0) for c in centre], axis=1)
            both_high = both.astype(bf16)
            both_low = (both - both_high.astype(f32)).astype(bf16)
            stacked = jnp.concatenate([both_high, both_high, both_low], axis=0)
            mixed = jnp.dot(own, stacked, preferred_element_type=f32)
            for q in range(2):
                t = 2 * pair + q
                for f in range(fields):
                    c = centre[q][f]
                    minus_x = src[f, t + 1, pl.ds(row - 1, ROWS), :]
                    plus_x = src[f, t + 1, pl.ds(row + 1, ROWS), :]
                    minus_y = src[f, t, pl.ds(row, ROWS), :]
                    plus_y = src[f, t + 2, pl.ds(row, ROWS), :]
                    edge = 0.0 if edge_ref is None else edge_ref[f, t, pl.ds(ROWS * it, ROWS), :]
                    minus_z = jnp.where(k_first, edge, lane_roll(c, 1))
                    plus_z = jnp.where(k_last, edge, lane_roll(c, -1))
                    near = (rates[f] + minus[0]) * minus_x + (rates[f] + plus[0]) * plus_x
                    near += (rates[f] + minus[1]) * minus_y + (rates[f] + plus[1]) * plus_y
                    near += (rates[f] + minus[2]) * minus_z + (rates[f] + plus[2]) * plus_z
                    own_terms = mixed[ROWS * f : ROWS * f + ROWS, LANES * q : LANES * q + LANES]
                    put(f, t, it, near + (c + own_terms))
        return carry

    lax.fori_loop(0, tiles // 2, two_tiles, 0)


def first_kernel(first, per_dev, ints_ref, vals_ref, u_ref, o_ref, rk_out_ref, sa_ref):
    _, fields, cells, plane = u_ref.shape
    tiles = plane // LANES
    facts = Facts(ints_ref, vals_ref, ints_ref[pl.program_id(0) + first], per_dev, fields)

    @pl.when(pl.program_id(0) == 0)
    def _():
        sa_ref[:, :, 0:PAD] = jnp.zeros((fields, tiles + 2, PAD, LANES), f32)
        sa_ref[:, :, PAD + cells :] = jnp.zeros((fields, tiles + 2, PAD, LANES), f32)

    load_block(u_ref, sa_ref, cells, tiles)
    wrap_planes(sa_ref, None, cells, tiles)

    def write(at, value):
        rk_out_ref[0, :, at : at + value.shape[1]] = value

    own_matrix(facts, fields, write)

    def put(f, t, it, value):
        o_ref[0, f, t, pl.ds(ROWS * it, ROWS), :] = value

    substep(sa_ref, put, None, rk_out_ref[0], facts, fields, cells, tiles)


def load_block(u_ref, state, cells, tiles):
    whole = {}

    def load(t, it):
        if (t, it // 2) not in whole:
            whole[t, it // 2] = u_ref[
                0, :, pl.ds(16 * (it // 2), 16), pl.ds(LANES * t, LANES)
            ].astype(f32)
        return whole[t, it // 2][:, ROWS * (it % 2) : ROWS * (it % 2) + ROWS]

    to_planes(load, state, cells, tiles)


def first_substep(ints, vals, blocks, first, count):
    per_dev, fields, cells, plane = blocks.shape
    tiles = plane // LANES
    size = fields * ROWS
    return pl.pallas_call(
        functools.partial(first_kernel, first, per_dev),
        grid_spec=pltpu.PrefetchScalarGridSpec(
            num_scalar_prefetch=2,
            grid=(count,),
            in_specs=[
                pl.BlockSpec((1, fields, cells, plane), lambda b, i, v: (i[b + first], 0, 0, 0))
            ],
            out_specs=[
                pl.BlockSpec((1, fields, tiles, cells, LANES), lambda b, i, v: (b, 0, 0, 0, 0)),
                pl.BlockSpec((1, size, 3 * size), lambda b, i, v: (b, 0, 0)),
            ],
            scratch_shapes=[pltpu.VMEM((fields, tiles + 2, cells + 2 * PAD, LANES), f32)],
        ),
        out_shape=[
            pltpu.HBM((count, fields, tiles, cells, LANES), f32),
            jax.ShapeDtypeStruct((count, size, 3 * size), bf16),
        ],
        compiler_params=pltpu.CompilerParams(vmem_limit_bytes=16 << 20),
        name="first_substep",
    )(ints, vals, in_hbm(blocks))


def place_layers(layer_of, facts, sa_ref, sb_ref, e_ref, side_ref, s_ref, fields, cells, tiles):
    groups = LANES // cells
    lane = lane_ids()
    at_row = row_ids()
    k_first = lane % cells == 0
    k_last = lane % cells == cells - 1
    minus, plus = facts.minus, facts.plus
    odd_lane = lane % 2 == 1
    odd_row = at_row % 2 == 1

    def face(face_no):
        layer = layer_of(face_no).astype(f32).reshape(fields, ROWS, LANES)
        mean = layer + jnp.where(odd_lane, lane_roll(layer, 1), lane_roll(layer, -1))
        mean = mean + jnp.where(odd_row, pltpu.roll(mean, 1, 1), pltpu.roll(mean, ROWS - 1, 1))
        return jnp.where(facts.coarse(face_no) > 0, mean * 0.25, layer)

    states = (sa_ref, sb_ref)
    rate = jnp.concatenate([jnp.full((1, ROWS, LANES), x, f32) for x in facts.rates], axis=0)

    low, high = face(4), lane_roll(face(5), cells - 1)
    weight = jnp.where(k_first, rate + minus[2], jnp.where(k_last, rate + plus[2], 0.0))
    for it in range(cells // ROWS):
        rows = pl.ds(ROWS * it, ROWS)
        for t in range(tiles):
            at = tiles * it + t
            edge = lane_roll(jnp.where(lane % cells == at, low, high), -at)
            e_ref[:, t, rows, :] = edge
            if s_ref is not None:
                sa_ref[:, t + 1, pl.ds(PAD + ROWS * it, ROWS), :] = (
                    s_ref[0, :, t, rows, :] + weight * edge
                )

    low, high = face(2), face(3)
    for it in range(cells // ROWS):
        rows = pl.ds(PAD + ROWS * it, ROWS)
        side = jnp.where(
            lane < cells,
            lane_roll(low, -cells * it),
            lane_roll(high, cells * (groups - 1 - it)),
        )
        side_ref[:, pl.ds(ROWS * it, ROWS), :] = side
        if s_ref is not None:
            sa_ref[:, 1, rows, :] += jnp.where(lane < cells, (rate + minus[1]) * side, 0.0)
            sa_ref[:, tiles, rows, :] += jnp.where(
                lane >= LANES - cells, (rate + plus[1]) * side, 0.0
            )

    low, high = face(0), face(1)
    low_part = (rate + minus[0]) * low
    high_part = (rate + plus[0]) * high
    for t in range(tiles):
        if s_ref is not None:
            sa_ref[:, t + 1, PAD : PAD + 1, :] += low_part[:, t : t + 1, :]
            sa_ref[:, t + 1, PAD + cells - 1 : PAD + cells, :] += high_part[:, t : t + 1, :]
        for state in states:
            state[:, t + 1, PAD - 1 : PAD, :] = low[:, t : t + 1, :]
            state[:, t + 1, PAD + cells : PAD + cells + 1, :] = high[:, t : t + 1, :]
    wrap_planes(sa_ref, side_ref, cells, tiles)


def make_step(own, facts, e_ref, side_ref, fields, cells, tiles):
    def step(src, dst):
        def put(f, t, it, value):
            dst[f, t + 1, pl.ds(PAD + ROWS * it, ROWS), :] = value

        substep(src, put, e_ref, own, facts, fields, cells, tiles)
        wrap_planes(dst, side_ref, cells, tiles)

    return step


def make_finish(o_ref, cells, tiles):
    def finish(src):
        def store(t, it, value):
            o_ref[0, :, pl.ds(16 * it, 16), pl.ds(LANES * t, LANES)] = value

        from_planes(src, store, cells, tiles)

    return finish


def stay_kernel(first, per_dev, ints_ref, vals_ref, s_ref, rk_ref, arr_ref, o_ref, sa_ref, sb_ref, e_ref, side_ref):
    _, fields, tiles, cells, _ = s_ref.shape
    facts = Facts(ints_ref, vals_ref, ints_ref[pl.program_id(0) + first], per_dev, fields)
    place_layers(
        lambda face_no: arr_ref[facts.lookup(face_no)],
        facts, sa_ref, sb_ref, e_ref, side_ref, s_ref, fields, cells, tiles,
    )
    step = make_step(rk_ref[0], facts, e_ref, side_ref, fields, cells, tiles)
    finish = make_finish(o_ref, cells, tiles)

    @pl.when(facts.n == 1)
    def _():
        finish(sa_ref)

    @pl.when(facts.n > 1)
    def _():
        def two(i, carry):
            step(sa_ref, sb_ref)
            step(sb_ref, sa_ref)
            return carry

        lax.fori_loop(0, (facts.n - 2) // 2, two, 0)
        step(sa_ref, sb_ref)
        finish(sb_ref)


def state_scratch(fields, cells, tiles):
    padded = (fields, tiles + 2, cells + 2 * PAD, LANES)
    return [
        pltpu.VMEM(padded, f32),
        pltpu.VMEM(padded, f32),
        pltpu.VMEM((fields, tiles, cells, LANES), f32),
        pltpu.VMEM((fields, cells, LANES), f32),
    ]


def advance_stay(ints, vals, started, own, arrived, plane, first, per_dev):
    count, fields, tiles, cells, _ = started.shape
    shape = (1, fields, cells, plane)
    return pl.pallas_call(
        functools.partial(stay_kernel, first, per_dev),
        grid_spec=pltpu.PrefetchScalarGridSpec(
            num_scalar_prefetch=2,
            grid=(count,),
            in_specs=[
                pl.BlockSpec((1,) + started.shape[1:], lambda b, i, v: (b, 0, 0, 0, 0)),
                pl.BlockSpec((1,) + own.shape[1:], lambda b, i, v: (b, 0, 0)),
                pl.BlockSpec(arrived.shape, lambda b, i, v: (0, 0, 0)),
            ],
            out_specs=pl.BlockSpec(shape, lambda b, i, v: (i[b + first], 0, 0, 0)),
            scratch_shapes=state_scratch(fields, cells, tiles),
        ),
        out_shape=jax.ShapeDtypeStruct((per_dev, fields, cells, plane), bf16),
        compiler_params=pltpu.CompilerParams(vmem_limit_bytes=20 << 20),
        name="advance_stay",
    )(ints, vals, in_hbm(started), own, arrived)


def traded_kernel(choices, ints_ref, vals_ref, *refs):
    raw_refs, layer_refs, refs = refs[:choices], refs[choices : 2 * choices], refs[2 * choices + 1 :]
    o_ref, sa_ref, sb_ref, e_ref, side_ref, rk_ref, raw_ref, layer_ref, sems = refs
    _, fields, cells, plane = raw_ref.shape
    tiles = plane // LANES
    facts = Facts(ints_ref, vals_ref, 0, 1, fields)
    choice = ints_ref[15]
    for c in range(choices):

        @pl.when(choice == c)
        def _():
            raw_copy = pltpu.make_async_copy(raw_refs[c], raw_ref, sems.at[0])
            layer_copy = pltpu.make_async_copy(layer_refs[c], layer_ref, sems.at[1])
            raw_copy.start()
            layer_copy.start()
            raw_copy.wait()
            layer_copy.wait()

    def write(at, value):
        rk_ref[:, at : at + value.shape[1]] = value

    own_matrix(facts, fields, write)
    load_block(raw_ref, sa_ref, cells, tiles)
    place_layers(
        lambda face_no: layer_ref[face_no],
        facts, sa_ref, sb_ref, e_ref, side_ref, None, fields, cells, tiles,
    )
    step = make_step(rk_ref[...], facts, e_ref, side_ref, fields, cells, tiles)
    finish = make_finish(o_ref, cells, tiles)

    @pl.when(facts.n == 1)
    def _():
        step(sa_ref, sb_ref)
        finish(sb_ref)

    @pl.when(facts.n > 1)
    def _():
        def two(i, carry):
            step(sa_ref, sb_ref)
            step(sb_ref, sa_ref)
            return carry

        lax.fori_loop(0, facts.n // 2, two, 0)
        finish(sa_ref)


def advance_traded(ints, vals, raws, layers, into):
    per_dev, fields, cells, plane = into.shape
    tiles = plane // LANES
    choices = len(raws)
    size = fields * ROWS
    anywhere = pl.BlockSpec(memory_space=pl.ANY)
    return pl.pallas_call(
        functools.partial(traded_kernel, choices),
        grid_spec=pltpu.PrefetchScalarGridSpec(
            num_scalar_prefetch=2,
            grid=(1,),
            in_specs=[anywhere] * (2 * choices + 1),
            out_specs=pl.BlockSpec((1, fields, cells, plane), lambda b, i, v: (i[14], 0, 0, 0)),
            scratch_shapes=state_scratch(fields, cells, tiles)
            + [
                pltpu.VMEM((size, 3 * size), bf16),
                pltpu.VMEM((1, fields, cells, plane), bf16),
                pltpu.VMEM((6, size, LANES), bf16),
                pltpu.SemaphoreType.DMA((2,)),
            ],
        ),
        out_shape=jax.ShapeDtypeStruct(into.shape, bf16),
        input_output_aliases={2 + 2 * choices: 0},
        compiler_params=pltpu.CompilerParams(vmem_limit_bytes=20 << 20),
        name="advance_traded",
    )(ints, vals, *raws, *layers, into)


def plan(wanted, my_index, per_dev):
    peers, requests = wanted.shape
    at = lax.broadcasted_iota(jnp.int32, wanted.shape, 1)
    source_dev = wanted // per_dev
    code = wanted % per_dev * 6 + jnp.bitwise_xor(at % 6, 1)
    key = at * 64 + code
    match = source_dev == my_index
    first = jnp.min(jnp.where(match, key, 64 * requests), axis=1) % 64
    second = jnp.max(jnp.where(match, key, 0), axis=1) % 64
    send = jnp.stack([first, second], axis=1).reshape(2 * peers)
    mine = lax.dynamic_slice_in_dim(wanted, my_index, 1, 0)[0]
    my_source = mine // per_dev
    order = jnp.arange(requests, dtype=jnp.int32)
    repeated = (my_source[:, None] == my_source[None, :]) & (order[None, :] < order[:, None])
    lookup = my_source * 2 + jnp.any(repeated, axis=1).astype(jnp.int32)
    return send, mine, lookup


def local(
    block_state,
    block_level,
    block_velocity,
    diffusivity,
    reaction_matrix,
    ghost_source,
    swap_bit,
    swap_slot,
):
    blocks = block_state[0]
    per_dev, fields, cells, plane = blocks.shape
    peers = lax.axis_size(("gy", "gz"))
    my_index = lax.axis_index(("gy", "gz"))
    levels = block_level[0]
    wanted = ghost_source[0].reshape(peers, per_dev * 6)
    send, mine, lookup = plan(wanted, my_index, per_dev)
    outgoing = pack_faces(blocks, send, 2 * peers)
    arrived = lax.all_to_all(outgoing, ("gy", "gz"), split_axis=0, concat_axis=0, tiled=True)

    own_levels = lax.dynamic_slice_in_dim(levels, my_index * per_dev, per_dev, 0)
    known = mine[:, None] == jnp.arange(levels.shape[0], dtype=jnp.int32)[None, :]
    source_levels = jnp.sum(jnp.where(known, levels[None, :], 0), axis=1)
    coarse = (source_levels.reshape(per_dev, 6) != own_levels[:, None]).astype(jnp.int32)
    bit_here = swap_bit[0, 0, 0]
    slot_here = swap_slot[0, 0, 0]
    rest = jnp.arange(per_dev, dtype=jnp.int32)
    rest = jnp.where(rest == 0, slot_here, rest - (rest <= slot_here))
    ints = jnp.concatenate([rest, own_levels, lookup, coarse.reshape(-1)])
    speeds = block_velocity[0]
    vals = jnp.concatenate([speeds.astype(f32).reshape(-1), diffusivity, reaction_matrix.reshape(-1)])
    pick = lambda x, size: lax.dynamic_slice_in_dim(x.reshape(-1), slot_here * size, size, 0)
    bits = range(lax.axis_size("gx").bit_length() - 1)
    offers = lambda x: [x] + [swapped(x, "gx", bit_no) for bit_no in bits]

    raws = offers(lax.dynamic_slice_in_dim(blocks, slot_here, 1, 0))
    label = jnp.concatenate(
        [pick(own_levels, 1).astype(bf16), pick(coarse, 6).astype(bf16), pick(speeds, 3)]
    )
    label = jnp.broadcast_to(jnp.pad(label, (0, LABEL[1] - label.shape[0]))[None], LABEL)
    label, *others = offers(label)
    for bit_no in bits:
        label = jnp.where(bit_here == bit_no, others[bit_no], label)
    label = label[0]
    traded_ints = jnp.concatenate(
        [
            jnp.zeros((1,), jnp.int32),
            label[0:1].astype(jnp.int32),
            jnp.arange(6, dtype=jnp.int32),
            label[1:7].astype(jnp.int32),
            slot_here[None],
            bit_here[None] + 1,
        ]
    )
    traded_vals = jnp.concatenate([label[7:10].astype(f32), diffusivity, reaction_matrix.reshape(-1)])

    stay = first_substep(ints, vals, blocks, 1, per_dev - 1)
    arrived, stay, traded_ints, traded_vals = lax.optimization_barrier(
        (arrived, stay, traded_ints, traded_vals)
    )
    layers = offers(jnp.take(arrived, pick(lookup, 6), axis=0))
    result = advance_stay(ints, vals, *stay, arrived, plane, 1, per_dev)
    raws, layers, result = lax.optimization_barrier((raws, layers, result))
    result = advance_traded(traded_ints, traded_vals, raws, layers, result)
    return result[None]


def solution(mesh):
    in_specs = (
        P("gx", ("gy", "gz"), None, None, None),
        P("gx", None),
        P("gx", ("gy", "gz"), None),
        P(),
        P(),
        P("gx", None, None),
        P("gx", "gy", "gz"),
        P("gx", "gy", "gz"),
    )
    out_specs = P("gx", ("gy", "gz"), None, None, None)
    return jax.shard_map(local, mesh=mesh, in_specs=in_specs, out_specs=out_specs, check_vma=False)
```

```python
import functools

import jax
import jax.numpy as jnp
from jax import lax
from jax.experimental import pallas as pl
from jax.experimental.pallas import tpu as pltpu
from jax.sharding import PartitionSpec as P

f32 = jnp.float32
bf16 = jnp.bfloat16
dt_base = 0.05
LANES = 128
ROWS = 8
PAD = 8
LABEL = (16, LANES)


def swapped(x, axis, bit):
    return lax.ppermute(x, axis, [(i, i ^ 1 << bit) for i in range(lax.axis_size(axis))])


def lane_roll(x, shift):
    shift = shift % LANES
    return x if shift == 0 else pltpu.roll(x, shift, x.ndim - 1)


def lane_ids():
    return lax.broadcasted_iota(jnp.int32, (1, ROWS, LANES), 2)


def row_ids():
    return lax.broadcasted_iota(jnp.int32, (1, ROWS, LANES), 1)


def pack_kernel(send_ref, u_ref, o_ref, sel_ref, face_ref):
    blk = pl.program_id(0)
    _, fields, cells, plane = u_ref.shape
    groups = LANES // cells
    tiles = plane // LANES

    @pl.when(blk == 0)
    def _():
        row = lax.broadcasted_iota(jnp.int32, sel_ref.shape, 0)
        col = lax.broadcasted_iota(jnp.int32, sel_ref.shape, 1)
        high = col // LANES
        within = col % LANES
        r = within % cells
        b = within // cells
        source = (tiles * b + r) * cells + high * (cells - 1)
        sel_ref[...] = jnp.where((r < tiles) & (row == source), 1.0, 0.0).astype(bf16)

    lane = lane_ids()
    group = lane // cells
    at_row = row_ids()

    def put(face_no, value):
        face_ref[blk * 6 + face_no] = value.reshape(fields * ROWS, LANES).astype(bf16)

    for face_no, edge in ((0, 0), (1, cells - 1)):
        pieces = [
            u_ref[0, :, edge : edge + 1, pl.ds(LANES * t, LANES)].astype(f32)
            for t in range(tiles)
        ]
        natural = jnp.concatenate(pieces, axis=1)
        total = jnp.zeros((fields, ROWS, LANES), f32)
        for d in range(groups):
            moved = lane_roll(natural, cells * d)
            for b in range(groups):
                for half in range(tiles // groups):
                    r = groups * half + (b - d) % groups
                    t = (tiles // groups) * b + half
                    shift = (r - t) % ROWS
                    here = pltpu.roll(moved, shift, 1) if shift else moved
                    total = jnp.where((group == b) & (at_row == r), here, total)
        put(face_no, total)
    for face_no, tile, source in ((2, 0, 0), (3, tiles - 1, groups - 1)):
        strip = u_ref[0, :, :, pl.ds(LANES * tile, LANES)].astype(f32)
        total = jnp.zeros((fields, ROWS, LANES), f32)
        for b in range(groups):
            moved = lane_roll(strip[:, ROWS * b : ROWS * b + ROWS], cells * (b - source))
            total = jnp.where(group == b, moved, total)
        put(face_no, total)
    picked = jnp.dot(
        u_ref[0].reshape(fields * cells, plane), sel_ref[...], preferred_element_type=f32
    ).reshape(fields, cells, 2 * LANES)
    for face_no, high in ((4, 0), (5, 1)):
        total = jnp.zeros((fields, ROWS, LANES), f32)
        for b in range(groups):
            part = picked[:, ROWS * b : ROWS * b + ROWS, LANES * high : LANES * high + LANES]
            total = total + lane_roll(part, tiles * b)
        put(face_no, total)

    @pl.when(blk == pl.num_programs(0) - 1)
    def _():
        def copy(slot, carry):
            o_ref[slot] = face_ref[send_ref[slot]]
            return carry

        lax.fori_loop(0, o_ref.shape[0], copy, 0)


def in_hbm(x):
    return pltpu.with_memory_space_constraint(x, pltpu.HBM)


def pack_faces(blocks, send, slots):
    per_dev, fields, cells, plane = blocks.shape
    return pl.pallas_call(
        pack_kernel,
        grid_spec=pltpu.PrefetchScalarGridSpec(
            num_scalar_prefetch=1,
            grid=(per_dev,),
            in_specs=[pl.BlockSpec((1, fields, cells, plane), lambda b, s: (b, 0, 0, 0))],
            out_specs=pl.BlockSpec((slots, fields * ROWS, LANES), lambda b, s: (0, 0, 0)),
            scratch_shapes=[
                pltpu.VMEM((plane, 2 * LANES), bf16),
                pltpu.VMEM((per_dev * 6, fields * ROWS, LANES), bf16),
            ],
        ),
        out_shape=jax.ShapeDtypeStruct((slots, fields * ROWS, LANES), bf16),
        compiler_params=pltpu.CompilerParams(vmem_limit_bytes=16 << 20),
        name="pack_faces",
    )(send, in_hbm(blocks))


class Facts:
    def __init__(self, ints_ref, vals_ref, blk, per_dev, fields):
        self.lookup = lambda face: ints_ref[2 * per_dev + blk * 6 + face]
        self.coarse = lambda face: ints_ref[8 * per_dev + blk * 6 + face]
        self.reaction = lambda f, e: vals_ref[3 * per_dev + fields + f * fields + e]
        self.n = jnp.left_shift(jnp.int32(1), ints_ref[per_dev + blk])
        scale = self.n.astype(f32)
        self.dt = dt_base / scale
        adv = self.dt * scale
        dif = self.dt * scale * scale
        velocity = [vals_ref[blk * 3 + d] for d in range(3)]
        self.minus = [adv * jnp.maximum(v, 0.0) for v in velocity]
        self.plus = [-(adv * jnp.minimum(v, 0.0)) for v in velocity]
        self.rates = [dif * vals_ref[3 * per_dev + f] for f in range(fields)]


def own_matrix(facts, fields, write):
    outflow = sum(facts.minus) + sum(facts.plus)
    size = fields * ROWS
    ri = lax.broadcasted_iota(jnp.int32, (size, size), 0)
    ci = lax.broadcasted_iota(jnp.int32, (size, size), 1)
    matrix = jnp.zeros((size, size), f32)
    for f in range(fields):
        line = jnp.zeros((size, size), f32)
        for e in range(fields):
            term = facts.dt * facts.reaction(f, e)
            if e == f:
                term = term - (6.0 * facts.rates[f] + outflow)
            line = jnp.where(ci // ROWS == e, term, line)
        matrix = jnp.where(ri // ROWS == f, line, matrix)
    matrix = jnp.where(ri % ROWS == ci % ROWS, matrix, 0.0)
    high = matrix.astype(bf16)
    write(0, high)
    write(size, (matrix - high.astype(f32)).astype(bf16))
    write(2 * size, high)


def to_planes(load, state, cells, tiles):
    groups = LANES // cells
    group = lane_ids() // cells
    for it in range(cells // ROWS):
        for half in range(tiles // groups):
            source = [load((tiles // groups) * b + half, it) for b in range(groups)]
            shifted = []
            for d in range(groups):
                x = source[d % groups]
                for g in range(1, groups):
                    x = jnp.where(group == g, source[(g + d) % groups], x)
                shifted.append(lane_roll(x, cells * d))
            for jj in range(groups):
                out = shifted[(0 - jj) % groups]
                for b in range(1, groups):
                    out = jnp.where(group == b, shifted[(b - jj) % groups], out)
                state[:, groups * half + jj + 1, pl.ds(PAD + ROWS * it, ROWS), :] = out


def from_planes(state, store, cells, tiles):
    groups = LANES // cells
    group = lane_ids() // cells
    for it in range(cells // 16):
        for half in range(tiles // groups):
            outs = [[] for _ in range(groups)]
            for sub in range(2):
                rows = pl.ds(PAD + 16 * it + ROWS * sub, ROWS)
                source = [state[:, groups * half + jj + 1, rows, :] for jj in range(groups)]
                shifted = []
                for d in range(groups):
                    x = source[(0 - d) % groups]
                    for g in range(1, groups):
                        x = jnp.where(group == g, source[(g - d) % groups], x)
                    shifted.append(lane_roll(x, -cells * d))
                for b in range(groups):
                    out = shifted[b % groups]
                    for jj in range(1, groups):
                        out = jnp.where(group == jj, shifted[(b - jj) % groups], out)
                    outs[b].append(out)
            for b in range(groups):
                both = jnp.concatenate(outs[b], axis=1).astype(bf16)
                store((tiles // groups) * b + half, it, both)


def wrap_planes(state, side_ref, cells, tiles):
    lane = lane_ids()
    for it in range(cells // ROWS):
        rows = pl.ds(PAD + ROWS * it, ROWS)
        side = 0.0 if side_ref is None else side_ref[:, pl.ds(ROWS * it, ROWS), :]
        state[:, 0, rows, :] = jnp.where(lane < cells, side, lane_roll(state[:, tiles, rows, :], cells))
        state[:, tiles + 1, rows, :] = jnp.where(
            lane >= LANES - cells, side, lane_roll(state[:, 1, rows, :], -cells)
        )


def substep(src, put, edge_ref, own, facts, fields, cells, tiles):
    lane = lax.broadcasted_iota(jnp.int32, (ROWS, LANES), 1)
    k_first = lane % cells == 0
    k_last = lane % cells == cells - 1
    minus, plus, rates = facts.minus, facts.plus, facts.rates

    def two_tiles(pair, carry):
        for it in range(cells // ROWS):
            row = PAD + ROWS * it
            centre = [
                [src[f, 2 * pair + 1 + q, pl.ds(row, ROWS), :] for f in range(fields)]
                for q in range(2)
            ]
            both = jnp.concatenate([jnp.concatenate(c, axis=0) for c in centre], axis=1)
            both_high = both.astype(bf16)
            both_low = (both - both_high.astype(f32)).astype(bf16)
            stacked = jnp.concatenate([both_high, both_high, both_low], axis=0)
            mixed = jnp.dot(own, stacked, preferred_element_type=f32)
            for q in range(2):
                t = 2 * pair + q
                for f in range(fields):
                    c = centre[q][f]
                    minus_x = src[f, t + 1, pl.ds(row - 1, ROWS), :]
                    plus_x = src[f, t + 1, pl.ds(row + 1, ROWS), :]
                    minus_y = src[f, t, pl.ds(row, ROWS), :]
                    plus_y = src[f, t + 2, pl.ds(row, ROWS), :]
                    edge = 0.0 if edge_ref is None else edge_ref[f, t, pl.ds(ROWS * it, ROWS), :]
                    minus_z = jnp.where(k_first, edge, lane_roll(c, 1))
                    plus_z = jnp.where(k_last, edge, lane_roll(c, -1))
                    near = (rates[f] + minus[0]) * minus_x + (rates[f] + plus[0]) * plus_x
                    near += (rates[f] + minus[1]) * minus_y + (rates[f] + plus[1]) * plus_y
                    near += (rates[f] + minus[2]) * minus_z + (rates[f] + plus[2]) * plus_z
                    own_terms = mixed[ROWS * f : ROWS * f + ROWS, LANES * q : LANES * q + LANES]
                    put(f, t, it, near + (c + own_terms))
        return carry

    lax.fori_loop(0, tiles // 2, two_tiles, 0)


def first_kernel(first, per_dev, ints_ref, vals_ref, u_ref, o_ref, rk_out_ref, sa_ref):
    _, fields, cells, plane = u_ref.shape
    tiles = plane // LANES
    facts = Facts(ints_ref, vals_ref, ints_ref[pl.program_id(0) + first], per_dev, fields)

    @pl.when(pl.program_id(0) == 0)
    def _():
        sa_ref[:, :, 0:PAD] = jnp.zeros((fields, tiles + 2, PAD, LANES), f32)
        sa_ref[:, :, PAD + cells :] = jnp.zeros((fields, tiles + 2, PAD, LANES), f32)

    load_block(u_ref, sa_ref, cells, tiles)
    wrap_planes(sa_ref, None, cells, tiles)

    def write(at, value):
        rk_out_ref[0, :, at : at + value.shape[1]] = value

    own_matrix(facts, fields, write)

    def put(f, t, it, value):
        o_ref[0, f, t, pl.ds(ROWS * it, ROWS), :] = value

    substep(sa_ref, put, None, rk_out_ref[0], facts, fields, cells, tiles)


def load_block(u_ref, state, cells, tiles):
    whole = {}

    def load(t, it):
        if (t, it // 2) not in whole:
            whole[t, it // 2] = u_ref[
                0, :, pl.ds(16 * (it // 2), 16), pl.ds(LANES * t, LANES)
            ].astype(f32)
        return whole[t, it // 2][:, ROWS * (it % 2) : ROWS * (it % 2) + ROWS]

    to_planes(load, state, cells, tiles)


def first_substep(ints, vals, blocks, first, count):
    per_dev, fields, cells, plane = blocks.shape
    tiles = plane // LANES
    size = fields * ROWS
    return pl.pallas_call(
        functools.partial(first_kernel, first, per_dev),
        grid_spec=pltpu.PrefetchScalarGridSpec(
            num_scalar_prefetch=2,
            grid=(count,),
            in_specs=[
                pl.BlockSpec((1, fields, cells, plane), lambda b, i, v: (i[b + first], 0, 0, 0))
            ],
            out_specs=[
                pl.BlockSpec((1, fields, tiles, cells, LANES), lambda b, i, v: (b, 0, 0, 0, 0)),
                pl.BlockSpec((1, size, 3 * size), lambda b, i, v: (b, 0, 0)),
            ],
            scratch_shapes=[pltpu.VMEM((fields, tiles + 2, cells + 2 * PAD, LANES), f32)],
        ),
        out_shape=[
            pltpu.HBM((count, fields, tiles, cells, LANES), f32),
            jax.ShapeDtypeStruct((count, size, 3 * size), bf16),
        ],
        compiler_params=pltpu.CompilerParams(vmem_limit_bytes=16 << 20),
        name="first_substep",
    )(ints, vals, in_hbm(blocks))


def place_layers(layer_of, facts, sa_ref, sb_ref, e_ref, side_ref, s_ref, fields, cells, tiles):
    groups = LANES // cells
    lane = lane_ids()
    at_row = row_ids()
    k_first = lane % cells == 0
    k_last = lane % cells == cells - 1
    minus, plus = facts.minus, facts.plus
    odd_lane = lane % 2 == 1
    odd_row = at_row % 2 == 1

    def face(face_no):
        layer = layer_of(face_no).astype(f32).reshape(fields, ROWS, LANES)
        mean = layer + jnp.where(odd_lane, lane_roll(layer, 1), lane_roll(layer, -1))
        mean = mean + jnp.where(odd_row, pltpu.roll(mean, 1, 1), pltpu.roll(mean, ROWS - 1, 1))
        return jnp.where(facts.coarse(face_no) > 0, mean * 0.25, layer)

    states = (sa_ref, sb_ref)
    rate = jnp.concatenate([jnp.full((1, ROWS, LANES), x, f32) for x in facts.rates], axis=0)

    low, high = face(4), lane_roll(face(5), cells - 1)
    weight = jnp.where(k_first, rate + minus[2], jnp.where(k_last, rate + plus[2], 0.0))
    for it in range(cells // ROWS):
        rows = pl.ds(ROWS * it, ROWS)
        for t in range(tiles):
            at = tiles * it + t
            edge = lane_roll(jnp.where(lane % cells == at, low, high), -at)
            e_ref[:, t, rows, :] = edge
            if s_ref is not None:
                sa_ref[:, t + 1, pl.ds(PAD + ROWS * it, ROWS), :] = (
                    s_ref[0, :, t, rows, :] + weight * edge
                )

    low, high = face(2), face(3)
    for it in range(cells // ROWS):
        rows = pl.ds(PAD + ROWS * it, ROWS)
        side = jnp.where(
            lane < cells,
            lane_roll(low, -cells * it),
            lane_roll(high, cells * (groups - 1 - it)),
        )
        side_ref[:, pl.ds(ROWS * it, ROWS), :] = side
        if s_ref is not None:
            sa_ref[:, 1, rows, :] += jnp.where(lane < cells, (rate + minus[1]) * side, 0.0)
            sa_ref[:, tiles, rows, :] += jnp.where(
                lane >= LANES - cells, (rate + plus[1]) * side, 0.0
            )

    low, high = face(0), face(1)
    low_part = (rate + minus[0]) * low
    high_part = (rate + plus[0]) * high
    for t in range(tiles):
        if s_ref is not None:
            sa_ref[:, t + 1, PAD : PAD + 1, :] += low_part[:, t : t + 1, :]
            sa_ref[:, t + 1, PAD + cells - 1 : PAD + cells, :] += high_part[:, t : t + 1, :]
        for state in states:
            state[:, t + 1, PAD - 1 : PAD, :] = low[:, t : t + 1, :]
            state[:, t + 1, PAD + cells : PAD + cells + 1, :] = high[:, t : t + 1, :]
    wrap_planes(sa_ref, side_ref, cells, tiles)


def make_step(own, facts, e_ref, side_ref, fields, cells, tiles):
    def step(src, dst):
        def put(f, t, it, value):
            dst[f, t + 1, pl.ds(PAD + ROWS * it, ROWS), :] = value

        substep(src, put, e_ref, own, facts, fields, cells, tiles)
        wrap_planes(dst, side_ref, cells, tiles)

    return step


def make_finish(o_ref, cells, tiles):
    def finish(src):
        def store(t, it, value):
            o_ref[0, :, pl.ds(16 * it, 16), pl.ds(LANES * t, LANES)] = value

        from_planes(src, store, cells, tiles)

    return finish


def stay_kernel(first, count, per_dev, ints_ref, vals_ref, s_ref, rk_ref, arr_ref, *refs):
    o_ref, sa_ref, sb_ref, e_ref, side_ref, layer_ref, sems = refs[-7:]
    _, fields, tiles, cells, _ = s_ref.shape
    at = pl.program_id(0)
    facts = Facts(ints_ref, vals_ref, ints_ref[at + first], per_dev, fields)

    def fetch(place, face_no, lookup):
        return pltpu.make_async_copy(
            arr_ref.at[lookup], layer_ref.at[place, face_no], sems.at[place, face_no]
        )

    @pl.when(at == 0)
    def _():
        for place in range(count):
            blk = ints_ref[place + first]
            for face_no in range(6):
                fetch(place, face_no, ints_ref[2 * per_dev + blk * 6 + face_no]).start()

    for face_no in range(6):
        fetch(at, face_no, facts.lookup(face_no)).wait()
    place_layers(
        lambda face_no: layer_ref[at, face_no],
        facts, sa_ref, sb_ref, e_ref, side_ref, s_ref, fields, cells, tiles,
    )
    step = make_step(rk_ref[0], facts, e_ref, side_ref, fields, cells, tiles)
    finish = make_finish(o_ref, cells, tiles)

    @pl.when(facts.n == 1)
    def _():
        finish(sa_ref)

    @pl.when(facts.n > 1)
    def _():
        def two(i, carry):
            step(sa_ref, sb_ref)
            step(sb_ref, sa_ref)
            return carry

        lax.fori_loop(0, (facts.n - 2) // 2, two, 0)
        step(sa_ref, sb_ref)
        finish(sb_ref)


def state_scratch(fields, cells, tiles):
    padded = (fields, tiles + 2, cells + 2 * PAD, LANES)
    return [
        pltpu.VMEM(padded, f32),
        pltpu.VMEM(padded, f32),
        pltpu.VMEM((fields, tiles, cells, LANES), f32),
        pltpu.VMEM((fields, cells, LANES), f32),
    ]


def advance_stay(ints, vals, started, own, arrived, plane, first, per_dev, skip, count, into=None):
    _, fields, tiles, cells, _ = started.shape
    shape = (1, fields, cells, plane)
    at = first + skip
    whole = [] if into is None else [into]
    return pl.pallas_call(
        functools.partial(stay_kernel, at, count, per_dev),
        grid_spec=pltpu.PrefetchScalarGridSpec(
            num_scalar_prefetch=2,
            grid=(count,),
            in_specs=[
                pl.BlockSpec((1,) + started.shape[1:], lambda b, i, v: (b + skip, 0, 0, 0, 0)),
                pl.BlockSpec((1,) + own.shape[1:], lambda b, i, v: (b + skip, 0, 0)),
                pl.BlockSpec(memory_space=pl.ANY),
            ]
            + [pl.BlockSpec(memory_space=pl.ANY) for _ in whole],
            out_specs=pl.BlockSpec(shape, lambda b, i, v: (i[b + at], 0, 0, 0)),
            scratch_shapes=state_scratch(fields, cells, tiles)
            + [
                pltpu.VMEM((count, 6) + arrived.shape[1:], bf16),
                pltpu.SemaphoreType.DMA((count, 6)),
            ],
        ),
        out_shape=jax.ShapeDtypeStruct((per_dev, fields, cells, plane), bf16),
        input_output_aliases={} if into is None else {5: 0},
        compiler_params=pltpu.CompilerParams(vmem_limit_bytes=20 << 20),
        name="advance_stay",
    )(ints, vals, in_hbm(started), own, arrived, *whole)


def traded_kernel(choices, ints_ref, vals_ref, *refs):
    raw_refs, layer_refs, refs = refs[:choices], refs[choices : 2 * choices], refs[2 * choices + 1 :]
    o_ref, sa_ref, sb_ref, e_ref, side_ref, rk_ref, raw_ref, layer_ref, sems = refs
    _, fields, cells, plane = raw_ref.shape
    tiles = plane // LANES
    facts = Facts(ints_ref, vals_ref, 0, 1, fields)
    choice = ints_ref[15]
    for c in range(choices):

        @pl.when(choice == c)
        def _():
            raw_copy = pltpu.make_async_copy(raw_refs[c], raw_ref, sems.at[0])
            layer_copy = pltpu.make_async_copy(layer_refs[c], layer_ref, sems.at[1])
            raw_copy.start()
            layer_copy.start()
            raw_copy.wait()
            layer_copy.wait()

    def write(at, value):
        rk_ref[:, at : at + value.shape[1]] = value

    own_matrix(facts, fields, write)
    load_block(raw_ref, sa_ref, cells, tiles)
    place_layers(
        lambda face_no: layer_ref[face_no],
        facts, sa_ref, sb_ref, e_ref, side_ref, None, fields, cells, tiles,
    )
    step = make_step(rk_ref[...], facts, e_ref, side_ref, fields, cells, tiles)
    finish = make_finish(o_ref, cells, tiles)

    @pl.when(facts.n == 1)
    def _():
        step(sa_ref, sb_ref)
        finish(sb_ref)

    @pl.when(facts.n > 1)
    def _():
        def two(i, carry):
            step(sa_ref, sb_ref)
            step(sb_ref, sa_ref)
            return carry

        lax.fori_loop(0, facts.n // 2, two, 0)
        finish(sa_ref)


def advance_traded(ints, vals, raws, layers, into):
    per_dev, fields, cells, plane = into.shape
    tiles = plane // LANES
    choices = len(raws)
    size = fields * ROWS
    anywhere = pl.BlockSpec(memory_space=pl.ANY)
    return pl.pallas_call(
        functools.partial(traded_kernel, choices),
        grid_spec=pltpu.PrefetchScalarGridSpec(
            num_scalar_prefetch=2,
            grid=(1,),
            in_specs=[anywhere] * (2 * choices + 1),
            out_specs=pl.BlockSpec((1, fields, cells, plane), lambda b, i, v: (i[14], 0, 0, 0)),
            scratch_shapes=state_scratch(fields, cells, tiles)
            + [
                pltpu.VMEM((size, 3 * size), bf16),
                pltpu.VMEM((1, fields, cells, plane), bf16),
                pltpu.VMEM((6, size, LANES), bf16),
                pltpu.SemaphoreType.DMA((2,)),
            ],
        ),
        out_shape=jax.ShapeDtypeStruct(into.shape, bf16),
        input_output_aliases={2 + 2 * choices: 0},
        compiler_params=pltpu.CompilerParams(vmem_limit_bytes=20 << 20),
        name="advance_traded",
    )(ints, vals, *raws, *layers, into)


def plan(wanted, my_index, per_dev):
    peers, requests = wanted.shape
    at = lax.broadcasted_iota(jnp.int32, wanted.shape, 1)
    source_dev = wanted // per_dev
    code = wanted % per_dev * 6 + jnp.bitwise_xor(at % 6, 1)
    key = at * 64 + code
    match = source_dev == my_index
    first = jnp.min(jnp.where(match, key, 64 * requests), axis=1) % 64
    second = jnp.max(jnp.where(match, key, 0), axis=1) % 64
    send = jnp.stack([first, second], axis=1).reshape(2 * peers)
    mine = lax.dynamic_slice_in_dim(wanted, my_index, 1, 0)[0]
    my_source = mine // per_dev
    order = jnp.arange(requests, dtype=jnp.int32)
    repeated = (my_source[:, None] == my_source[None, :]) & (order[None, :] < order[:, None])
    lookup = my_source * 2 + jnp.any(repeated, axis=1).astype(jnp.int32)
    return send, mine, lookup


def local(
    block_state,
    block_level,
    block_velocity,
    diffusivity,
    reaction_matrix,
    ghost_source,
    swap_bit,
    swap_slot,
):
    blocks = block_state[0]
    per_dev, fields, cells, plane = blocks.shape
    peers = lax.axis_size(("gy", "gz"))
    my_index = lax.axis_index(("gy", "gz"))
    levels = block_level[0]
    wanted = ghost_source[0].reshape(peers, per_dev * 6)
    send, mine, lookup = plan(wanted, my_index, per_dev)
    outgoing = pack_faces(blocks, send, 2 * peers)
    arrived = lax.all_to_all(outgoing, ("gy", "gz"), split_axis=0, concat_axis=0, tiled=True)

    own_levels = lax.dynamic_slice_in_dim(levels, my_index * per_dev, per_dev, 0)
    known = mine[:, None] == jnp.arange(levels.shape[0], dtype=jnp.int32)[None, :]
    source_levels = jnp.sum(jnp.where(known, levels[None, :], 0), axis=1)
    coarse = (source_levels.reshape(per_dev, 6) != own_levels[:, None]).astype(jnp.int32)
    bit_here = swap_bit[0, 0, 0]
    slot_here = swap_slot[0, 0, 0]
    rest = jnp.arange(per_dev, dtype=jnp.int32)
    rest = jnp.where(rest == 0, slot_here, rest - (rest <= slot_here))
    ints = jnp.concatenate([rest, own_levels, lookup, coarse.reshape(-1)])
    speeds = block_velocity[0]
    vals = jnp.concatenate([speeds.astype(f32).reshape(-1), diffusivity, reaction_matrix.reshape(-1)])
    pick = lambda x, size: lax.dynamic_slice_in_dim(x.reshape(-1), slot_here * size, size, 0)
    bits = range(lax.axis_size("gx").bit_length() - 1)
    offers = lambda x: [x] + [swapped(x, "gx", bit_no) for bit_no in bits]

    raws = offers(lax.dynamic_slice_in_dim(blocks, slot_here, 1, 0))
    label = jnp.concatenate(
        [pick(own_levels, 1).astype(bf16), pick(coarse, 6).astype(bf16), pick(speeds, 3)]
    )
    label = jnp.broadcast_to(jnp.pad(label, (0, LABEL[1] - label.shape[0]))[None], LABEL)
    label, *others = offers(label)
    for bit_no in bits:
        label = jnp.where(bit_here == bit_no, others[bit_no], label)
    label = label[0]
    traded_ints = jnp.concatenate(
        [
            jnp.zeros((1,), jnp.int32),
            label[0:1].astype(jnp.int32),
            jnp.arange(6, dtype=jnp.int32),
            label[1:7].astype(jnp.int32),
            slot_here[None],
            bit_here[None] + 1,
        ]
    )
    traded_vals = jnp.concatenate([label[7:10].astype(f32), diffusivity, reaction_matrix.reshape(-1)])

    stay = first_substep(ints, vals, blocks, 1, per_dev - 1)
    arrived, stay, traded_ints, traded_vals = lax.optimization_barrier(
        (arrived, stay, traded_ints, traded_vals)
    )
    layers = jnp.take(arrived, pick(lookup, 6), axis=0, mode="clip")
    result = advance_stay(ints, vals, *stay, arrived, plane, 1, per_dev, 0, 1)
    layers, result = lax.optimization_barrier((layers, result))
    layers = offers(layers)
    result = advance_stay(ints, vals, *stay, arrived, plane, 1, per_dev, 1, per_dev - 2, result)
    raws, layers, result = lax.optimization_barrier((raws, layers, result))
    result = advance_traded(traded_ints, traded_vals, raws, layers, result)
    return result[None]


def solution(mesh):
    in_specs = (
        P("gx", ("gy", "gz"), None, None, None),
        P("gx", None),
        P("gx", ("gy", "gz"), None),
        P(),
        P(),
        P("gx", None, None),
        P("gx", "gy", "gz"),
        P("gx", "gy", "gz"),
    )
    out_specs = P("gx", ("gy", "gz"), None, None, None)
    return jax.shard_map(local, mesh=mesh, in_specs=in_specs, out_specs=out_specs, check_vma=False)
```

```python
import functools

import jax
import jax.numpy as jnp
from jax import lax
from jax.experimental import pallas as pl
from jax.experimental.pallas import tpu as pltpu
from jax.sharding import PartitionSpec as P

f32 = jnp.float32
bf16 = jnp.bfloat16
dt_base = 0.05
LANES = 128
ROWS = 8
PAD = 8
LABEL = (16, LANES)


def swapped(x, axis, bit):
    return lax.ppermute(x, axis, [(i, i ^ 1 << bit) for i in range(lax.axis_size(axis))])


def lane_roll(x, shift):
    shift = shift % LANES
    return x if shift == 0 else pltpu.roll(x, shift, x.ndim - 1)


def lane_ids():
    return lax.broadcasted_iota(jnp.int32, (1, ROWS, LANES), 2)


def row_ids():
    return lax.broadcasted_iota(jnp.int32, (1, ROWS, LANES), 1)


def pack_kernel(send_ref, u_ref, o_ref, sel_ref, face_ref):
    blk = pl.program_id(0)
    _, fields, cells, plane = u_ref.shape
    groups = LANES // cells
    tiles = plane // LANES

    @pl.when(blk == 0)
    def _():
        row = lax.broadcasted_iota(jnp.int32, sel_ref.shape, 0)
        col = lax.broadcasted_iota(jnp.int32, sel_ref.shape, 1)
        high = col // LANES
        within = col % LANES
        r = within % cells
        b = within // cells
        source = (tiles * b + r) * cells + high * (cells - 1)
        sel_ref[...] = jnp.where((r < tiles) & (row == source), 1.0, 0.0).astype(bf16)

    lane = lane_ids()
    group = lane // cells
    at_row = row_ids()

    def put(face_no, value):
        face_ref[blk * 6 + face_no] = value.reshape(fields * ROWS, LANES).astype(bf16)

    for face_no, edge in ((0, 0), (1, cells - 1)):
        pieces = [
            u_ref[0, :, edge : edge + 1, pl.ds(LANES * t, LANES)].astype(f32)
            for t in range(tiles)
        ]
        natural = jnp.concatenate(pieces, axis=1)
        total = jnp.zeros((fields, ROWS, LANES), f32)
        for d in range(groups):
            moved = lane_roll(natural, cells * d)
            for b in range(groups):
                for half in range(tiles // groups):
                    r = groups * half + (b - d) % groups
                    t = (tiles // groups) * b + half
                    shift = (r - t) % ROWS
                    here = pltpu.roll(moved, shift, 1) if shift else moved
                    total = jnp.where((group == b) & (at_row == r), here, total)
        put(face_no, total)
    for face_no, tile, source in ((2, 0, 0), (3, tiles - 1, groups - 1)):
        strip = u_ref[0, :, :, pl.ds(LANES * tile, LANES)].astype(f32)
        total = jnp.zeros((fields, ROWS, LANES), f32)
        for b in range(groups):
            moved = lane_roll(strip[:, ROWS * b : ROWS * b + ROWS], cells * (b - source))
            total = jnp.where(group == b, moved, total)
        put(face_no, total)
    picked = jnp.dot(
        u_ref[0].reshape(fields * cells, plane), sel_ref[...], preferred_element_type=f32
    ).reshape(fields, cells, 2 * LANES)
    for face_no, high in ((4, 0), (5, 1)):
        total = jnp.zeros((fields, ROWS, LANES), f32)
        for b in range(groups):
            part = picked[:, ROWS * b : ROWS * b + ROWS, LANES * high : LANES * high + LANES]
            total = total + lane_roll(part, tiles * b)
        put(face_no, total)

    @pl.when(blk == pl.num_programs(0) - 1)
    def _():
        def copy(slot, carry):
            o_ref[slot] = face_ref[send_ref[slot]]
            return carry

        lax.fori_loop(0, o_ref.shape[0], copy, 0)


def in_hbm(x):
    return pltpu.with_memory_space_constraint(x, pltpu.HBM)


def pack_faces(blocks, send, slots):
    per_dev, fields, cells, plane = blocks.shape
    return pl.pallas_call(
        pack_kernel,
        grid_spec=pltpu.PrefetchScalarGridSpec(
            num_scalar_prefetch=1,
            grid=(per_dev,),
            in_specs=[pl.BlockSpec((1, fields, cells, plane), lambda b, s: (b, 0, 0, 0))],
            out_specs=pl.BlockSpec((slots, fields * ROWS, LANES), lambda b, s: (0, 0, 0)),
            scratch_shapes=[
                pltpu.VMEM((plane, 2 * LANES), bf16),
                pltpu.VMEM((per_dev * 6, fields * ROWS, LANES), bf16),
            ],
        ),
        out_shape=jax.ShapeDtypeStruct((slots, fields * ROWS, LANES), bf16),
        compiler_params=pltpu.CompilerParams(vmem_limit_bytes=16 << 20),
        name="pack_faces",
    )(send, in_hbm(blocks))


class Facts:
    def __init__(self, ints_ref, vals_ref, blk, per_dev, fields):
        self.lookup = lambda face: ints_ref[2 * per_dev + blk * 6 + face]
        self.coarse = lambda face: ints_ref[8 * per_dev + blk * 6 + face]
        self.reaction = lambda f, e: vals_ref[3 * per_dev + fields + f * fields + e]
        self.n = jnp.left_shift(jnp.int32(1), ints_ref[per_dev + blk])
        scale = self.n.astype(f32)
        self.dt = dt_base / scale
        adv = self.dt * scale
        dif = self.dt * scale * scale
        velocity = [vals_ref[blk * 3 + d] for d in range(3)]
        self.minus = [adv * jnp.maximum(v, 0.0) for v in velocity]
        self.plus = [-(adv * jnp.minimum(v, 0.0)) for v in velocity]
        self.rates = [dif * vals_ref[3 * per_dev + f] for f in range(fields)]


def own_matrix(facts, fields, write):
    outflow = sum(facts.minus) + sum(facts.plus)
    size = fields * ROWS
    ri = lax.broadcasted_iota(jnp.int32, (size, size), 0)
    ci = lax.broadcasted_iota(jnp.int32, (size, size), 1)
    matrix = jnp.zeros((size, size), f32)
    for f in range(fields):
        line = jnp.zeros((size, size), f32)
        for e in range(fields):
            term = facts.dt * facts.reaction(f, e)
            if e == f:
                term = term - (6.0 * facts.rates[f] + outflow)
            line = jnp.where(ci // ROWS == e, term, line)
        matrix = jnp.where(ri // ROWS == f, line, matrix)
    matrix = jnp.where(ri % ROWS == ci % ROWS, matrix, 0.0)
    high = matrix.astype(bf16)
    write(0, high)
    write(size, (matrix - high.astype(f32)).astype(bf16))
    write(2 * size, high)


def to_planes(load, state, cells, tiles):
    groups = LANES // cells
    group = lane_ids() // cells
    for it in range(cells // ROWS):
        for half in range(tiles // groups):
            source = [load((tiles // groups) * b + half, it) for b in range(groups)]
            shifted = []
            for d in range(groups):
                x = source[d % groups]
                for g in range(1, groups):
                    x = jnp.where(group == g, source[(g + d) % groups], x)
                shifted.append(lane_roll(x, cells * d))
            for jj in range(groups):
                out = shifted[(0 - jj) % groups]
                for b in range(1, groups):
                    out = jnp.where(group == b, shifted[(b - jj) % groups], out)
                state[:, groups * half + jj + 1, pl.ds(PAD + ROWS * it, ROWS), :] = out


def from_planes(state, store, cells, tiles):
    groups = LANES // cells
    group = lane_ids() // cells
    for it in range(cells // 16):
        for half in range(tiles // groups):
            outs = [[] for _ in range(groups)]
            for sub in range(2):
                rows = pl.ds(PAD + 16 * it + ROWS * sub, ROWS)
                source = [state[:, groups * half + jj + 1, rows, :] for jj in range(groups)]
                shifted = []
                for d in range(groups):
                    x = source[(0 - d) % groups]
                    for g in range(1, groups):
                        x = jnp.where(group == g, source[(g - d) % groups], x)
                    shifted.append(lane_roll(x, -cells * d))
                for b in range(groups):
                    out = shifted[b % groups]
                    for jj in range(1, groups):
                        out = jnp.where(group == jj, shifted[(b - jj) % groups], out)
                    outs[b].append(out)
            for b in range(groups):
                both = jnp.concatenate(outs[b], axis=1).astype(bf16)
                store((tiles // groups) * b + half, it, both)


def wrap_planes(state, side_ref, cells, tiles):
    lane = lane_ids()
    for it in range(cells // ROWS):
        rows = pl.ds(PAD + ROWS * it, ROWS)
        side = 0.0 if side_ref is None else side_ref[:, pl.ds(ROWS * it, ROWS), :]
        state[:, 0, rows, :] = jnp.where(lane < cells, side, lane_roll(state[:, tiles, rows, :], cells))
        state[:, tiles + 1, rows, :] = jnp.where(
            lane >= LANES - cells, side, lane_roll(state[:, 1, rows, :], -cells)
        )


def substep(src, put, edge_ref, own, facts, fields, cells, tiles):
    lane = lax.broadcasted_iota(jnp.int32, (ROWS, LANES), 1)
    k_first = lane % cells == 0
    k_last = lane % cells == cells - 1
    minus, plus, rates = facts.minus, facts.plus, facts.rates

    def two_tiles(pair, carry):
        for it in range(cells // ROWS):
            row = PAD + ROWS * it
            centre = [
                [src[f, 2 * pair + 1 + q, pl.ds(row, ROWS), :] for f in range(fields)]
                for q in range(2)
            ]
            both = jnp.concatenate([jnp.concatenate(c, axis=0) for c in centre], axis=1)
            both_high = both.astype(bf16)
            both_low = (both - both_high.astype(f32)).astype(bf16)
            stacked = jnp.concatenate([both_high, both_high, both_low], axis=0)
            mixed = jnp.dot(own, stacked, preferred_element_type=f32)
            for q in range(2):
                t = 2 * pair + q
                for f in range(fields):
                    c = centre[q][f]
                    minus_x = src[f, t + 1, pl.ds(row - 1, ROWS), :]
                    plus_x = src[f, t + 1, pl.ds(row + 1, ROWS), :]
                    minus_y = src[f, t, pl.ds(row, ROWS), :]
                    plus_y = src[f, t + 2, pl.ds(row, ROWS), :]
                    edge = 0.0 if edge_ref is None else edge_ref[f, t, pl.ds(ROWS * it, ROWS), :]
                    minus_z = jnp.where(k_first, edge, lane_roll(c, 1))
                    plus_z = jnp.where(k_last, edge, lane_roll(c, -1))
                    near = (rates[f] + minus[0]) * minus_x + (rates[f] + plus[0]) * plus_x
                    near += (rates[f] + minus[1]) * minus_y + (rates[f] + plus[1]) * plus_y
                    near += (rates[f] + minus[2]) * minus_z + (rates[f] + plus[2]) * plus_z
                    own_terms = mixed[ROWS * f : ROWS * f + ROWS, LANES * q : LANES * q + LANES]
                    put(f, t, it, near + (c + own_terms))
        return carry

    lax.fori_loop(0, tiles // 2, two_tiles, 0)


def first_kernel(first, per_dev, ints_ref, vals_ref, u_ref, o_ref, rk_out_ref, sa_ref):
    _, fields, cells, plane = u_ref.shape
    tiles = plane // LANES
    facts = Facts(ints_ref, vals_ref, ints_ref[pl.program_id(0) + first], per_dev, fields)

    @pl.when(pl.program_id(0) == 0)
    def _():
        sa_ref[:, :, 0:PAD] = jnp.zeros((fields, tiles + 2, PAD, LANES), f32)
        sa_ref[:, :, PAD + cells :] = jnp.zeros((fields, tiles + 2, PAD, LANES), f32)

    load_block(u_ref, sa_ref, cells, tiles)
    wrap_planes(sa_ref, None, cells, tiles)

    def write(at, value):
        rk_out_ref[0, :, at : at + value.shape[1]] = value

    own_matrix(facts, fields, write)

    def put(f, t, it, value):
        o_ref[0, f, t, pl.ds(ROWS * it, ROWS), :] = value

    substep(sa_ref, put, None, rk_out_ref[0], facts, fields, cells, tiles)


def load_block(u_ref, state, cells, tiles):
    whole = {}

    def load(t, it):
        if (t, it // 2) not in whole:
            whole[t, it // 2] = u_ref[
                0, :, pl.ds(16 * (it // 2), 16), pl.ds(LANES * t, LANES)
            ].astype(f32)
        return whole[t, it // 2][:, ROWS * (it % 2) : ROWS * (it % 2) + ROWS]

    to_planes(load, state, cells, tiles)


def first_substep(ints, vals, blocks, first, count):
    per_dev, fields, cells, plane = blocks.shape
    tiles = plane // LANES
    size = fields * ROWS
    return pl.pallas_call(
        functools.partial(first_kernel, first, per_dev),
        grid_spec=pltpu.PrefetchScalarGridSpec(
            num_scalar_prefetch=2,
            grid=(count,),
            in_specs=[
                pl.BlockSpec((1, fields, cells, plane), lambda b, i, v: (i[b + first], 0, 0, 0))
            ],
            out_specs=[
                pl.BlockSpec((1, fields, tiles, cells, LANES), lambda b, i, v: (b, 0, 0, 0, 0)),
                pl.BlockSpec((1, size, 3 * size), lambda b, i, v: (b, 0, 0)),
            ],
            scratch_shapes=[pltpu.VMEM((fields, tiles + 2, cells + 2 * PAD, LANES), f32)],
        ),
        out_shape=[
            pltpu.HBM((count, fields, tiles, cells, LANES), f32),
            jax.ShapeDtypeStruct((count, size, 3 * size), bf16),
        ],
        compiler_params=pltpu.CompilerParams(vmem_limit_bytes=16 << 20),
        name="first_substep",
    )(ints, vals, in_hbm(blocks))


def place_layers(layer_of, facts, sa_ref, sb_ref, e_ref, side_ref, s_ref, fields, cells, tiles):
    groups = LANES // cells
    lane = lane_ids()
    at_row = row_ids()
    k_first = lane % cells == 0
    k_last = lane % cells == cells - 1
    minus, plus = facts.minus, facts.plus
    odd_lane = lane % 2 == 1
    odd_row = at_row % 2 == 1

    def face(face_no):
        layer = layer_of(face_no).astype(f32).reshape(fields, ROWS, LANES)
        mean = layer + jnp.where(odd_lane, lane_roll(layer, 1), lane_roll(layer, -1))
        mean = mean + jnp.where(odd_row, pltpu.roll(mean, 1, 1), pltpu.roll(mean, ROWS - 1, 1))
        return jnp.where(facts.coarse(face_no) > 0, mean * 0.25, layer)

    states = (sa_ref, sb_ref)
    rate = jnp.concatenate([jnp.full((1, ROWS, LANES), x, f32) for x in facts.rates], axis=0)

    low, high = face(4), lane_roll(face(5), cells - 1)
    weight = jnp.where(k_first, rate + minus[2], jnp.where(k_last, rate + plus[2], 0.0))
    for it in range(cells // ROWS):
        rows = pl.ds(ROWS * it, ROWS)
        for t in range(tiles):
            at = tiles * it + t
            edge = lane_roll(jnp.where(lane % cells == at, low, high), -at)
            e_ref[:, t, rows, :] = edge
            if s_ref is not None:
                sa_ref[:, t + 1, pl.ds(PAD + ROWS * it, ROWS), :] = (
                    s_ref[0, :, t, rows, :] + weight * edge
                )

    low, high = face(2), face(3)
    for it in range(cells // ROWS):
        rows = pl.ds(PAD + ROWS * it, ROWS)
        side = jnp.where(
            lane < cells,
            lane_roll(low, -cells * it),
            lane_roll(high, cells * (groups - 1 - it)),
        )
        side_ref[:, pl.ds(ROWS * it, ROWS), :] = side
        if s_ref is not None:
            sa_ref[:, 1, rows, :] += jnp.where(lane < cells, (rate + minus[1]) * side, 0.0)
            sa_ref[:, tiles, rows, :] += jnp.where(
                lane >= LANES - cells, (rate + plus[1]) * side, 0.0
            )

    low, high = face(0), face(1)
    low_part = (rate + minus[0]) * low
    high_part = (rate + plus[0]) * high
    for t in range(tiles):
        if s_ref is not None:
            sa_ref[:, t + 1, PAD : PAD + 1, :] += low_part[:, t : t + 1, :]
            sa_ref[:, t + 1, PAD + cells - 1 : PAD + cells, :] += high_part[:, t : t + 1, :]
        for state in states:
            state[:, t + 1, PAD - 1 : PAD, :] = low[:, t : t + 1, :]
            state[:, t + 1, PAD + cells : PAD + cells + 1, :] = high[:, t : t + 1, :]
    wrap_planes(sa_ref, side_ref, cells, tiles)


def make_step(own, facts, e_ref, side_ref, fields, cells, tiles):
    def step(src, dst):
        def put(f, t, it, value):
            dst[f, t + 1, pl.ds(PAD + ROWS * it, ROWS), :] = value

        substep(src, put, e_ref, own, facts, fields, cells, tiles)
        wrap_planes(dst, side_ref, cells, tiles)

    return step


def make_finish(o_ref, cells, tiles):
    def finish(src):
        def store(t, it, value):
            o_ref[0, :, pl.ds(16 * it, 16), pl.ds(LANES * t, LANES)] = value

        from_planes(src, store, cells, tiles)

    return finish


def stay_kernel(first, count, per_dev, ints_ref, vals_ref, s_ref, rk_ref, arr_ref, *refs):
    o_ref, sa_ref, sb_ref, e_ref, side_ref, layer_ref, sems = refs[-7:]
    _, fields, tiles, cells, _ = s_ref.shape
    at = pl.program_id(0)
    facts = Facts(ints_ref, vals_ref, ints_ref[at + first], per_dev, fields)

    def fetch(place, face_no, lookup):
        return pltpu.make_async_copy(
            arr_ref.at[lookup], layer_ref.at[place, face_no], sems.at[place, face_no]
        )

    @pl.when(at == 0)
    def _():
        for place in range(count):
            blk = ints_ref[place + first]
            for face_no in range(6):
                fetch(place, face_no, ints_ref[2 * per_dev + blk * 6 + face_no]).start()

    for face_no in range(6):
        fetch(at, face_no, facts.lookup(face_no)).wait()
    place_layers(
        lambda face_no: layer_ref[at, face_no],
        facts, sa_ref, sb_ref, e_ref, side_ref, s_ref, fields, cells, tiles,
    )
    step = make_step(rk_ref[0], facts, e_ref, side_ref, fields, cells, tiles)
    finish = make_finish(o_ref, cells, tiles)

    @pl.when(facts.n == 1)
    def _():
        finish(sa_ref)

    @pl.when(facts.n > 1)
    def _():
        def two(i, carry):
            step(sa_ref, sb_ref)
            step(sb_ref, sa_ref)
            return carry

        lax.fori_loop(0, (facts.n - 2) // 2, two, 0)
        step(sa_ref, sb_ref)
        finish(sb_ref)


def state_scratch(fields, cells, tiles):
    padded = (fields, tiles + 2, cells + 2 * PAD, LANES)
    return [
        pltpu.VMEM(padded, f32),
        pltpu.VMEM(padded, f32),
        pltpu.VMEM((fields, tiles, cells, LANES), f32),
        pltpu.VMEM((fields, cells, LANES), f32),
    ]


def advance_stay(ints, vals, started, own, arrived, plane, first, per_dev):
    count, fields, tiles, cells, _ = started.shape
    shape = (1, fields, cells, plane)
    return pl.pallas_call(
        functools.partial(stay_kernel, first, count, per_dev),
        grid_spec=pltpu.PrefetchScalarGridSpec(
            num_scalar_prefetch=2,
            grid=(count,),
            in_specs=[
                pl.BlockSpec((1,) + started.shape[1:], lambda b, i, v: (b, 0, 0, 0, 0)),
                pl.BlockSpec((1,) + own.shape[1:], lambda b, i, v: (b, 0, 0)),
                pl.BlockSpec(memory_space=pl.ANY),
            ],
            out_specs=pl.BlockSpec(shape, lambda b, i, v: (i[b + first], 0, 0, 0)),
            scratch_shapes=state_scratch(fields, cells, tiles)
            + [
                pltpu.VMEM((count, 6) + arrived.shape[1:], bf16),
                pltpu.SemaphoreType.DMA((count, 6)),
            ],
        ),
        out_shape=jax.ShapeDtypeStruct((per_dev, fields, cells, plane), bf16),
        compiler_params=pltpu.CompilerParams(vmem_limit_bytes=20 << 20),
        name="advance_stay",
    )(ints, vals, in_hbm(started), own, arrived)


def traded_kernel(choices, ints_ref, vals_ref, *refs):
    raw_refs, layers_ref, refs = refs[:choices], refs[choices], refs[choices + 2 :]
    o_ref, sa_ref, sb_ref, e_ref, side_ref, rk_ref, raw_ref, layer_ref, sems = refs
    _, fields, cells, plane = raw_ref.shape
    tiles = plane // LANES
    facts = Facts(ints_ref, vals_ref, 0, 1, fields)
    choice = ints_ref[15]
    layer_copy = pltpu.make_async_copy(layers_ref, layer_ref, sems.at[1])
    layer_copy.start()
    for c in range(choices):

        @pl.when(choice == c)
        def _():
            raw_copy = pltpu.make_async_copy(raw_refs[c], raw_ref, sems.at[0])
            raw_copy.start()
            raw_copy.wait()

    layer_copy.wait()

    def write(at, value):
        rk_ref[:, at : at + value.shape[1]] = value

    own_matrix(facts, fields, write)
    load_block(raw_ref, sa_ref, cells, tiles)
    place_layers(
        lambda face_no: layer_ref[face_no],
        facts, sa_ref, sb_ref, e_ref, side_ref, None, fields, cells, tiles,
    )
    step = make_step(rk_ref[...], facts, e_ref, side_ref, fields, cells, tiles)
    finish = make_finish(o_ref, cells, tiles)

    @pl.when(facts.n == 1)
    def _():
        step(sa_ref, sb_ref)
        finish(sb_ref)

    @pl.when(facts.n > 1)
    def _():
        def two(i, carry):
            step(sa_ref, sb_ref)
            step(sb_ref, sa_ref)
            return carry

        lax.fori_loop(0, facts.n // 2, two, 0)
        finish(sa_ref)


def advance_traded(ints, vals, raws, layers, into):
    per_dev, fields, cells, plane = into.shape
    tiles = plane // LANES
    choices = len(raws)
    size = fields * ROWS
    anywhere = pl.BlockSpec(memory_space=pl.ANY)
    return pl.pallas_call(
        functools.partial(traded_kernel, choices),
        grid_spec=pltpu.PrefetchScalarGridSpec(
            num_scalar_prefetch=2,
            grid=(1,),
            in_specs=[anywhere] * (choices + 2),
            out_specs=pl.BlockSpec((1, fields, cells, plane), lambda b, i, v: (i[14], 0, 0, 0)),
            scratch_shapes=state_scratch(fields, cells, tiles)
            + [
                pltpu.VMEM((size, 3 * size), bf16),
                pltpu.VMEM((1, fields, cells, plane), bf16),
                pltpu.VMEM((6, size, LANES), bf16),
                pltpu.SemaphoreType.DMA((2,)),
            ],
        ),
        out_shape=jax.ShapeDtypeStruct(into.shape, bf16),
        input_output_aliases={3 + choices: 0},
        compiler_params=pltpu.CompilerParams(vmem_limit_bytes=20 << 20),
        name="advance_traded",
    )(ints, vals, *raws, layers, into)


def plan(wanted, my_index, per_dev):
    peers, requests = wanted.shape
    at = lax.broadcasted_iota(jnp.int32, wanted.shape, 1)
    source_dev = wanted // per_dev
    code = wanted % per_dev * 6 + jnp.bitwise_xor(at % 6, 1)
    key = at * 64 + code
    match = source_dev == my_index
    first = jnp.min(jnp.where(match, key, 64 * requests), axis=1) % 64
    second = jnp.max(jnp.where(match, key, 0), axis=1) % 64
    send = jnp.stack([first, second], axis=1).reshape(2 * peers)
    mine = lax.dynamic_slice_in_dim(wanted, my_index, 1, 0)[0]
    my_source = mine // per_dev
    order = jnp.arange(requests, dtype=jnp.int32)
    repeated = (my_source[:, None] == my_source[None, :]) & (order[None, :] < order[:, None])
    lookup = my_source * 2 + jnp.any(repeated, axis=1).astype(jnp.int32)
    return send, mine, lookup


def local(
    block_state,
    block_level,
    block_velocity,
    diffusivity,
    reaction_matrix,
    ghost_source,
    swap_bit,
    swap_slot,
):
    blocks = block_state[0]
    per_dev, fields, cells, plane = blocks.shape
    peers = lax.axis_size(("gy", "gz"))
    my_index = lax.axis_index(("gy", "gz"))
    levels = block_level[0]
    wanted = ghost_source[0].reshape(peers, per_dev * 6)
    send, mine, lookup = plan(wanted, my_index, per_dev)
    outgoing = pack_faces(blocks, send, 2 * peers)
    arrived = lax.all_to_all(outgoing, ("gy", "gz"), split_axis=0, concat_axis=0, tiled=True)

    own_levels = lax.dynamic_slice_in_dim(levels, my_index * per_dev, per_dev, 0)
    known = mine[:, None] == jnp.arange(levels.shape[0], dtype=jnp.int32)[None, :]
    source_levels = jnp.sum(jnp.where(known, levels[None, :], 0), axis=1)
    coarse = (source_levels.reshape(per_dev, 6) != own_levels[:, None]).astype(jnp.int32)
    bit_here = swap_bit[0, 0, 0]
    slot_here = swap_slot[0, 0, 0]
    rest = jnp.arange(per_dev, dtype=jnp.int32)
    rest = jnp.where(rest == 0, slot_here, rest - (rest <= slot_here))
    ints = jnp.concatenate([rest, own_levels, lookup, coarse.reshape(-1)])
    speeds = block_velocity[0]
    vals = jnp.concatenate([speeds.astype(f32).reshape(-1), diffusivity, reaction_matrix.reshape(-1)])
    pick = lambda x, size: lax.dynamic_slice_in_dim(x.reshape(-1), slot_here * size, size, 0)
    bits = range(lax.axis_size("gx").bit_length() - 1)
    offers = lambda x: [x] + [swapped(x, "gx", bit_no) for bit_no in bits]

    flip = jnp.where(bit_here < 0, 0, jnp.left_shift(1, jnp.maximum(bit_here, 0)))
    partner = jnp.bitwise_xor(lax.axis_index("gx").astype(jnp.int32), flip)

    def to_partner(x):
        to = jnp.arange(lax.axis_size("gx"), dtype=jnp.int32)[:, None, None, None] == partner
        return lax.psum_scatter(jnp.where(to, x[None], 0), "gx", scatter_dimension=0, tiled=True)[0]

    raws = offers(lax.dynamic_slice_in_dim(blocks, slot_here, 1, 0))
    label = jnp.concatenate(
        [pick(own_levels, 1).astype(bf16), pick(coarse, 6).astype(bf16), pick(speeds, 3)]
    )
    label = jnp.broadcast_to(jnp.pad(label, (0, LABEL[1] - label.shape[0]))[None], LABEL)
    label = to_partner(label[None])[0, 0]
    traded_ints = jnp.concatenate(
        [
            jnp.zeros((1,), jnp.int32),
            label[0:1].astype(jnp.int32),
            jnp.arange(6, dtype=jnp.int32),
            label[1:7].astype(jnp.int32),
            slot_here[None],
            bit_here[None] + 1,
        ]
    )
    traded_vals = jnp.concatenate([label[7:10].astype(f32), diffusivity, reaction_matrix.reshape(-1)])

    stay = first_substep(ints, vals, blocks, 1, per_dev - 1)
    arrived, stay, raws = lax.optimization_barrier((arrived, stay, raws))
    layers = jnp.take(arrived, pick(lookup, 6), axis=0, mode="clip")
    layers = to_partner(layers)
    result = advance_stay(ints, vals, *stay, arrived, plane, 1, per_dev)
    raws, layers, result = lax.optimization_barrier((raws, layers, result))
    result = advance_traded(traded_ints, traded_vals, raws, layers, result)
    return result[None]


def solution(mesh):
    in_specs = (
        P("gx", ("gy", "gz"), None, None, None),
        P("gx", None),
        P("gx", ("gy", "gz"), None),
        P(),
        P(),
        P("gx", None, None),
        P("gx", "gy", "gz"),
        P("gx", "gy", "gz"),
    )
    out_specs = P("gx", ("gy", "gz"), None, None, None)
    return jax.shard_map(local, mesh=mesh, in_specs=in_specs, out_specs=out_specs, check_vma=False)
```

```python
import functools

import jax
import jax.numpy as jnp
from jax import lax
from jax.experimental import pallas as pl
from jax.experimental.pallas import tpu as pltpu
from jax.sharding import PartitionSpec as P

f32 = jnp.float32
bf16 = jnp.bfloat16
dt_base = 0.05
LANES = 128
ROWS = 8
PAD = 8
LABEL = (16, LANES)


def swapped(x, axis, bit):
    return lax.ppermute(x, axis, [(i, i ^ 1 << bit) for i in range(lax.axis_size(axis))])


def lane_roll(x, shift):
    shift = shift % LANES
    return x if shift == 0 else pltpu.roll(x, shift, x.ndim - 1)


def lane_ids():
    return lax.broadcasted_iota(jnp.int32, (1, ROWS, LANES), 2)


def row_ids():
    return lax.broadcasted_iota(jnp.int32, (1, ROWS, LANES), 1)


def pack_kernel(send_ref, u_ref, o_ref, sel_ref, face_ref):
    blk = pl.program_id(0)
    _, fields, cells, plane = u_ref.shape
    groups = LANES // cells
    tiles = plane // LANES

    @pl.when(blk == 0)
    def _():
        row = lax.broadcasted_iota(jnp.int32, sel_ref.shape, 0)
        col = lax.broadcasted_iota(jnp.int32, sel_ref.shape, 1)
        high = col // LANES
        within = col % LANES
        r = within % cells
        b = within // cells
        source = (tiles * b + r) * cells + high * (cells - 1)
        sel_ref[...] = jnp.where((r < tiles) & (row == source), 1.0, 0.0).astype(bf16)

    lane = lane_ids()
    group = lane // cells
    at_row = row_ids()

    def put(face_no, value):
        face_ref[blk * 6 + face_no] = value.reshape(fields * ROWS, LANES).astype(bf16)

    for face_no, edge in ((0, 0), (1, cells - 1)):
        pieces = [
            u_ref[0, :, edge : edge + 1, pl.ds(LANES * t, LANES)].astype(f32)
            for t in range(tiles)
        ]
        natural = jnp.concatenate(pieces, axis=1)
        total = jnp.zeros((fields, ROWS, LANES), f32)
        for d in range(groups):
            moved = lane_roll(natural, cells * d)
            for b in range(groups):
                for half in range(tiles // groups):
                    r = groups * half + (b - d) % groups
                    t = (tiles // groups) * b + half
                    shift = (r - t) % ROWS
                    here = pltpu.roll(moved, shift, 1) if shift else moved
                    total = jnp.where((group == b) & (at_row == r), here, total)
        put(face_no, total)
    for face_no, tile, source in ((2, 0, 0), (3, tiles - 1, groups - 1)):
        strip = u_ref[0, :, :, pl.ds(LANES * tile, LANES)].astype(f32)
        total = jnp.zeros((fields, ROWS, LANES), f32)
        for b in range(groups):
            moved = lane_roll(strip[:, ROWS * b : ROWS * b + ROWS], cells * (b - source))
            total = jnp.where(group == b, moved, total)
        put(face_no, total)
    picked = jnp.dot(
        u_ref[0].reshape(fields * cells, plane), sel_ref[...], preferred_element_type=f32
    ).reshape(fields, cells, 2 * LANES)
    for face_no, high in ((4, 0), (5, 1)):
        total = jnp.zeros((fields, ROWS, LANES), f32)
        for b in range(groups):
            part = picked[:, ROWS * b : ROWS * b + ROWS, LANES * high : LANES * high + LANES]
            total = total + lane_roll(part, tiles * b)
        put(face_no, total)

    @pl.when(blk == pl.num_programs(0) - 1)
    def _():
        def copy(slot, carry):
            o_ref[slot] = face_ref[send_ref[slot]]
            return carry

        lax.fori_loop(0, o_ref.shape[0], copy, 0)


def in_hbm(x):
    return pltpu.with_memory_space_constraint(x, pltpu.HBM)


def pack_faces(blocks, send, slots):
    per_dev, fields, cells, plane = blocks.shape
    return pl.pallas_call(
        pack_kernel,
        grid_spec=pltpu.PrefetchScalarGridSpec(
            num_scalar_prefetch=1,
            grid=(per_dev,),
            in_specs=[pl.BlockSpec((1, fields, cells, plane), lambda b, s: (b, 0, 0, 0))],
            out_specs=pl.BlockSpec((slots, fields * ROWS, LANES), lambda b, s: (0, 0, 0)),
            scratch_shapes=[
                pltpu.VMEM((plane, 2 * LANES), bf16),
                pltpu.VMEM((per_dev * 6, fields * ROWS, LANES), bf16),
            ],
        ),
        out_shape=jax.ShapeDtypeStruct((slots, fields * ROWS, LANES), bf16),
        compiler_params=pltpu.CompilerParams(vmem_limit_bytes=16 << 20),
        name="pack_faces",
    )(send, blocks)


class Facts:
    def __init__(self, ints_ref, vals_ref, blk, per_dev, fields):
        self.lookup = lambda face: ints_ref[2 * per_dev + blk * 6 + face]
        self.coarse = lambda face: ints_ref[8 * per_dev + blk * 6 + face]
        self.reaction = lambda f, e: vals_ref[3 * per_dev + fields + f * fields + e]
        self.n = jnp.left_shift(jnp.int32(1), ints_ref[per_dev + blk])
        scale = self.n.astype(f32)
        self.dt = dt_base / scale
        adv = self.dt * scale
        dif = self.dt * scale * scale
        velocity = [vals_ref[blk * 3 + d] for d in range(3)]
        self.minus = [adv * jnp.maximum(v, 0.0) for v in velocity]
        self.plus = [-(adv * jnp.minimum(v, 0.0)) for v in velocity]
        self.rates = [dif * vals_ref[3 * per_dev + f] for f in range(fields)]


def own_matrix(facts, fields, write):
    outflow = sum(facts.minus) + sum(facts.plus)
    size = fields * ROWS
    ri = lax.broadcasted_iota(jnp.int32, (size, size), 0)
    ci = lax.broadcasted_iota(jnp.int32, (size, size), 1)
    matrix = jnp.zeros((size, size), f32)
    for f in range(fields):
        line = jnp.zeros((size, size), f32)
        for e in range(fields):
            term = facts.dt * facts.reaction(f, e)
            if e == f:
                term = term - (6.0 * facts.rates[f] + outflow)
            line = jnp.where(ci // ROWS == e, term, line)
        matrix = jnp.where(ri // ROWS == f, line, matrix)
    matrix = jnp.where(ri % ROWS == ci % ROWS, matrix, 0.0)
    high = matrix.astype(bf16)
    write(0, high)
    write(size, (matrix - high.astype(f32)).astype(bf16))
    write(2 * size, high)


def to_planes(load, state, cells, tiles):
    groups = LANES // cells
    group = lane_ids() // cells
    for it in range(cells // ROWS):
        for half in range(tiles // groups):
            source = [load((tiles // groups) * b + half, it) for b in range(groups)]
            shifted = []
            for d in range(groups):
                x = source[d % groups]
                for g in range(1, groups):
                    x = jnp.where(group == g, source[(g + d) % groups], x)
                shifted.append(lane_roll(x, cells * d))
            for jj in range(groups):
                out = shifted[(0 - jj) % groups]
                for b in range(1, groups):
                    out = jnp.where(group == b, shifted[(b - jj) % groups], out)
                state[:, groups * half + jj + 1, pl.ds(PAD + ROWS * it, ROWS), :] = out


def from_planes(state, store, cells, tiles):
    groups = LANES // cells
    group = lane_ids() // cells
    for it in range(cells // 16):
        for half in range(tiles // groups):
            outs = [[] for _ in range(groups)]
            for sub in range(2):
                rows = pl.ds(PAD + 16 * it + ROWS * sub, ROWS)
                source = [state[:, groups * half + jj + 1, rows, :] for jj in range(groups)]
                shifted = []
                for d in range(groups):
                    x = source[(0 - d) % groups]
                    for g in range(1, groups):
                        x = jnp.where(group == g, source[(g - d) % groups], x)
                    shifted.append(lane_roll(x, -cells * d))
                for b in range(groups):
                    out = shifted[b % groups]
                    for jj in range(1, groups):
                        out = jnp.where(group == jj, shifted[(b - jj) % groups], out)
                    outs[b].append(out)
            for b in range(groups):
                both = jnp.concatenate(outs[b], axis=1).astype(bf16)
                store((tiles // groups) * b + half, it, both)


def wrap_planes(state, side_ref, cells, tiles):
    lane = lane_ids()
    for it in range(cells // ROWS):
        rows = pl.ds(PAD + ROWS * it, ROWS)
        side = 0.0 if side_ref is None else side_ref[:, pl.ds(ROWS * it, ROWS), :]
        state[:, 0, rows, :] = jnp.where(lane < cells, side, lane_roll(state[:, tiles, rows, :], cells))
        state[:, tiles + 1, rows, :] = jnp.where(
            lane >= LANES - cells, side, lane_roll(state[:, 1, rows, :], -cells)
        )


def substep(src, put, edge_ref, own, facts, fields, cells, tiles):
    lane = lax.broadcasted_iota(jnp.int32, (ROWS, LANES), 1)
    k_first = lane % cells == 0
    k_last = lane % cells == cells - 1
    minus, plus, rates = facts.minus, facts.plus, facts.rates

    def two_tiles(pair, carry):
        for it in range(cells // ROWS):
            row = PAD + ROWS * it
            centre = [
                [src[f, 2 * pair + 1 + q, pl.ds(row, ROWS), :] for f in range(fields)]
                for q in range(2)
            ]
            both = jnp.concatenate([jnp.concatenate(c, axis=0) for c in centre], axis=1)
            both_high = both.astype(bf16)
            both_low = (both - both_high.astype(f32)).astype(bf16)
            stacked = jnp.concatenate([both_high, both_high, both_low], axis=0)
            mixed = jnp.dot(own, stacked, preferred_element_type=f32)
            for q in range(2):
                t = 2 * pair + q
                for f in range(fields):
                    c = centre[q][f]
                    minus_x = src[f, t + 1, pl.ds(row - 1, ROWS), :]
                    plus_x = src[f, t + 1, pl.ds(row + 1, ROWS), :]
                    minus_y = src[f, t, pl.ds(row, ROWS), :]
                    plus_y = src[f, t + 2, pl.ds(row, ROWS), :]
                    edge = 0.0 if edge_ref is None else edge_ref[f, t, pl.ds(ROWS * it, ROWS), :]
                    minus_z = jnp.where(k_first, edge, lane_roll(c, 1))
                    plus_z = jnp.where(k_last, edge, lane_roll(c, -1))
                    near = (rates[f] + minus[0]) * minus_x + (rates[f] + plus[0]) * plus_x
                    near += (rates[f] + minus[1]) * minus_y + (rates[f] + plus[1]) * plus_y
                    near += (rates[f] + minus[2]) * minus_z + (rates[f] + plus[2]) * plus_z
                    own_terms = mixed[ROWS * f : ROWS * f + ROWS, LANES * q : LANES * q + LANES]
                    put(f, t, it, near + (c + own_terms))
        return carry

    lax.fori_loop(0, tiles // 2, two_tiles, 0)


def first_kernel(first, per_dev, ints_ref, vals_ref, u_ref, o_ref, rk_out_ref, sa_ref):
    _, fields, cells, plane = u_ref.shape
    tiles = plane // LANES
    facts = Facts(ints_ref, vals_ref, ints_ref[pl.program_id(0) + first], per_dev, fields)

    @pl.when(pl.program_id(0) == 0)
    def _():
        sa_ref[:, :, 0:PAD] = jnp.zeros((fields, tiles + 2, PAD, LANES), f32)
        sa_ref[:, :, PAD + cells :] = jnp.zeros((fields, tiles + 2, PAD, LANES), f32)

    load_block(u_ref, sa_ref, cells, tiles)
    wrap_planes(sa_ref, None, cells, tiles)

    def write(at, value):
        rk_out_ref[0, :, at : at + value.shape[1]] = value

    own_matrix(facts, fields, write)

    def put(f, t, it, value):
        o_ref[0, f, t, pl.ds(ROWS * it, ROWS), :] = value

    substep(sa_ref, put, None, rk_out_ref[0], facts, fields, cells, tiles)


def load_block(u_ref, state, cells, tiles):
    whole = {}

    def load(t, it):
        if (t, it // 2) not in whole:
            whole[t, it // 2] = u_ref[
                0, :, pl.ds(16 * (it // 2), 16), pl.ds(LANES * t, LANES)
            ].astype(f32)
        return whole[t, it // 2][:, ROWS * (it % 2) : ROWS * (it % 2) + ROWS]

    to_planes(load, state, cells, tiles)


def first_substep(ints, vals, blocks, first, count):
    per_dev, fields, cells, plane = blocks.shape
    tiles = plane // LANES
    size = fields * ROWS
    return pl.pallas_call(
        functools.partial(first_kernel, first, per_dev),
        grid_spec=pltpu.PrefetchScalarGridSpec(
            num_scalar_prefetch=2,
            grid=(count,),
            in_specs=[
                pl.BlockSpec((1, fields, cells, plane), lambda b, i, v: (i[b + first], 0, 0, 0))
            ],
            out_specs=[
                pl.BlockSpec((1, fields, tiles, cells, LANES), lambda b, i, v: (b, 0, 0, 0, 0)),
                pl.BlockSpec((1, size, 3 * size), lambda b, i, v: (b, 0, 0)),
            ],
            scratch_shapes=[pltpu.VMEM((fields, tiles + 2, cells + 2 * PAD, LANES), f32)],
        ),
        out_shape=[
            pltpu.HBM((count, fields, tiles, cells, LANES), f32),
            jax.ShapeDtypeStruct((count, size, 3 * size), bf16),
        ],
        compiler_params=pltpu.CompilerParams(vmem_limit_bytes=16 << 20),
        name="first_substep",
    )(ints, vals, in_hbm(blocks))


def place_layers(layer_of, facts, sa_ref, sb_ref, e_ref, side_ref, s_ref, fields, cells, tiles):
    groups = LANES // cells
    lane = lane_ids()
    at_row = row_ids()
    k_first = lane % cells == 0
    k_last = lane % cells == cells - 1
    minus, plus = facts.minus, facts.plus
    odd_lane = lane % 2 == 1
    odd_row = at_row % 2 == 1

    def face(face_no):
        layer = layer_of(face_no).astype(f32).reshape(fields, ROWS, LANES)
        mean = layer + jnp.where(odd_lane, lane_roll(layer, 1), lane_roll(layer, -1))
        mean = mean + jnp.where(odd_row, pltpu.roll(mean, 1, 1), pltpu.roll(mean, ROWS - 1, 1))
        return jnp.where(facts.coarse(face_no) > 0, mean * 0.25, layer)

    states = (sa_ref, sb_ref)
    rate = jnp.concatenate([jnp.full((1, ROWS, LANES), x, f32) for x in facts.rates], axis=0)

    low, high = face(4), lane_roll(face(5), cells - 1)
    weight = jnp.where(k_first, rate + minus[2], jnp.where(k_last, rate + plus[2], 0.0))
    for it in range(cells // ROWS):
        rows = pl.ds(ROWS * it, ROWS)
        for t in range(tiles):
            at = tiles * it + t
            edge = lane_roll(jnp.where(lane % cells == at, low, high), -at)
            e_ref[:, t, rows, :] = edge
            if s_ref is not None:
                sa_ref[:, t + 1, pl.ds(PAD + ROWS * it, ROWS), :] = (
                    s_ref[0, :, t, rows, :] + weight * edge
                )

    low, high = face(2), face(3)
    for it in range(cells // ROWS):
        rows = pl.ds(PAD + ROWS * it, ROWS)
        side = jnp.where(
            lane < cells,
            lane_roll(low, -cells * it),
            lane_roll(high, cells * (groups - 1 - it)),
        )
        side_ref[:, pl.ds(ROWS * it, ROWS), :] = side
        if s_ref is not None:
            sa_ref[:, 1, rows, :] += jnp.where(lane < cells, (rate + minus[1]) * side, 0.0)
            sa_ref[:, tiles, rows, :] += jnp.where(
                lane >= LANES - cells, (rate + plus[1]) * side, 0.0
            )

    low, high = face(0), face(1)
    low_part = (rate + minus[0]) * low
    high_part = (rate + plus[0]) * high
    for t in range(tiles):
        if s_ref is not None:
            sa_ref[:, t + 1, PAD : PAD + 1, :] += low_part[:, t : t + 1, :]
            sa_ref[:, t + 1, PAD + cells - 1 : PAD + cells, :] += high_part[:, t : t + 1, :]
        for state in states:
            state[:, t + 1, PAD - 1 : PAD, :] = low[:, t : t + 1, :]
            state[:, t + 1, PAD + cells : PAD + cells + 1, :] = high[:, t : t + 1, :]
    wrap_planes(sa_ref, side_ref, cells, tiles)


def make_step(own, facts, e_ref, side_ref, fields, cells, tiles):
    def step(src, dst):
        def put(f, t, it, value):
            dst[f, t + 1, pl.ds(PAD + ROWS * it, ROWS), :] = value

        substep(src, put, e_ref, own, facts, fields, cells, tiles)
        wrap_planes(dst, side_ref, cells, tiles)

    return step


def make_finish(o_ref, cells, tiles):
    def finish(src):
        def store(t, it, value):
            o_ref[0, :, pl.ds(16 * it, 16), pl.ds(LANES * t, LANES)] = value

        from_planes(src, store, cells, tiles)

    return finish


def stay_kernel(first, count, per_dev, ints_ref, vals_ref, s_ref, rk_ref, arr_ref, *refs):
    o_ref, sa_ref, sb_ref, e_ref, side_ref, layer_ref, sems = refs[-7:]
    _, fields, tiles, cells, _ = s_ref.shape
    at = pl.program_id(0)
    facts = Facts(ints_ref, vals_ref, ints_ref[at + first], per_dev, fields)

    def fetch(place, face_no, lookup):
        return pltpu.make_async_copy(
            arr_ref.at[lookup], layer_ref.at[place, face_no], sems.at[place, face_no]
        )

    @pl.when(at == 0)
    def _():
        for place in range(count):
            blk = ints_ref[place + first]
            for face_no in range(6):
                fetch(place, face_no, ints_ref[2 * per_dev + blk * 6 + face_no]).start()

    for face_no in range(6):
        fetch(at, face_no, facts.lookup(face_no)).wait()
    place_layers(
        lambda face_no: layer_ref[at, face_no],
        facts, sa_ref, sb_ref, e_ref, side_ref, s_ref, fields, cells, tiles,
    )
    step = make_step(rk_ref[0], facts, e_ref, side_ref, fields, cells, tiles)
    finish = make_finish(o_ref, cells, tiles)

    @pl.when(facts.n == 1)
    def _():
        finish(sa_ref)

    @pl.when(facts.n > 1)
    def _():
        def two(i, carry):
            step(sa_ref, sb_ref)
            step(sb_ref, sa_ref)
            return carry

        lax.fori_loop(0, (facts.n - 2) // 2, two, 0)
        step(sa_ref, sb_ref)
        finish(sb_ref)


def state_scratch(fields, cells, tiles):
    padded = (fields, tiles + 2, cells + 2 * PAD, LANES)
    return [
        pltpu.VMEM(padded, f32),
        pltpu.VMEM(padded, f32),
        pltpu.VMEM((fields, tiles, cells, LANES), f32),
        pltpu.VMEM((fields, cells, LANES), f32),
    ]


def advance_stay(ints, vals, started, own, arrived, plane, first, per_dev):
    count, fields, tiles, cells, _ = started.shape
    shape = (1, fields, cells, plane)
    return pl.pallas_call(
        functools.partial(stay_kernel, first, count, per_dev),
        grid_spec=pltpu.PrefetchScalarGridSpec(
            num_scalar_prefetch=2,
            grid=(count,),
            in_specs=[
                pl.BlockSpec((1,) + started.shape[1:], lambda b, i, v: (b, 0, 0, 0, 0)),
                pl.BlockSpec((1,) + own.shape[1:], lambda b, i, v: (b, 0, 0)),
                pl.BlockSpec(memory_space=pl.ANY),
            ],
            out_specs=pl.BlockSpec(shape, lambda b, i, v: (i[b + first], 0, 0, 0)),
            scratch_shapes=state_scratch(fields, cells, tiles)
            + [
                pltpu.VMEM((count, 6) + arrived.shape[1:], bf16),
                pltpu.SemaphoreType.DMA((count, 6)),
            ],
        ),
        out_shape=jax.ShapeDtypeStruct((per_dev, fields, cells, plane), bf16),
        compiler_params=pltpu.CompilerParams(vmem_limit_bytes=20 << 20),
        name="advance_stay",
    )(ints, vals, in_hbm(started), own, arrived)


def traded_kernel(choices, ints_ref, vals_ref, own_ref, *refs):
    raw_refs, layer_refs, refs = refs[:choices], refs[choices : 2 * choices], refs[2 * choices + 1 :]
    o_ref, sa_ref, sb_ref, e_ref, side_ref, raw_ref, layer_ref, sems = refs
    _, fields, cells, plane = raw_ref.shape
    tiles = plane // LANES
    facts = Facts(ints_ref, vals_ref, 0, 1, fields)
    choice = ints_ref[15]
    for c in range(choices):

        @pl.when(choice == c)
        def _():
            raw_copy = pltpu.make_async_copy(raw_refs[c], raw_ref, sems.at[0])
            layer_copy = pltpu.make_async_copy(layer_refs[c], layer_ref, sems.at[1])
            raw_copy.start()
            layer_copy.start()
            raw_copy.wait()
            layer_copy.wait()

    load_block(raw_ref, sa_ref, cells, tiles)
    place_layers(
        lambda face_no: layer_ref[face_no],
        facts, sa_ref, sb_ref, e_ref, side_ref, None, fields, cells, tiles,
    )
    step = make_step(own_ref[...], facts, e_ref, side_ref, fields, cells, tiles)
    finish = make_finish(o_ref, cells, tiles)

    @pl.when(facts.n == 1)
    def _():
        step(sa_ref, sb_ref)
        finish(sb_ref)

    @pl.when(facts.n > 1)
    def _():
        def two(i, carry):
            step(sa_ref, sb_ref)
            step(sb_ref, sa_ref)
            return carry

        lax.fori_loop(0, facts.n // 2, two, 0)
        finish(sa_ref)


def matrix_kernel(fields, ints_ref, vals_ref, o_ref):
    def write(at, value):
        o_ref[:, at : at + value.shape[1]] = value

    own_matrix(Facts(ints_ref, vals_ref, 0, 1, fields), fields, write)


def traded_matrix(ints, vals, fields):
    shape = (fields * ROWS, 3 * fields * ROWS)
    return pl.pallas_call(
        functools.partial(matrix_kernel, fields),
        grid_spec=pltpu.PrefetchScalarGridSpec(
            num_scalar_prefetch=2,
            grid=(1,),
            in_specs=[],
            out_specs=pl.BlockSpec(shape, lambda b, i, v: (0, 0)),
        ),
        out_shape=jax.ShapeDtypeStruct(shape, bf16),
        name="traded_matrix",
    )(ints, vals)


def advance_traded(ints, vals, own, raws, layers, into):
    per_dev, fields, cells, plane = into.shape
    tiles = plane // LANES
    choices = len(raws)
    size = fields * ROWS
    anywhere = pl.BlockSpec(memory_space=pl.ANY)
    return pl.pallas_call(
        functools.partial(traded_kernel, choices),
        grid_spec=pltpu.PrefetchScalarGridSpec(
            num_scalar_prefetch=2,
            grid=(1,),
            in_specs=[pl.BlockSpec(own.shape, lambda b, i, v: (0, 0))] + [anywhere] * (2 * choices + 1),
            out_specs=pl.BlockSpec((1, fields, cells, plane), lambda b, i, v: (i[14], 0, 0, 0)),
            scratch_shapes=state_scratch(fields, cells, tiles)
            + [
                pltpu.VMEM((1, fields, cells, plane), bf16),
                pltpu.VMEM((6, size, LANES), bf16),
                pltpu.SemaphoreType.DMA((2,)),
            ],
        ),
        out_shape=jax.ShapeDtypeStruct(into.shape, bf16),
        input_output_aliases={3 + 2 * choices: 0},
        compiler_params=pltpu.CompilerParams(vmem_limit_bytes=20 << 20),
        name="advance_traded",
    )(ints, vals, own, *raws, *layers, into)


def plan(wanted, my_index, per_dev):
    peers, requests = wanted.shape
    at = lax.broadcasted_iota(jnp.int32, wanted.shape, 1)
    source_dev = wanted // per_dev
    code = wanted % per_dev * 6 + jnp.bitwise_xor(at % 6, 1)
    key = at * 64 + code
    match = source_dev == my_index
    first = jnp.min(jnp.where(match, key, 64 * requests), axis=1) % 64
    second = jnp.max(jnp.where(match, key, 0), axis=1) % 64
    send = jnp.stack([first, second], axis=1).reshape(2 * peers)
    mine = lax.dynamic_slice_in_dim(wanted, my_index, 1, 0)[0]
    my_source = mine // per_dev
    order = jnp.arange(requests, dtype=jnp.int32)
    repeated = (my_source[:, None] == my_source[None, :]) & (order[None, :] < order[:, None])
    lookup = my_source * 2 + jnp.any(repeated, axis=1).astype(jnp.int32)
    return send, mine, lookup


def local(
    block_state,
    block_level,
    block_velocity,
    diffusivity,
    reaction_matrix,
    ghost_source,
    swap_bit,
    swap_slot,
):
    blocks = block_state[0]
    per_dev, fields, cells, plane = blocks.shape
    peers = lax.axis_size(("gy", "gz"))
    my_index = lax.axis_index(("gy", "gz"))
    levels = block_level[0]
    wanted = ghost_source[0].reshape(peers, per_dev * 6)
    send, mine, lookup = plan(wanted, my_index, per_dev)
    outgoing = pack_faces(blocks, send, 2 * peers)
    arrived = lax.all_to_all(outgoing, ("gy", "gz"), split_axis=0, concat_axis=0, tiled=True)

    own_levels = lax.dynamic_slice_in_dim(levels, my_index * per_dev, per_dev, 0)
    known = mine[:, None] == jnp.arange(levels.shape[0], dtype=jnp.int32)[None, :]
    source_levels = jnp.sum(jnp.where(known, levels[None, :], 0), axis=1)
    coarse = (source_levels.reshape(per_dev, 6) != own_levels[:, None]).astype(jnp.int32)
    bit_here = swap_bit[0, 0, 0]
    slot_here = swap_slot[0, 0, 0]
    rest = jnp.arange(per_dev, dtype=jnp.int32)
    rest = jnp.where(rest == 0, slot_here, rest - (rest <= slot_here))
    ints = jnp.concatenate([rest, own_levels, lookup, coarse.reshape(-1)])
    speeds = block_velocity[0]
    vals = jnp.concatenate([speeds.astype(f32).reshape(-1), diffusivity, reaction_matrix.reshape(-1)])
    pick = lambda x, size: lax.dynamic_slice_in_dim(x.reshape(-1), slot_here * size, size, 0)
    bits = range(lax.axis_size("gx").bit_length() - 1)
    offers = lambda x: [x] + [swapped(x, "gx", bit_no) for bit_no in bits]

    raws = offers(lax.dynamic_slice_in_dim(blocks, slot_here, 1, 0))
    label = jnp.concatenate(
        [pick(own_levels, 1).astype(bf16), pick(coarse, 6).astype(bf16), pick(speeds, 3)]
    )
    label = jnp.broadcast_to(jnp.pad(label, (0, LABEL[1] - label.shape[0]))[None], LABEL)
    label, *others = offers(label)
    for bit_no in bits:
        label = jnp.where(bit_here == bit_no, others[bit_no], label)
    label = label[0]
    traded_ints = jnp.concatenate(
        [
            jnp.zeros((1,), jnp.int32),
            label[0:1].astype(jnp.int32),
            jnp.arange(6, dtype=jnp.int32),
            label[1:7].astype(jnp.int32),
            slot_here[None],
            bit_here[None] + 1,
        ]
    )
    traded_vals = jnp.concatenate([label[7:10].astype(f32), diffusivity, reaction_matrix.reshape(-1)])

    stay = first_substep(ints, vals, blocks, 1, per_dev - 1)
    own = traded_matrix(traded_ints, traded_vals, fields)
    arrived, stay, traded_ints, traded_vals, own = lax.optimization_barrier(
        (arrived, stay, traded_ints, traded_vals, own)
    )
    layers = jnp.take(arrived, pick(lookup, 6), axis=0, mode="clip")
    layers = offers(layers)
    result = advance_stay(ints, vals, *stay, arrived, plane, 1, per_dev)
    raws, layers, result = lax.optimization_barrier((raws, layers, result))
    result = advance_traded(traded_ints, traded_vals, own, raws, layers, result)
    return result[None]


def solution(mesh):
    in_specs = (
        P("gx", ("gy", "gz"), None, None, None),
        P("gx", None),
        P("gx", ("gy", "gz"), None),
        P(),
        P(),
        P("gx", None, None),
        P("gx", "gy", "gz"),
        P("gx", "gy", "gz"),
    )
    out_specs = P("gx", ("gy", "gz"), None, None, None)
    return jax.shard_map(local, mesh=mesh, in_specs=in_specs, out_specs=out_specs, check_vma=False)
```

```python
import functools

import jax
import jax.numpy as jnp
from jax import lax
from jax.experimental import pallas as pl
from jax.experimental.pallas import tpu as pltpu
from jax.sharding import PartitionSpec as P

f32 = jnp.float32
bf16 = jnp.bfloat16
dt_base = 0.05
LANES = 128
ROWS = 8
PAD = 8
LABEL = (16, LANES)


def swapped(x, axis, bit):
    return lax.ppermute(x, axis, [(i, i ^ 1 << bit) for i in range(lax.axis_size(axis))])


def lane_roll(x, shift):
    shift = shift % LANES
    return x if shift == 0 else pltpu.roll(x, shift, x.ndim - 1)


def lane_ids():
    return lax.broadcasted_iota(jnp.int32, (1, ROWS, LANES), 2)


def row_ids():
    return lax.broadcasted_iota(jnp.int32, (1, ROWS, LANES), 1)


def pack_kernel(send_ref, u_ref, o_ref, sel_ref, face_ref):
    blk = pl.program_id(0)
    _, fields, cells, plane = u_ref.shape
    groups = LANES // cells
    tiles = plane // LANES

    @pl.when(blk == 0)
    def _():
        row = lax.broadcasted_iota(jnp.int32, sel_ref.shape, 0)
        col = lax.broadcasted_iota(jnp.int32, sel_ref.shape, 1)
        high = col // LANES
        within = col % LANES
        r = within % cells
        b = within // cells
        source = (tiles * b + r) * cells + high * (cells - 1)
        sel_ref[...] = jnp.where((r < tiles) & (row == source), 1.0, 0.0).astype(bf16)

    lane = lane_ids()
    group = lane // cells
    at_row = row_ids()

    def put(face_no, value):
        face_ref[blk * 6 + face_no] = value.reshape(fields * ROWS, LANES).astype(bf16)

    for face_no, edge in ((0, 0), (1, cells - 1)):
        pieces = [
            u_ref[0, :, edge : edge + 1, pl.ds(LANES * t, LANES)].astype(f32)
            for t in range(tiles)
        ]
        natural = jnp.concatenate(pieces, axis=1)
        total = jnp.zeros((fields, ROWS, LANES), f32)
        for d in range(groups):
            moved = lane_roll(natural, cells * d)
            for b in range(groups):
                for half in range(tiles // groups):
                    r = groups * half + (b - d) % groups
                    t = (tiles // groups) * b + half
                    shift = (r - t) % ROWS
                    here = pltpu.roll(moved, shift, 1) if shift else moved
                    total = jnp.where((group == b) & (at_row == r), here, total)
        put(face_no, total)
    for face_no, tile, source in ((2, 0, 0), (3, tiles - 1, groups - 1)):
        strip = u_ref[0, :, :, pl.ds(LANES * tile, LANES)].astype(f32)
        total = jnp.zeros((fields, ROWS, LANES), f32)
        for b in range(groups):
            moved = lane_roll(strip[:, ROWS * b : ROWS * b + ROWS], cells * (b - source))
            total = jnp.where(group == b, moved, total)
        put(face_no, total)
    picked = jnp.dot(
        u_ref[0].reshape(fields * cells, plane), sel_ref[...], preferred_element_type=f32
    ).reshape(fields, cells, 2 * LANES)
    for face_no, high in ((4, 0), (5, 1)):
        total = jnp.zeros((fields, ROWS, LANES), f32)
        for b in range(groups):
            part = picked[:, ROWS * b : ROWS * b + ROWS, LANES * high : LANES * high + LANES]
            total = total + lane_roll(part, tiles * b)
        put(face_no, total)

    @pl.when(blk == pl.num_programs(0) - 1)
    def _():
        def copy(slot, carry):
            o_ref[slot] = face_ref[send_ref[slot]]
            return carry

        lax.fori_loop(0, o_ref.shape[0], copy, 0)


def in_hbm(x):
    return pltpu.with_memory_space_constraint(x, pltpu.HBM)


def pack_faces(blocks, send, slots):
    per_dev, fields, cells, plane = blocks.shape
    return pl.pallas_call(
        pack_kernel,
        grid_spec=pltpu.PrefetchScalarGridSpec(
            num_scalar_prefetch=1,
            grid=(per_dev,),
            in_specs=[pl.BlockSpec((1, fields, cells, plane), lambda b, s: (b, 0, 0, 0))],
            out_specs=pl.BlockSpec((slots, fields * ROWS, LANES), lambda b, s: (0, 0, 0)),
            scratch_shapes=[
                pltpu.VMEM((plane, 2 * LANES), bf16),
                pltpu.VMEM((per_dev * 6, fields * ROWS, LANES), bf16),
            ],
        ),
        out_shape=jax.ShapeDtypeStruct((slots, fields * ROWS, LANES), bf16),
        compiler_params=pltpu.CompilerParams(vmem_limit_bytes=16 << 20),
        name="pack_faces",
    )(send, in_hbm(blocks))


class Facts:
    def __init__(self, ints_ref, vals_ref, blk, per_dev, fields):
        self.lookup = lambda face: ints_ref[2 * per_dev + blk * 6 + face]
        self.coarse = lambda face: ints_ref[8 * per_dev + blk * 6 + face]
        self.reaction = lambda f, e: vals_ref[3 * per_dev + fields + f * fields + e]
        self.n = jnp.left_shift(jnp.int32(1), ints_ref[per_dev + blk])
        scale = self.n.astype(f32)
        self.dt = dt_base / scale
        adv = self.dt * scale
        dif = self.dt * scale * scale
        velocity = [vals_ref[blk * 3 + d] for d in range(3)]
        self.minus = [adv * jnp.maximum(v, 0.0) for v in velocity]
        self.plus = [-(adv * jnp.minimum(v, 0.0)) for v in velocity]
        self.rates = [dif * vals_ref[3 * per_dev + f] for f in range(fields)]


def own_matrix(facts, fields, write):
    outflow = sum(facts.minus) + sum(facts.plus)
    size = fields * ROWS
    ri = lax.broadcasted_iota(jnp.int32, (size, size), 0)
    ci = lax.broadcasted_iota(jnp.int32, (size, size), 1)
    matrix = jnp.zeros((size, size), f32)
    for f in range(fields):
        line = jnp.zeros((size, size), f32)
        for e in range(fields):
            term = facts.dt * facts.reaction(f, e)
            if e == f:
                term = term - (6.0 * facts.rates[f] + outflow)
            line = jnp.where(ci // ROWS == e, term, line)
        matrix = jnp.where(ri // ROWS == f, line, matrix)
    matrix = jnp.where(ri % ROWS == ci % ROWS, matrix, 0.0)
    high = matrix.astype(bf16)
    write(0, high)
    write(size, (matrix - high.astype(f32)).astype(bf16))
    write(2 * size, high)


def to_planes(load, state, cells, tiles):
    groups = LANES // cells
    group = lane_ids() // cells
    for it in range(cells // ROWS):
        for half in range(tiles // groups):
            source = [load((tiles // groups) * b + half, it) for b in range(groups)]
            shifted = []
            for d in range(groups):
                x = source[d % groups]
                for g in range(1, groups):
                    x = jnp.where(group == g, source[(g + d) % groups], x)
                shifted.append(lane_roll(x, cells * d))
            for jj in range(groups):
                out = shifted[(0 - jj) % groups]
                for b in range(1, groups):
                    out = jnp.where(group == b, shifted[(b - jj) % groups], out)
                state[:, groups * half + jj + 1, pl.ds(PAD + ROWS * it, ROWS), :] = out


def from_planes(state, store, cells, tiles):
    groups = LANES // cells
    group = lane_ids() // cells
    for it in range(cells // 16):
        for half in range(tiles // groups):
            outs = [[] for _ in range(groups)]
            for sub in range(2):
                rows = pl.ds(PAD + 16 * it + ROWS * sub, ROWS)
                source = [state[:, groups * half + jj + 1, rows, :] for jj in range(groups)]
                shifted = []
                for d in range(groups):
                    x = source[(0 - d) % groups]
                    for g in range(1, groups):
                        x = jnp.where(group == g, source[(g - d) % groups], x)
                    shifted.append(lane_roll(x, -cells * d))
                for b in range(groups):
                    out = shifted[b % groups]
                    for jj in range(1, groups):
                        out = jnp.where(group == jj, shifted[(b - jj) % groups], out)
                    outs[b].append(out)
            for b in range(groups):
                both = jnp.concatenate(outs[b], axis=1).astype(bf16)
                store((tiles // groups) * b + half, it, both)


def wrap_planes(state, side_ref, cells, tiles):
    lane = lane_ids()
    for it in range(cells // ROWS):
        rows = pl.ds(PAD + ROWS * it, ROWS)
        side = 0.0 if side_ref is None else side_ref[:, pl.ds(ROWS * it, ROWS), :]
        state[:, 0, rows, :] = jnp.where(lane < cells, side, lane_roll(state[:, tiles, rows, :], cells))
        state[:, tiles + 1, rows, :] = jnp.where(
            lane >= LANES - cells, side, lane_roll(state[:, 1, rows, :], -cells)
        )


def substep(src, put, edge_ref, own, facts, fields, cells, tiles):
    lane = lax.broadcasted_iota(jnp.int32, (ROWS, LANES), 1)
    k_first = lane % cells == 0
    k_last = lane % cells == cells - 1
    minus, plus, rates = facts.minus, facts.plus, facts.rates

    def two_tiles(pair, carry):
        for it in range(cells // ROWS):
            row = PAD + ROWS * it
            centre = [
                [src[f, 2 * pair + 1 + q, pl.ds(row, ROWS), :] for f in range(fields)]
                for q in range(2)
            ]
            both = jnp.concatenate([jnp.concatenate(c, axis=0) for c in centre], axis=1)
            both_high = both.astype(bf16)
            both_low = (both - both_high.astype(f32)).astype(bf16)
            stacked = jnp.concatenate([both_high, both_high, both_low], axis=0)
            mixed = jnp.dot(own, stacked, preferred_element_type=f32)
            for q in range(2):
                t = 2 * pair + q
                for f in range(fields):
                    c = centre[q][f]
                    minus_x = src[f, t + 1, pl.ds(row - 1, ROWS), :]
                    plus_x = src[f, t + 1, pl.ds(row + 1, ROWS), :]
                    minus_y = src[f, t, pl.ds(row, ROWS), :]
                    plus_y = src[f, t + 2, pl.ds(row, ROWS), :]
                    edge = 0.0 if edge_ref is None else edge_ref[f, t, pl.ds(ROWS * it, ROWS), :]
                    minus_z = jnp.where(k_first, edge, lane_roll(c, 1))
                    plus_z = jnp.where(k_last, edge, lane_roll(c, -1))
                    near = (rates[f] + minus[0]) * minus_x + (rates[f] + plus[0]) * plus_x
                    near += (rates[f] + minus[1]) * minus_y + (rates[f] + plus[1]) * plus_y
                    near += (rates[f] + minus[2]) * minus_z + (rates[f] + plus[2]) * plus_z
                    own_terms = mixed[ROWS * f : ROWS * f + ROWS, LANES * q : LANES * q + LANES]
                    put(f, t, it, near + (c + own_terms))
        return carry

    lax.fori_loop(0, tiles // 2, two_tiles, 0, unroll=2)


def first_kernel(first, per_dev, ints_ref, vals_ref, u_ref, o_ref, rk_out_ref, sa_ref):
    _, fields, cells, plane = u_ref.shape
    tiles = plane // LANES
    facts = Facts(ints_ref, vals_ref, ints_ref[pl.program_id(0) + first], per_dev, fields)

    @pl.when(pl.program_id(0) == 0)
    def _():
        sa_ref[:, :, 0:PAD] = jnp.zeros((fields, tiles + 2, PAD, LANES), f32)
        sa_ref[:, :, PAD + cells :] = jnp.zeros((fields, tiles + 2, PAD, LANES), f32)

    load_block(u_ref, sa_ref, cells, tiles)
    wrap_planes(sa_ref, None, cells, tiles)

    def write(at, value):
        rk_out_ref[0, :, at : at + value.shape[1]] = value

    own_matrix(facts, fields, write)

    def put(f, t, it, value):
        o_ref[0, f, t, pl.ds(ROWS * it, ROWS), :] = value

    substep(sa_ref, put, None, rk_out_ref[0], facts, fields, cells, tiles)


def load_block(u_ref, state, cells, tiles):
    whole = {}

    def load(t, it):
        if (t, it // 2) not in whole:
            whole[t, it // 2] = u_ref[
                0, :, pl.ds(16 * (it // 2), 16), pl.ds(LANES * t, LANES)
            ].astype(f32)
        return whole[t, it // 2][:, ROWS * (it % 2) : ROWS * (it % 2) + ROWS]

    to_planes(load, state, cells, tiles)


def first_substep(ints, vals, blocks, first, count):
    per_dev, fields, cells, plane = blocks.shape
    tiles = plane // LANES
    size = fields * ROWS
    return pl.pallas_call(
        functools.partial(first_kernel, first, per_dev),
        grid_spec=pltpu.PrefetchScalarGridSpec(
            num_scalar_prefetch=2,
            grid=(count,),
            in_specs=[
                pl.BlockSpec((1, fields, cells, plane), lambda b, i, v: (i[b + first], 0, 0, 0))
            ],
            out_specs=[
                pl.BlockSpec((1, fields, tiles, cells, LANES), lambda b, i, v: (b, 0, 0, 0, 0)),
                pl.BlockSpec((1, size, 3 * size), lambda b, i, v: (b, 0, 0)),
            ],
            scratch_shapes=[pltpu.VMEM((fields, tiles + 2, cells + 2 * PAD, LANES), f32)],
        ),
        out_shape=[
            pltpu.HBM((count, fields, tiles, cells, LANES), f32),
            jax.ShapeDtypeStruct((count, size, 3 * size), bf16),
        ],
        compiler_params=pltpu.CompilerParams(vmem_limit_bytes=16 << 20),
        name="first_substep",
    )(ints, vals, in_hbm(blocks))


def place_layers(layer_of, facts, sa_ref, sb_ref, e_ref, side_ref, s_ref, fields, cells, tiles):
    groups = LANES // cells
    lane = lane_ids()
    at_row = row_ids()
    k_first = lane % cells == 0
    k_last = lane % cells == cells - 1
    minus, plus = facts.minus, facts.plus
    odd_lane = lane % 2 == 1
    odd_row = at_row % 2 == 1

    def face(face_no):
        layer = layer_of(face_no).astype(f32).reshape(fields, ROWS, LANES)
        mean = layer + jnp.where(odd_lane, lane_roll(layer, 1), lane_roll(layer, -1))
        mean = mean + jnp.where(odd_row, pltpu.roll(mean, 1, 1), pltpu.roll(mean, ROWS - 1, 1))
        return jnp.where(facts.coarse(face_no) > 0, mean * 0.25, layer)

    states = (sa_ref, sb_ref)
    rate = jnp.concatenate([jnp.full((1, ROWS, LANES), x, f32) for x in facts.rates], axis=0)

    low, high = face(4), lane_roll(face(5), cells - 1)
    weight = jnp.where(k_first, rate + minus[2], jnp.where(k_last, rate + plus[2], 0.0))
    for it in range(cells // ROWS):
        rows = pl.ds(ROWS * it, ROWS)
        for t in range(tiles):
            at = tiles * it + t
            edge = lane_roll(jnp.where(lane % cells == at, low, high), -at)
            e_ref[:, t, rows, :] = edge
            if s_ref is not None:
                sa_ref[:, t + 1, pl.ds(PAD + ROWS * it, ROWS), :] = (
                    s_ref[0, :, t, rows, :] + weight * edge
                )

    low, high = face(2), face(3)
    for it in range(cells // ROWS):
        rows = pl.ds(PAD + ROWS * it, ROWS)
        side = jnp.where(
            lane < cells,
            lane_roll(low, -cells * it),
            lane_roll(high, cells * (groups - 1 - it)),
        )
        side_ref[:, pl.ds(ROWS * it, ROWS), :] = side
        if s_ref is not None:
            sa_ref[:, 1, rows, :] += jnp.where(lane < cells, (rate + minus[1]) * side, 0.0)
            sa_ref[:, tiles, rows, :] += jnp.where(
                lane >= LANES - cells, (rate + plus[1]) * side, 0.0
            )

    low, high = face(0), face(1)
    low_part = (rate + minus[0]) * low
    high_part = (rate + plus[0]) * high
    for t in range(tiles):
        if s_ref is not None:
            sa_ref[:, t + 1, PAD : PAD + 1, :] += low_part[:, t : t + 1, :]
            sa_ref[:, t + 1, PAD + cells - 1 : PAD + cells, :] += high_part[:, t : t + 1, :]
        for state in states:
            state[:, t + 1, PAD - 1 : PAD, :] = low[:, t : t + 1, :]
            state[:, t + 1, PAD + cells : PAD + cells + 1, :] = high[:, t : t + 1, :]
    wrap_planes(sa_ref, side_ref, cells, tiles)


def make_step(own, facts, e_ref, side_ref, fields, cells, tiles):
    def step(src, dst):
        def put(f, t, it, value):
            dst[f, t + 1, pl.ds(PAD + ROWS * it, ROWS), :] = value

        substep(src, put, e_ref, own, facts, fields, cells, tiles)
        wrap_planes(dst, side_ref, cells, tiles)

    return step


def make_finish(o_ref, cells, tiles):
    def finish(src):
        def store(t, it, value):
            o_ref[0, :, pl.ds(16 * it, 16), pl.ds(LANES * t, LANES)] = value

        from_planes(src, store, cells, tiles)

    return finish


def stay_kernel(first, per_dev, ints_ref, vals_ref, s_ref, rk_ref, arr_ref, o_ref, sa_ref, sb_ref, e_ref, side_ref):
    _, fields, tiles, cells, _ = s_ref.shape
    facts = Facts(ints_ref, vals_ref, ints_ref[pl.program_id(0) + first], per_dev, fields)
    place_layers(
        lambda face_no: arr_ref[facts.lookup(face_no)],
        facts, sa_ref, sb_ref, e_ref, side_ref, s_ref, fields, cells, tiles,
    )
    step = make_step(rk_ref[0], facts, e_ref, side_ref, fields, cells, tiles)
    finish = make_finish(o_ref, cells, tiles)

    @pl.when(facts.n == 1)
    def _():
        finish(sa_ref)

    @pl.when(facts.n > 1)
    def _():
        def two(i, carry):
            step(sa_ref, sb_ref)
            step(sb_ref, sa_ref)
            return carry

        lax.fori_loop(0, (facts.n - 2) // 2, two, 0)
        step(sa_ref, sb_ref)
        finish(sb_ref)


def state_scratch(fields, cells, tiles):
    padded = (fields, tiles + 2, cells + 2 * PAD, LANES)
    return [
        pltpu.VMEM(padded, f32),
        pltpu.VMEM(padded, f32),
        pltpu.VMEM((fields, tiles, cells, LANES), f32),
        pltpu.VMEM((fields, cells, LANES), f32),
    ]


def advance_stay(ints, vals, started, own, arrived, plane, first, per_dev):
    count, fields, tiles, cells, _ = started.shape
    shape = (1, fields, cells, plane)
    return pl.pallas_call(
        functools.partial(stay_kernel, first, per_dev),
        grid_spec=pltpu.PrefetchScalarGridSpec(
            num_scalar_prefetch=2,
            grid=(count,),
            in_specs=[
                pl.BlockSpec((1,) + started.shape[1:], lambda b, i, v: (b, 0, 0, 0, 0)),
                pl.BlockSpec((1,) + own.shape[1:], lambda b, i, v: (b, 0, 0)),
                pl.BlockSpec(arrived.shape, lambda b, i, v: (0, 0, 0)),
            ],
            out_specs=pl.BlockSpec(shape, lambda b, i, v: (i[b + first], 0, 0, 0)),
            scratch_shapes=state_scratch(fields, cells, tiles),
        ),
        out_shape=jax.ShapeDtypeStruct((per_dev, fields, cells, plane), bf16),
        compiler_params=pltpu.CompilerParams(vmem_limit_bytes=20 << 20),
        name="advance_stay",
    )(ints, vals, in_hbm(started), own, arrived)


def traded_kernel(choices, ints_ref, vals_ref, *refs):
    raw_refs, layer_refs, refs = refs[:choices], refs[choices : 2 * choices], refs[2 * choices + 1 :]
    o_ref, sa_ref, sb_ref, e_ref, side_ref, rk_ref, raw_ref, layer_ref, sems = refs
    _, fields, cells, plane = raw_ref.shape
    tiles = plane // LANES
    facts = Facts(ints_ref, vals_ref, 0, 1, fields)
    choice = ints_ref[15]
    for c in range(choices):

        @pl.when(choice == c)
        def _():
            raw_copy = pltpu.make_async_copy(raw_refs[c], raw_ref, sems.at[0])
            layer_copy = pltpu.make_async_copy(layer_refs[c], layer_ref, sems.at[1])
            raw_copy.start()
            layer_copy.start()
            raw_copy.wait()
            layer_copy.wait()

    def write(at, value):
        rk_ref[:, at : at + value.shape[1]] = value

    own_matrix(facts, fields, write)
    load_block(raw_ref, sa_ref, cells, tiles)
    place_layers(
        lambda face_no: layer_ref[face_no],
        facts, sa_ref, sb_ref, e_ref, side_ref, None, fields, cells, tiles,
    )
    step = make_step(rk_ref[...], facts, e_ref, side_ref, fields, cells, tiles)
    finish = make_finish(o_ref, cells, tiles)

    @pl.when(facts.n == 1)
    def _():
        step(sa_ref, sb_ref)
        finish(sb_ref)

    @pl.when(facts.n > 1)
    def _():
        def two(i, carry):
            step(sa_ref, sb_ref)
            step(sb_ref, sa_ref)
            return carry

        lax.fori_loop(0, facts.n // 2, two, 0)
        finish(sa_ref)


def advance_traded(ints, vals, raws, layers, into):
    per_dev, fields, cells, plane = into.shape
    tiles = plane // LANES
    choices = len(raws)
    size = fields * ROWS
    anywhere = pl.BlockSpec(memory_space=pl.ANY)
    return pl.pallas_call(
        functools.partial(traded_kernel, choices),
        grid_spec=pltpu.PrefetchScalarGridSpec(
            num_scalar_prefetch=2,
            grid=(1,),
            in_specs=[anywhere] * (2 * choices + 1),
            out_specs=pl.BlockSpec((1, fields, cells, plane), lambda b, i, v: (i[14], 0, 0, 0)),
            scratch_shapes=state_scratch(fields, cells, tiles)
            + [
                pltpu.VMEM((size, 3 * size), bf16),
                pltpu.VMEM((1, fields, cells, plane), bf16),
                pltpu.VMEM((6, size, LANES), bf16),
                pltpu.SemaphoreType.DMA((2,)),
            ],
        ),
        out_shape=jax.ShapeDtypeStruct(into.shape, bf16),
        input_output_aliases={2 + 2 * choices: 0},
        compiler_params=pltpu.CompilerParams(vmem_limit_bytes=20 << 20),
        name="advance_traded",
    )(ints, vals, *raws, *layers, into)


def plan(wanted, my_index, per_dev):
    peers, requests = wanted.shape
    at = lax.broadcasted_iota(jnp.int32, wanted.shape, 1)
    source_dev = wanted // per_dev
    code = wanted % per_dev * 6 + jnp.bitwise_xor(at % 6, 1)
    key = at * 64 + code
    match = source_dev == my_index
    first = jnp.min(jnp.where(match, key, 64 * requests), axis=1) % 64
    second = jnp.max(jnp.where(match, key, 0), axis=1) % 64
    send = jnp.stack([first, second], axis=1).reshape(2 * peers)
    mine = lax.dynamic_slice_in_dim(wanted, my_index, 1, 0)[0]
    my_source = mine // per_dev
    order = jnp.arange(requests, dtype=jnp.int32)
    repeated = (my_source[:, None] == my_source[None, :]) & (order[None, :] < order[:, None])
    lookup = my_source * 2 + jnp.any(repeated, axis=1).astype(jnp.int32)
    return send, mine, lookup


def local(
    block_state,
    block_level,
    block_velocity,
    diffusivity,
    reaction_matrix,
    ghost_source,
    swap_bit,
    swap_slot,
):
    blocks = block_state[0]
    per_dev, fields, cells, plane = blocks.shape
    peers = lax.axis_size(("gy", "gz"))
    my_index = lax.axis_index(("gy", "gz"))
    levels = block_level[0]
    wanted = ghost_source[0].reshape(peers, per_dev * 6)
    send, mine, lookup = plan(wanted, my_index, per_dev)
    outgoing = pack_faces(blocks, send, 2 * peers)
    arrived = lax.all_to_all(outgoing, ("gy", "gz"), split_axis=0, concat_axis=0, tiled=True)

    own_levels = lax.dynamic_slice_in_dim(levels, my_index * per_dev, per_dev, 0)
    known = mine[:, None] == jnp.arange(levels.shape[0], dtype=jnp.int32)[None, :]
    source_levels = jnp.sum(jnp.where(known, levels[None, :], 0), axis=1)
    coarse = (source_levels.reshape(per_dev, 6) != own_levels[:, None]).astype(jnp.int32)
    bit_here = swap_bit[0, 0, 0]
    slot_here = swap_slot[0, 0, 0]
    rest = jnp.arange(per_dev, dtype=jnp.int32)
    rest = jnp.where(rest == 0, slot_here, rest - (rest <= slot_here))
    ints = jnp.concatenate([rest, own_levels, lookup, coarse.reshape(-1)])
    speeds = block_velocity[0]
    vals = jnp.concatenate([speeds.astype(f32).reshape(-1), diffusivity, reaction_matrix.reshape(-1)])
    pick = lambda x, size: lax.dynamic_slice_in_dim(x.reshape(-1), slot_here * size, size, 0)
    bits = range(lax.axis_size("gx").bit_length() - 1)
    offers = lambda x: [x] + [swapped(x, "gx", bit_no) for bit_no in bits]

    raws = offers(lax.dynamic_slice_in_dim(blocks, slot_here, 1, 0))
    label = jnp.concatenate(
        [pick(own_levels, 1).astype(bf16), pick(coarse, 6).astype(bf16), pick(speeds, 3)]
    )
    label = jnp.broadcast_to(jnp.pad(label, (0, LABEL[1] - label.shape[0]))[None], LABEL)
    label, *others = offers(label)
    for bit_no in bits:
        label = jnp.where(bit_here == bit_no, others[bit_no], label)
    label = label[0]
    traded_ints = jnp.concatenate(
        [
            jnp.zeros((1,), jnp.int32),
            label[0:1].astype(jnp.int32),
            jnp.arange(6, dtype=jnp.int32),
            label[1:7].astype(jnp.int32),
            slot_here[None],
            bit_here[None] + 1,
        ]
    )
    traded_vals = jnp.concatenate([label[7:10].astype(f32), diffusivity, reaction_matrix.reshape(-1)])

    stay = first_substep(ints, vals, blocks, 1, per_dev - 1)
    arrived, stay, traded_ints, traded_vals = lax.optimization_barrier(
        (arrived, stay, traded_ints, traded_vals)
    )
    layers = offers(jnp.take(arrived, pick(lookup, 6), axis=0, mode="clip"))
    result = advance_stay(ints, vals, *stay, arrived, plane, 1, per_dev)
    raws, layers, result = lax.optimization_barrier((raws, layers, result))
    result = advance_traded(traded_ints, traded_vals, raws, layers, result)
    return result[None]


def solution(mesh):
    in_specs = (
        P("gx", ("gy", "gz"), None, None, None),
        P("gx", None),
        P("gx", ("gy", "gz"), None),
        P(),
        P(),
        P("gx", None, None),
        P("gx", "gy", "gz"),
        P("gx", "gy", "gz"),
    )
    out_specs = P("gx", ("gy", "gz"), None, None, None)
    return jax.shard_map(local, mesh=mesh, in_specs=in_specs, out_specs=out_specs, check_vma=False)
```

```python
import functools

import jax
import jax.numpy as jnp
from jax import lax
from jax.experimental import pallas as pl
from jax.experimental.pallas import tpu as pltpu
from jax.sharding import PartitionSpec as P

f32 = jnp.float32
bf16 = jnp.bfloat16
dt_base = 0.05
LANES = 128
ROWS = 8
PAD = 8
LABEL = (16, LANES)


def swapped(x, axis, bit):
    return lax.ppermute(x, axis, [(i, i ^ 1 << bit) for i in range(lax.axis_size(axis))])


def lane_roll(x, shift):
    shift = shift % LANES
    return x if shift == 0 else pltpu.roll(x, shift, x.ndim - 1)


def lane_ids():
    return lax.broadcasted_iota(jnp.int32, (1, ROWS, LANES), 2)


def row_ids():
    return lax.broadcasted_iota(jnp.int32, (1, ROWS, LANES), 1)


def pack_kernel(send_ref, u_ref, o_ref, sel_ref, face_ref):
    blk = pl.program_id(0)
    _, fields, cells, plane = u_ref.shape
    groups = LANES // cells
    tiles = plane // LANES

    @pl.when(blk == 0)
    def _():
        row = lax.broadcasted_iota(jnp.int32, sel_ref.shape, 0)
        col = lax.broadcasted_iota(jnp.int32, sel_ref.shape, 1)
        high = col // LANES
        within = col % LANES
        r = within % cells
        b = within // cells
        source = (tiles * b + r) * cells + high * (cells - 1)
        sel_ref[...] = jnp.where((r < tiles) & (row == source), 1.0, 0.0).astype(bf16)

    lane = lane_ids()
    group = lane // cells
    at_row = row_ids()

    def put(face_no, value):
        face_ref[blk * 6 + face_no] = value.reshape(fields * ROWS, LANES).astype(bf16)

    for face_no, edge in ((0, 0), (1, cells - 1)):
        pieces = [
            u_ref[0, :, edge : edge + 1, pl.ds(LANES * t, LANES)].astype(f32)
            for t in range(tiles)
        ]
        natural = jnp.concatenate(pieces, axis=1)
        total = jnp.zeros((fields, ROWS, LANES), f32)
        for d in range(groups):
            moved = lane_roll(natural, cells * d)
            for b in range(groups):
                for half in range(tiles // groups):
                    r = groups * half + (b - d) % groups
                    t = (tiles // groups) * b + half
                    shift = (r - t) % ROWS
                    here = pltpu.roll(moved, shift, 1) if shift else moved
                    total = jnp.where((group == b) & (at_row == r), here, total)
        put(face_no, total)
    for face_no, tile, source in ((2, 0, 0), (3, tiles - 1, groups - 1)):
        strip = u_ref[0, :, :, pl.ds(LANES * tile, LANES)].astype(f32)
        total = jnp.zeros((fields, ROWS, LANES), f32)
        for b in range(groups):
            moved = lane_roll(strip[:, ROWS * b : ROWS * b + ROWS], cells * (b - source))
            total = jnp.where(group == b, moved, total)
        put(face_no, total)
    picked = jnp.dot(
        u_ref[0].reshape(fields * cells, plane), sel_ref[...], preferred_element_type=f32
    ).reshape(fields, cells, 2 * LANES)
    for face_no, high in ((4, 0), (5, 1)):
        total = jnp.zeros((fields, ROWS, LANES), f32)
        for b in range(groups):
            part = picked[:, ROWS * b : ROWS * b + ROWS, LANES * high : LANES * high + LANES]
            total = total + lane_roll(part, tiles * b)
        put(face_no, total)

    @pl.when(blk == pl.num_programs(0) - 1)
    def _():
        def copy(slot, carry):
            o_ref[slot] = face_ref[send_ref[slot]]
            return carry

        lax.fori_loop(0, o_ref.shape[0], copy, 0)


def in_hbm(x):
    return pltpu.with_memory_space_constraint(x, pltpu.HBM)


def pack_faces(blocks, send, slots):
    per_dev, fields, cells, plane = blocks.shape
    return pl.pallas_call(
        pack_kernel,
        grid_spec=pltpu.PrefetchScalarGridSpec(
            num_scalar_prefetch=1,
            grid=(per_dev,),
            in_specs=[pl.BlockSpec((1, fields, cells, plane), lambda b, s: (b, 0, 0, 0))],
            out_specs=pl.BlockSpec((slots, fields * ROWS, LANES), lambda b, s: (0, 0, 0)),
            scratch_shapes=[
                pltpu.VMEM((plane, 2 * LANES), bf16),
                pltpu.VMEM((per_dev * 6, fields * ROWS, LANES), bf16),
            ],
        ),
        out_shape=jax.ShapeDtypeStruct((slots, fields * ROWS, LANES), bf16),
        compiler_params=pltpu.CompilerParams(vmem_limit_bytes=16 << 20),
        name="pack_faces",
    )(send, in_hbm(blocks))


class Facts:
    def __init__(self, ints_ref, vals_ref, blk, per_dev, fields):
        self.lookup = lambda face: ints_ref[2 * per_dev + blk * 6 + face]
        self.coarse = lambda face: ints_ref[8 * per_dev + blk * 6 + face]
        self.reaction = lambda f, e: vals_ref[3 * per_dev + fields + f * fields + e]
        self.n = jnp.left_shift(jnp.int32(1), ints_ref[per_dev + blk])
        scale = self.n.astype(f32)
        self.dt = dt_base / scale
        adv = self.dt * scale
        dif = self.dt * scale * scale
        velocity = [vals_ref[blk * 3 + d] for d in range(3)]
        self.minus = [adv * jnp.maximum(v, 0.0) for v in velocity]
        self.plus = [-(adv * jnp.minimum(v, 0.0)) for v in velocity]
        self.rates = [dif * vals_ref[3 * per_dev + f] for f in range(fields)]


def own_matrix(facts, fields, write):
    outflow = sum(facts.minus) + sum(facts.plus)
    size = fields * ROWS
    ri = lax.broadcasted_iota(jnp.int32, (size, size), 0)
    ci = lax.broadcasted_iota(jnp.int32, (size, size), 1)
    matrix = jnp.zeros((size, size), f32)
    for f in range(fields):
        line = jnp.zeros((size, size), f32)
        for e in range(fields):
            term = facts.dt * facts.reaction(f, e)
            if e == f:
                term = term - (6.0 * facts.rates[f] + outflow)
            line = jnp.where(ci // ROWS == e, term, line)
        matrix = jnp.where(ri // ROWS == f, line, matrix)
    matrix = jnp.where(ri % ROWS == ci % ROWS, matrix, 0.0)
    high = matrix.astype(bf16)
    write(0, high)
    write(size, (matrix - high.astype(f32)).astype(bf16))
    write(2 * size, high)


def to_planes(load, state, cells, tiles):
    groups = LANES // cells
    group = lane_ids() // cells
    for it in range(cells // ROWS):
        for half in range(tiles // groups):
            source = [load((tiles // groups) * b + half, it) for b in range(groups)]
            shifted = []
            for d in range(groups):
                x = source[d % groups]
                for g in range(1, groups):
                    x = jnp.where(group == g, source[(g + d) % groups], x)
                shifted.append(lane_roll(x, cells * d))
            for jj in range(groups):
                out = shifted[(0 - jj) % groups]
                for b in range(1, groups):
                    out = jnp.where(group == b, shifted[(b - jj) % groups], out)
                state[:, groups * half + jj + 1, pl.ds(PAD + ROWS * it, ROWS), :] = out


def from_planes(state, store, cells, tiles):
    groups = LANES // cells
    group = lane_ids() // cells
    for it in range(cells // 16):
        for half in range(tiles // groups):
            outs = [[] for _ in range(groups)]
            for sub in range(2):
                rows = pl.ds(PAD + 16 * it + ROWS * sub, ROWS)
                source = [state[:, groups * half + jj + 1, rows, :] for jj in range(groups)]
                shifted = []
                for d in range(groups):
                    x = source[(0 - d) % groups]
                    for g in range(1, groups):
                        x = jnp.where(group == g, source[(g - d) % groups], x)
                    shifted.append(lane_roll(x, -cells * d))
                for b in range(groups):
                    out = shifted[b % groups]
                    for jj in range(1, groups):
                        out = jnp.where(group == jj, shifted[(b - jj) % groups], out)
                    outs[b].append(out)
            for b in range(groups):
                both = jnp.concatenate(outs[b], axis=1).astype(bf16)
                store((tiles // groups) * b + half, it, both)


def wrap_planes(state, side_ref, cells, tiles):
    lane = lane_ids()
    for it in range(cells // ROWS):
        rows = pl.ds(PAD + ROWS * it, ROWS)
        side = 0.0 if side_ref is None else side_ref[:, pl.ds(ROWS * it, ROWS), :]
        state[:, 0, rows, :] = jnp.where(lane < cells, side, lane_roll(state[:, tiles, rows, :], cells))
        state[:, tiles + 1, rows, :] = jnp.where(
            lane >= LANES - cells, side, lane_roll(state[:, 1, rows, :], -cells)
        )


def substep(src, put, edge_ref, own, facts, fields, cells, tiles):
    lane = lax.broadcasted_iota(jnp.int32, (ROWS, LANES), 1)
    k_first = lane % cells == 0
    k_last = lane % cells == cells - 1
    minus, plus, rates = facts.minus, facts.plus, facts.rates

    def two_tiles(pair, carry):
        for it in range(cells // ROWS):
            row = PAD + ROWS * it
            centre = [
                [src[f, 2 * pair + 1 + q, pl.ds(row, ROWS), :] for f in range(fields)]
                for q in range(2)
            ]
            both = jnp.concatenate([jnp.concatenate(c, axis=0) for c in centre], axis=1)
            both_high = both.astype(bf16)
            both_low = (both - both_high.astype(f32)).astype(bf16)
            stacked = jnp.concatenate([both_high, both_high, both_low], axis=0)
            mixed = jnp.dot(own, stacked, preferred_element_type=f32)
            for q in range(2):
                t = 2 * pair + q
                for f in range(fields):
                    c = centre[q][f]
                    minus_x = src[f, t + 1, pl.ds(row - 1, ROWS), :]
                    plus_x = src[f, t + 1, pl.ds(row + 1, ROWS), :]
                    minus_y = src[f, t, pl.ds(row, ROWS), :]
                    plus_y = src[f, t + 2, pl.ds(row, ROWS), :]
                    edge = 0.0 if edge_ref is None else edge_ref[f, t, pl.ds(ROWS * it, ROWS), :]
                    minus_z = jnp.where(k_first, edge, lane_roll(c, 1))
                    plus_z = jnp.where(k_last, edge, lane_roll(c, -1))
                    near = (rates[f] + minus[0]) * minus_x + (rates[f] + plus[0]) * plus_x
                    near += (rates[f] + minus[1]) * minus_y + (rates[f] + plus[1]) * plus_y
                    near += (rates[f] + minus[2]) * minus_z + (rates[f] + plus[2]) * plus_z
                    own_terms = mixed[ROWS * f : ROWS * f + ROWS, LANES * q : LANES * q + LANES]
                    put(f, t, it, near + (c + own_terms))
        return carry

    lax.fori_loop(0, tiles // 2, two_tiles, 0, unroll=4)


def first_kernel(first, per_dev, ints_ref, vals_ref, u_ref, o_ref, rk_out_ref, sa_ref):
    _, fields, cells, plane = u_ref.shape
    tiles = plane // LANES
    facts = Facts(ints_ref, vals_ref, ints_ref[pl.program_id(0) + first], per_dev, fields)

    @pl.when(pl.program_id(0) == 0)
    def _():
        sa_ref[:, :, 0:PAD] = jnp.zeros((fields, tiles + 2, PAD, LANES), f32)
        sa_ref[:, :, PAD + cells :] = jnp.zeros((fields, tiles + 2, PAD, LANES), f32)

    load_block(u_ref, sa_ref, cells, tiles)
    wrap_planes(sa_ref, None, cells, tiles)

    def write(at, value):
        rk_out_ref[0, :, at : at + value.shape[1]] = value

    own_matrix(facts, fields, write)

    def put(f, t, it, value):
        o_ref[0, f, t, pl.ds(ROWS * it, ROWS), :] = value

    substep(sa_ref, put, None, rk_out_ref[0], facts, fields, cells, tiles)


def load_block(u_ref, state, cells, tiles):
    whole = {}

    def load(t, it):
        if (t, it // 2) not in whole:
            whole[t, it // 2] = u_ref[
                0, :, pl.ds(16 * (it // 2), 16), pl.ds(LANES * t, LANES)
            ].astype(f32)
        return whole[t, it // 2][:, ROWS * (it % 2) : ROWS * (it % 2) + ROWS]

    to_planes(load, state, cells, tiles)


def first_substep(ints, vals, blocks, first, count):
    per_dev, fields, cells, plane = blocks.shape
    tiles = plane // LANES
    size = fields * ROWS
    return pl.pallas_call(
        functools.partial(first_kernel, first, per_dev),
        grid_spec=pltpu.PrefetchScalarGridSpec(
            num_scalar_prefetch=2,
            grid=(count,),
            in_specs=[
                pl.BlockSpec((1, fields, cells, plane), lambda b, i, v: (i[b + first], 0, 0, 0))
            ],
            out_specs=[
                pl.BlockSpec((1, fields, tiles, cells, LANES), lambda b, i, v: (b, 0, 0, 0, 0)),
                pl.BlockSpec((1, size, 3 * size), lambda b, i, v: (b, 0, 0)),
            ],
            scratch_shapes=[pltpu.VMEM((fields, tiles + 2, cells + 2 * PAD, LANES), f32)],
        ),
        out_shape=[
            pltpu.HBM((count, fields, tiles, cells, LANES), f32),
            jax.ShapeDtypeStruct((count, size, 3 * size), bf16),
        ],
        compiler_params=pltpu.CompilerParams(vmem_limit_bytes=16 << 20),
        name="first_substep",
    )(ints, vals, in_hbm(blocks))


def place_layers(layer_of, facts, sa_ref, sb_ref, e_ref, side_ref, s_ref, fields, cells, tiles):
    groups = LANES // cells
    lane = lane_ids()
    at_row = row_ids()
    k_first = lane % cells == 0
    k_last = lane % cells == cells - 1
    minus, plus = facts.minus, facts.plus
    odd_lane = lane % 2 == 1
    odd_row = at_row % 2 == 1

    def face(face_no):
        layer = layer_of(face_no).astype(f32).reshape(fields, ROWS, LANES)
        mean = layer + jnp.where(odd_lane, lane_roll(layer, 1), lane_roll(layer, -1))
        mean = mean + jnp.where(odd_row, pltpu.roll(mean, 1, 1), pltpu.roll(mean, ROWS - 1, 1))
        return jnp.where(facts.coarse(face_no) > 0, mean * 0.25, layer)

    states = (sa_ref, sb_ref)
    rate = jnp.concatenate([jnp.full((1, ROWS, LANES), x, f32) for x in facts.rates], axis=0)

    low, high = face(4), lane_roll(face(5), cells - 1)
    weight = jnp.where(k_first, rate + minus[2], jnp.where(k_last, rate + plus[2], 0.0))
    for it in range(cells // ROWS):
        rows = pl.ds(ROWS * it, ROWS)
        for t in range(tiles):
            at = tiles * it + t
            edge = lane_roll(jnp.where(lane % cells == at, low, high), -at)
            e_ref[:, t, rows, :] = edge
            if s_ref is not None:
                sa_ref[:, t + 1, pl.ds(PAD + ROWS * it, ROWS), :] = (
                    s_ref[0, :, t, rows, :] + weight * edge
                )

    low, high = face(2), face(3)
    for it in range(cells // ROWS):
        rows = pl.ds(PAD + ROWS * it, ROWS)
        side = jnp.where(
            lane < cells,
            lane_roll(low, -cells * it),
            lane_roll(high, cells * (groups - 1 - it)),
        )
        side_ref[:, pl.ds(ROWS * it, ROWS), :] = side
        if s_ref is not None:
            sa_ref[:, 1, rows, :] += jnp.where(lane < cells, (rate + minus[1]) * side, 0.0)
            sa_ref[:, tiles, rows, :] += jnp.where(
                lane >= LANES - cells, (rate + plus[1]) * side, 0.0
            )

    low, high = face(0), face(1)
    low_part = (rate + minus[0]) * low
    high_part = (rate + plus[0]) * high
    for t in range(tiles):
        if s_ref is not None:
            sa_ref[:, t + 1, PAD : PAD + 1, :] += low_part[:, t : t + 1, :]
            sa_ref[:, t + 1, PAD + cells - 1 : PAD + cells, :] += high_part[:, t : t + 1, :]
        for state in states:
            state[:, t + 1, PAD - 1 : PAD, :] = low[:, t : t + 1, :]
            state[:, t + 1, PAD + cells : PAD + cells + 1, :] = high[:, t : t + 1, :]
    wrap_planes(sa_ref, side_ref, cells, tiles)


def make_step(own, facts, e_ref, side_ref, fields, cells, tiles):
    def step(src, dst):
        def put(f, t, it, value):
            dst[f, t + 1, pl.ds(PAD + ROWS * it, ROWS), :] = value

        substep(src, put, e_ref, own, facts, fields, cells, tiles)
        wrap_planes(dst, side_ref, cells, tiles)

    return step


def make_finish(o_ref, cells, tiles):
    def finish(src):
        def store(t, it, value):
            o_ref[0, :, pl.ds(16 * it, 16), pl.ds(LANES * t, LANES)] = value

        from_planes(src, store, cells, tiles)

    return finish


def stay_kernel(first, per_dev, ints_ref, vals_ref, s_ref, rk_ref, arr_ref, o_ref, sa_ref, sb_ref, e_ref, side_ref):
    _, fields, tiles, cells, _ = s_ref.shape
    facts = Facts(ints_ref, vals_ref, ints_ref[pl.program_id(0) + first], per_dev, fields)
    place_layers(
        lambda face_no: arr_ref[facts.lookup(face_no)],
        facts, sa_ref, sb_ref, e_ref, side_ref, s_ref, fields, cells, tiles,
    )
    step = make_step(rk_ref[0], facts, e_ref, side_ref, fields, cells, tiles)
    finish = make_finish(o_ref, cells, tiles)

    @pl.when(facts.n == 1)
    def _():
        finish(sa_ref)

    @pl.when(facts.n > 1)
    def _():
        def two(i, carry):
            step(sa_ref, sb_ref)
            step(sb_ref, sa_ref)
            return carry

        lax.fori_loop(0, (facts.n - 2) // 2, two, 0)
        step(sa_ref, sb_ref)
        finish(sb_ref)


def state_scratch(fields, cells, tiles):
    padded = (fields, tiles + 2, cells + 2 * PAD, LANES)
    return [
        pltpu.VMEM(padded, f32),
        pltpu.VMEM(padded, f32),
        pltpu.VMEM((fields, tiles, cells, LANES), f32),
        pltpu.VMEM((fields, cells, LANES), f32),
    ]


def advance_stay(ints, vals, started, own, arrived, plane, first, per_dev):
    count, fields, tiles, cells, _ = started.shape
    shape = (1, fields, cells, plane)
    return pl.pallas_call(
        functools.partial(stay_kernel, first, per_dev),
        grid_spec=pltpu.PrefetchScalarGridSpec(
            num_scalar_prefetch=2,
            grid=(count,),
            in_specs=[
                pl.BlockSpec((1,) + started.shape[1:], lambda b, i, v: (b, 0, 0, 0, 0)),
                pl.BlockSpec((1,) + own.shape[1:], lambda b, i, v: (b, 0, 0)),
                pl.BlockSpec(arrived.shape, lambda b, i, v: (0, 0, 0)),
            ],
            out_specs=pl.BlockSpec(shape, lambda b, i, v: (i[b + first], 0, 0, 0)),
            scratch_shapes=state_scratch(fields, cells, tiles),
        ),
        out_shape=jax.ShapeDtypeStruct((per_dev, fields, cells, plane), bf16),
        compiler_params=pltpu.CompilerParams(vmem_limit_bytes=20 << 20),
        name="advance_stay",
    )(ints, vals, in_hbm(started), own, arrived)


def traded_kernel(choices, ints_ref, vals_ref, *refs):
    raw_refs, layer_refs, refs = refs[:choices], refs[choices : 2 * choices], refs[2 * choices + 1 :]
    o_ref, sa_ref, sb_ref, e_ref, side_ref, rk_ref, raw_ref, layer_ref, sems = refs
    _, fields, cells, plane = raw_ref.shape
    tiles = plane // LANES
    facts = Facts(ints_ref, vals_ref, 0, 1, fields)
    choice = ints_ref[15]
    for c in range(choices):

        @pl.when(choice == c)
        def _():
            raw_copy = pltpu.make_async_copy(raw_refs[c], raw_ref, sems.at[0])
            layer_copy = pltpu.make_async_copy(layer_refs[c], layer_ref, sems.at[1])
            raw_copy.start()
            layer_copy.start()
            raw_copy.wait()
            layer_copy.wait()

    def write(at, value):
        rk_ref[:, at : at + value.shape[1]] = value

    own_matrix(facts, fields, write)
    load_block(raw_ref, sa_ref, cells, tiles)
    place_layers(
        lambda face_no: layer_ref[face_no],
        facts, sa_ref, sb_ref, e_ref, side_ref, None, fields, cells, tiles,
    )
    step = make_step(rk_ref[...], facts, e_ref, side_ref, fields, cells, tiles)
    finish = make_finish(o_ref, cells, tiles)

    @pl.when(facts.n == 1)
    def _():
        step(sa_ref, sb_ref)
        finish(sb_ref)

    @pl.when(facts.n > 1)
    def _():
        def two(i, carry):
            step(sa_ref, sb_ref)
            step(sb_ref, sa_ref)
            return carry

        lax.fori_loop(0, facts.n // 2, two, 0)
        finish(sa_ref)


def advance_traded(ints, vals, raws, layers, into):
    per_dev, fields, cells, plane = into.shape
    tiles = plane // LANES
    choices = len(raws)
    size = fields * ROWS
    anywhere = pl.BlockSpec(memory_space=pl.ANY)
    return pl.pallas_call(
        functools.partial(traded_kernel, choices),
        grid_spec=pltpu.PrefetchScalarGridSpec(
            num_scalar_prefetch=2,
            grid=(1,),
            in_specs=[anywhere] * (2 * choices + 1),
            out_specs=pl.BlockSpec((1, fields, cells, plane), lambda b, i, v: (i[14], 0, 0, 0)),
            scratch_shapes=state_scratch(fields, cells, tiles)
            + [
                pltpu.VMEM((size, 3 * size), bf16),
                pltpu.VMEM((1, fields, cells, plane), bf16),
                pltpu.VMEM((6, size, LANES), bf16),
                pltpu.SemaphoreType.DMA((2,)),
            ],
        ),
        out_shape=jax.ShapeDtypeStruct(into.shape, bf16),
        input_output_aliases={2 + 2 * choices: 0},
        compiler_params=pltpu.CompilerParams(vmem_limit_bytes=20 << 20),
        name="advance_traded",
    )(ints, vals, *raws, *layers, into)


def plan(wanted, my_index, per_dev):
    peers, requests = wanted.shape
    at = lax.broadcasted_iota(jnp.int32, wanted.shape, 1)
    source_dev = wanted // per_dev
    code = wanted % per_dev * 6 + jnp.bitwise_xor(at % 6, 1)
    key = at * 64 + code
    match = source_dev == my_index
    first = jnp.min(jnp.where(match, key, 64 * requests), axis=1) % 64
    second = jnp.max(jnp.where(match, key, 0), axis=1) % 64
    send = jnp.stack([first, second], axis=1).reshape(2 * peers)
    mine = lax.dynamic_slice_in_dim(wanted, my_index, 1, 0)[0]
    my_source = mine // per_dev
    order = jnp.arange(requests, dtype=jnp.int32)
    repeated = (my_source[:, None] == my_source[None, :]) & (order[None, :] < order[:, None])
    lookup = my_source * 2 + jnp.any(repeated, axis=1).astype(jnp.int32)
    return send, mine, lookup


def local(
    block_state,
    block_level,
    block_velocity,
    diffusivity,
    reaction_matrix,
    ghost_source,
    swap_bit,
    swap_slot,
):
    blocks = block_state[0]
    per_dev, fields, cells, plane = blocks.shape
    peers = lax.axis_size(("gy", "gz"))
    my_index = lax.axis_index(("gy", "gz"))
    levels = block_level[0]
    wanted = ghost_source[0].reshape(peers, per_dev * 6)
    send, mine, lookup = plan(wanted, my_index, per_dev)
    outgoing = pack_faces(blocks, send, 2 * peers)
    arrived = lax.all_to_all(outgoing, ("gy", "gz"), split_axis=0, concat_axis=0, tiled=True)

    own_levels = lax.dynamic_slice_in_dim(levels, my_index * per_dev, per_dev, 0)
    known = mine[:, None] == jnp.arange(levels.shape[0], dtype=jnp.int32)[None, :]
    source_levels = jnp.sum(jnp.where(known, levels[None, :], 0), axis=1)
    coarse = (source_levels.reshape(per_dev, 6) != own_levels[:, None]).astype(jnp.int32)
    bit_here = swap_bit[0, 0, 0]
    slot_here = swap_slot[0, 0, 0]
    rest = jnp.arange(per_dev, dtype=jnp.int32)
    rest = jnp.where(rest == 0, slot_here, rest - (rest <= slot_here))
    ints = jnp.concatenate([rest, own_levels, lookup, coarse.reshape(-1)])
    speeds = block_velocity[0]
    vals = jnp.concatenate([speeds.astype(f32).reshape(-1), diffusivity, reaction_matrix.reshape(-1)])
    pick = lambda x, size: lax.dynamic_slice_in_dim(x.reshape(-1), slot_here * size, size, 0)
    bits = range(lax.axis_size("gx").bit_length() - 1)
    offers = lambda x: [x] + [swapped(x, "gx", bit_no) for bit_no in bits]

    raws = offers(lax.dynamic_slice_in_dim(blocks, slot_here, 1, 0))
    label = jnp.concatenate(
        [pick(own_levels, 1).astype(bf16), pick(coarse, 6).astype(bf16), pick(speeds, 3)]
    )
    label = jnp.broadcast_to(jnp.pad(label, (0, LABEL[1] - label.shape[0]))[None], LABEL)
    label, *others = offers(label)
    for bit_no in bits:
        label = jnp.where(bit_here == bit_no, others[bit_no], label)
    label = label[0]
    traded_ints = jnp.concatenate(
        [
            jnp.zeros((1,), jnp.int32),
            label[0:1].astype(jnp.int32),
            jnp.arange(6, dtype=jnp.int32),
            label[1:7].astype(jnp.int32),
            slot_here[None],
            bit_here[None] + 1,
        ]
    )
    traded_vals = jnp.concatenate([label[7:10].astype(f32), diffusivity, reaction_matrix.reshape(-1)])

    stay = first_substep(ints, vals, blocks, 1, per_dev - 1)
    arrived, stay, traded_ints, traded_vals = lax.optimization_barrier(
        (arrived, stay, traded_ints, traded_vals)
    )
    layers = offers(jnp.take(arrived, pick(lookup, 6), axis=0, mode="clip"))
    result = advance_stay(ints, vals, *stay, arrived, plane, 1, per_dev)
    raws, layers, result = lax.optimization_barrier((raws, layers, result))
    result = advance_traded(traded_ints, traded_vals, raws, layers, result)
    return result[None]


def solution(mesh):
    in_specs = (
        P("gx", ("gy", "gz"), None, None, None),
        P("gx", None),
        P("gx", ("gy", "gz"), None),
        P(),
        P(),
        P("gx", None, None),
        P("gx", "gy", "gz"),
        P("gx", "gy", "gz"),
    )
    out_specs = P("gx", ("gy", "gz"), None, None, None)
    return jax.shard_map(local, mesh=mesh, in_specs=in_specs, out_specs=out_specs, check_vma=False)
```
